256 devices in a mesh: dom: 64 (over x, z, core), feat: 4 (over y).
Axes of the slice: x: 4, y: 4, z: 8, core: 2. Of those that a mesh axis runs over, the one named last changes fastest.
Arguments:
- features: bfloat16 [98304, 1024], P('dom', 'feat'), may hold values from -6 to 6
- first_self: bfloat16 [1024, 256], P('feat'), may hold values from -0.1875 to 0.1875
- first_neighbor: bfloat16 [1024, 256], P('feat'), may hold values from -0.1875 to 0.1875
- first_bias: float32 [256], replicated, may hold values from -3 to 3
- second_self: bfloat16 [256, 256], replicated, may hold values from -0.375 to 0.375
- second_neighbor: bfloat16 [256, 256], replicated, may hold values from -0.375 to 0.375
- send_rows: int32 [64, 2048], P('dom'), may hold values from 0 to 1535
- arrive_count: int32 [64, 64], P('dom'), may hold values from 1 to 32, as said below
- self_slot: int32 [32768], P('dom'), may hold values from 0 to 2047, as said below
- neighbor_slot: int32 [32768, 25], P('dom'), may hold values from 0 to 2047, as said below
- degree: int32 [32768], P('dom'), may hold values from 1 to 25
- seed_self: int32 [8192], P('dom'), may hold values from 0 to 511
- seed_neighbor: int32 [8192, 10], P('dom'), may hold values from 0 to 511
- cotangent: bfloat16 [8192, 256], P('dom'), may hold values from -0.25 to 0.25
Outputs:
- seed_embedding: bfloat16 [8192, 256], P('dom')
- grad_first_self: float32 [1024, 256], P('feat')
- grad_first_neighbor: float32 [1024, 256], P('feat')
- grad_second_self: float32 [256, 256], replicated
- grad_second_neighbor: float32 [256, 256], replicated
The draws below stay inside these ranges and needn't reach their ends.
Inputs may be any that keep to these rules, and one draw needn't show every extreme that they name: `arrive_count`: some owner receives 32 filled slots from every source in every draw. `self_slot`: each entry names slot s * 32 + k of its owner's received slots, with k < arrive_count[owner, s]; the owner that receives 32 filled slots from every source has a mid node at each end of the range. `neighbor_slot`: each entry names slot s * 32 + k of its owner's received slots, with k < arrive_count[owner, s]; the owner that receives 32 filled slots from every source has a mid node at each end of the range.
All inputs are finite; a program needn't handle non-finite values.
Results may differ from the reference program's by a relative error of at most 0.017.
Values may be sent and summed in bfloat16 or wider, within the bound.
No kernel may reach another device: no remote copies, remote signals or barrier semaphores. Data moves between devices by JAX's collectives and lax.ppermute only.
A program may use at most 128 MiB of HBM per device.

```python
import jax
import jax.numpy as jnp
from jax import lax

DIN = 1024
H = 256
C = 256
K1 = 25
K2 = 10
F_DEV = 1536
CAP = 32
M_DEV = 512
S_DEV = 128
F_TOT = 98304
M_TOT = 32768
S_TOT = 8192
N_DOM = 64
N_FEAT = 4


def owner_counts(key):
    load_key, count_key, busy_key = jax.random.split(jax.random.fold_in(key, 11), 3)
    owner_load = jax.random.randint(load_key, (N_DOM, 1), CAP // 4, CAP + 1)
    counts = jax.random.randint(count_key, (N_DOM, N_DOM), owner_load // 2, owner_load + 1)
    busiest = jax.random.randint(busy_key, (), 0, N_DOM)
    owner_index = lax.broadcasted_iota(jnp.int32, (N_DOM, N_DOM), 0)
    return (jnp.where(owner_index == busiest, CAP, counts).astype(jnp.int32), busiest)


def slot_picks(key, table_shape, salt_value):
    counts, busiest = owner_counts(key)
    source_key, offset_key = jax.random.split(jax.random.fold_in(key, salt_value), 2)
    row_index = lax.broadcasted_iota(jnp.int32, table_shape, 0)
    owner_index = row_index // M_DEV
    source = jax.random.randint(source_key, table_shape, 0, N_DOM)
    slot_limit = counts[owner_index, source]
    offset = jax.random.randint(offset_key, table_shape, 0, slot_limit)
    picks = source * CAP + offset
    picks = jnp.where(row_index == busiest * M_DEV, N_DOM * CAP - 1, picks)
    picks = jnp.where(row_index == busiest * M_DEV + 1, 0, picks)
    return picks.astype(jnp.int32)


def draw_arrive_count(key, part):
    counts, busiest = owner_counts(key)
    return counts


def draw_self_slot(key, part):
    return slot_picks(key, (M_TOT,), 31)


def draw_neighbor_slot(key, part):
    return slot_picks(key, (M_TOT, K1), 37)


def place_ends(array, rng, smallest, top_value):
    longest = array.shape.index(max(array.shape))
    spots = []
    for shift in (0, 1):
        where = [jax.random.randint(jax.random.fold_in(rng, axis), (), 0, length) for axis, length in enumerate(array.shape)]
        where[longest] = (where[longest] + shift) % array.shape[longest]
        spots.append(tuple(where))
    return array.at[spots[0]].set(smallest).at[spots[1]].set(top_value)


def level_of(key, dims, pieces, smallest, top_value):
    loudness = 1.0
    for axis_at, parts in pieces:
        heights = jax.random.uniform(jax.random.fold_in(jax.random.fold_in(key, 6), axis_at), (parts,), jnp.float32, smallest / len(pieces), top_value / len(pieces))
        loudness = loudness * jnp.repeat(jnp.exp(heights), dims[axis_at] // parts).reshape((-1,) + (1,) * (len(dims) - 1 - axis_at))
    return loudness


def scatter_about(stream_key, extent, scale, most, shards=(), held_as=jnp.bfloat16):
    array = scale * jax.random.normal(stream_key, extent, jnp.float32)
    if shards:
        array = array * level_of(stream_key, extent, shards, -0.22, 0.18)
    return jnp.clip(array, -most, most).astype(held_as)


def setup_inputs(seed: int = 0) -> dict:
    key_of = jax.random.split(jax.random.key(seed), 15)
    return {
        "features": scatter_about(key_of[0], (F_TOT, DIN), 1.0, 6.0, ((0, 64), (1, 4))),
        "first_self": scatter_about(key_of[1], (DIN, H), DIN ** -0.5, 0.1875, ((0, 4),)),
        "first_neighbor": scatter_about(key_of[2], (DIN, H), DIN ** -0.5, 0.1875, ((0, 4),)),
        "first_bias": scatter_about(key_of[3], (H,), 0.5, 3.0, (), jnp.float32),
        "second_self": scatter_about(key_of[4], (H, C), H ** -0.5, 0.375),
        "second_neighbor": scatter_about(key_of[5], (H, C), H ** -0.5, 0.375),
        "send_rows": place_ends(jax.random.randint(key_of[6], (N_DOM, N_DOM * CAP), 0, F_DEV), jax.random.fold_in(key_of[6], 1), 0, F_DEV - 1).astype(jnp.int32),
        "arrive_count": draw_arrive_count(jax.random.fold_in(key_of[14], 71), 0),
        "self_slot": draw_self_slot(jax.random.fold_in(key_of[14], 71), 0),
        "neighbor_slot": draw_neighbor_slot(jax.random.fold_in(key_of[14], 71), 0),
        "degree": place_ends(jax.random.randint(key_of[10], (M_TOT,), 1, K1 + 1), jax.random.fold_in(key_of[10], 1), 1, K1).astype(jnp.int32),
        "seed_self": place_ends(jax.random.randint(key_of[11], (S_TOT,), 0, M_DEV), jax.random.fold_in(key_of[11], 1), 0, M_DEV - 1).astype(jnp.int32),
        "seed_neighbor": place_ends(jax.random.randint(key_of[12], (S_TOT, K2), 0, M_DEV), jax.random.fold_in(key_of[12], 1), 0, M_DEV - 1).astype(jnp.int32),
        "cotangent": scatter_about(key_of[13], (S_TOT, C), 0.015625, 0.25, ((0, 64),)),
    }


def full_product(left_rows, right_rows):
    return jnp.dot(left_rows.astype(jnp.float32), right_rows.astype(jnp.float32), precision=lax.Precision.HIGHEST)

def inner_rows(left_rows, right_rows):
    return lax.dot_general(left_rows.astype(jnp.float32), right_rows.astype(jnp.float32), (((0,), (0,)), ((), ())), precision=lax.Precision.HIGHEST)

def reference(features, first_self, first_neighbor, first_bias, second_self, second_neighbor, send_rows, arrive_count, self_slot, neighbor_slot, degree, seed_self, seed_neighbor, cotangent):
    paired = jnp.concatenate([first_self, first_neighbor], axis=1).astype(jnp.float32)
    slice_cols = DIN // N_FEAT
    source_feats = features.reshape(N_DOM, F_DEV, DIN)

    def project(operands):
        block_feats, block_rows = operands
        picked = jnp.take(block_feats, block_rows, axis=0).astype(jnp.float32)
        total = jnp.zeros((N_DOM * CAP, 2 * H), jnp.float32)
        for slice_index in range(N_FEAT):
            lower = slice_index * slice_cols
            partial_value = jnp.dot(picked[:, lower:lower + slice_cols], paired[lower:lower + slice_cols], precision=lax.Precision.HIGHEST)
            rounded = lax.optimization_barrier(partial_value.astype(jnp.bfloat16))
            total = total + rounded.astype(jnp.float32)
        return total.astype(jnp.bfloat16)
    projected = lax.map(project, (source_feats, send_rows)).reshape(N_DOM, N_DOM, CAP, 2 * H)
    mids_self = self_slot.reshape(N_DOM, M_DEV)
    mids_near = neighbor_slot.reshape(N_DOM, M_DEV, K1)
    mids_degree = degree.reshape(N_DOM, M_DEV)
    seeds_self = seed_self.reshape(N_DOM, S_DEV)
    seeds_near = seed_neighbor.reshape(N_DOM, S_DEV, K2)
    seeds_cot = cotangent.reshape(N_DOM, S_DEV, C)

    def owner(index):
        arriving = lax.dynamic_index_in_dim(projected, index, 1, keepdims=False).reshape(N_DOM * CAP, 2 * H)
        counts = lax.dynamic_index_in_dim(arrive_count, index, 0, keepdims=False)
        valid_mask = (lax.broadcasted_iota(jnp.int32, (N_DOM, CAP), 1) < counts[:, None]).reshape(N_DOM * CAP, 1)
        slot_table = arriving * valid_mask.astype(jnp.bfloat16)
        own_slots = mids_self[index]
        near_slots = mids_near[index]
        node_degree = mids_degree[index]
        self_rows = jnp.take(slot_table[:, :H], own_slots, axis=0).astype(jnp.float32)
        near_rows = jnp.take(slot_table[:, H:], near_slots, axis=0).astype(jnp.float32)
        live_mask = lax.broadcasted_iota(jnp.int32, near_slots.shape, 1) < node_degree[:, None]
        degree_float = node_degree.astype(jnp.float32)
        near_mean = lax.optimization_barrier(jnp.sum(jnp.where(live_mask[:, :, None], near_rows, 0.0), axis=1)) / degree_float[:, None]
        pre = self_rows + near_mean + first_bias[None, :]
        sigma = jax.nn.sigmoid(pre)
        active = (pre * sigma).astype(jnp.bfloat16)
        slope = lax.optimization_barrier((sigma * (1.0 + pre * (1.0 - sigma))).astype(jnp.bfloat16))
        seed_own = seeds_self[index]
        seed_near = seeds_near[index]
        seed_rows = jnp.take(active, seed_own, axis=0)
        seed_mean = (lax.optimization_barrier(jnp.sum(jnp.take(active, seed_near, axis=0).astype(jnp.float32), axis=1)) / K2).astype(jnp.bfloat16)
        embedding = (full_product(seed_rows, second_self) + full_product(seed_mean, second_neighbor)).astype(jnp.bfloat16)
        upstream = seeds_cot[index].astype(jnp.float32)
        grad_two_self = inner_rows(seed_rows, upstream)
        grad_two_near = inner_rows(seed_mean, upstream)
        back_self = full_product(upstream, second_self.astype(jnp.float32).T)
        back_near = full_product(upstream, second_neighbor.astype(jnp.float32).T) / K2
        spread = jnp.broadcast_to(back_near[:, None, :], (S_DEV, K2, H)).reshape(S_DEV * K2, H)
        grad_active = jnp.zeros((M_DEV, H), jnp.float32).at[seed_own].add(back_self)
        grad_active = grad_active.at[seed_near.reshape(-1)].add(spread)
        grad_pre = grad_active * slope.astype(jnp.float32)
        near_share = jnp.where(live_mask[:, :, None], grad_pre[:, None, :] / degree_float[:, None, None], 0.0)
        grad_self_slots = jnp.zeros((N_DOM * CAP, H), jnp.float32).at[own_slots].add(grad_pre)
        grad_near_slots = jnp.zeros((N_DOM * CAP, H), jnp.float32).at[near_slots.reshape(-1)].add(near_share.reshape(-1, H))
        grad_table = (jnp.concatenate([grad_self_slots, grad_near_slots], axis=1) * valid_mask.astype(jnp.float32)).astype(jnp.bfloat16)
        return (embedding, grad_table, grad_two_self, grad_two_near)
    embeddings, grad_tables, grad_two_self, grad_two_near = lax.map(owner, jnp.arange(N_DOM, dtype=jnp.int32))
    grad_tables = grad_tables.reshape(N_DOM, N_DOM, CAP, 2 * H)

    def source_grad(total, index):
        block_feats = lax.dynamic_index_in_dim(source_feats, index, 0, keepdims=False)
        block_rows = lax.dynamic_index_in_dim(send_rows, index, 0, keepdims=False)
        picked = jnp.take(block_feats, block_rows, axis=0)
        returned = lax.dynamic_index_in_dim(grad_tables, index, 1, keepdims=False).reshape(N_DOM * CAP, 2 * H)
        return (total + inner_rows(picked, returned), None)
    grad_first, unused_tail = lax.scan(source_grad, jnp.zeros((DIN, 2 * H), jnp.float32), jnp.arange(N_DOM, dtype=jnp.int32))
    return (embeddings.reshape(S_TOT, C), grad_first[:, :H], grad_first[:, H:], lax.optimization_barrier(jnp.sum(grad_two_self, axis=0)), lax.optimization_barrier(jnp.sum(grad_two_near, axis=0)))
```

```python
import jax
import jax.numpy as jnp
from jax import lax
from jax.experimental import pallas as pl
from jax.experimental.pallas import tpu as pltpu
from jax.sharding import PartitionSpec as P

BF16 = jnp.bfloat16
F32 = jnp.float32
I32 = jnp.int32


def dot(left, right, left_dim=1, right_dim=0):
    return lax.dot_general(
        left, right, (((left_dim,), (right_dim,)), ((), ())), preferred_element_type=F32
    )


def call(body, outs, args, name, flops=0, moved=0, vmem=None, scratch=()):
    specs = [pl.BlockSpec(memory_space=pltpu.VMEM) for _ in args]
    out_specs = [pl.BlockSpec(memory_space=pltpu.VMEM) for _ in outs]
    return pl.pallas_call(
        body,
        out_shape=[jax.ShapeDtypeStruct(shape, dtype) for shape, dtype in outs],
        in_specs=specs,
        out_specs=out_specs,
        scratch_shapes=scratch,
        name=name,
        compiler_params=pltpu.CompilerParams(vmem_limit_bytes=vmem or (24 << 20)),
        cost_estimate=pl.CostEstimate(flops=flops, bytes_accessed=moved, transcendentals=0),
    )(*args)


def project_body(x_ref, self_ref, near_ref, out_ref):
    slices, rows, width = out_ref.shape
    half = width // 2
    step = rows // 4
    for at in range(slices):
        weight = jnp.concatenate(
            [self_ref[:, at * half : (at + 1) * half], near_ref[:, at * half : (at + 1) * half]],
            axis=1,
        )
        for piece in range(4):
            span = pl.ds(piece * step, step)
            out_ref[at, span, :] = dot(x_ref[span, :], weight).astype(BF16)


def pick_tables_body(column_ref, row_ref, x_ref, pick_ref, spread_ref, xt_ref):
    slots, rows = pick_ref.shape
    step = 128

    def fill_pick(at, carry):
        span = pl.ds(pl.multiple_of(at * step, step), step)
        lane = lax.broadcasted_iota(I32, (step, rows), 1)
        pick_ref[span, :] = jnp.where(column_ref[span, :] == lane, 1.0, 0.0).astype(BF16)
        return carry

    lax.fori_loop(0, slots // step, fill_pick, 0)

    def fill_spread(at, carry):
        span = pl.ds(pl.multiple_of(at * step, step), step)
        line = lax.broadcasted_iota(I32, (step, slots), 0) + at * step
        spread_ref[span, :] = jnp.where(row_ref[...] == line, 1.0, 0.0).astype(BF16)
        return carry

    lax.fori_loop(0, rows // step, fill_spread, 0)
    xt_ref[...] = x_ref[...].T


def count_tables_body(
    self_ref, near_ref, degree_ref, seed_ref, seed_near_ref,
    self_table, near_table, seed_table, seed_near_table, live_ref,
):
    slots, mids = near_table.shape
    fan = near_ref.shape[0]
    step = 32
    live = lax.broadcasted_iota(I32, (fan, mids), 0) < degree_ref[...]
    live_ref[...] = jnp.where(live, near_ref[...], -1)

    def fill(at, carry):
        span = pl.ds(pl.multiple_of(at * step, step), step)
        line = lax.broadcasted_iota(I32, (step, mids), 0) + at * step
        total = jnp.zeros((step, mids), F32)
        for j in range(fan):
            total = total + jnp.where(live_ref[j : j + 1, :] == line, 1.0, 0.0)
        near_table[span, :] = total.astype(BF16)
        self_table[span, :] = jnp.where(self_ref[...] == line, 1.0, 0.0).astype(BF16)
        return carry

    lax.fori_loop(0, slots // step, fill, 0)
    seeds = seed_table.shape[1]
    line = lax.broadcasted_iota(I32, (mids, seeds), 0)
    seed_table[...] = jnp.where(seed_ref[...] == line, 1.0, 0.0).astype(BF16)
    total = jnp.zeros((mids, seeds), F32)
    for j in range(seed_near_ref.shape[0]):
        total = total + jnp.where(seed_near_ref[j : j + 1, :] == line, 1.0, 0.0)
    seed_near_table[...] = total.astype(BF16)


def send_body(parts_ref, pick_ref, out_ref):
    slices = parts_ref.shape[0]
    total = parts_ref[0].astype(F32)
    for at in range(1, slices):
        total = total + parts_ref[at].astype(F32)
    total = total.astype(BF16)
    slots = pick_ref.shape[0]
    step = slots // 8
    for piece in range(8):
        span = pl.ds(piece * step, step)
        out_ref[span, :] = dot(pick_ref[span, :], total).astype(BF16)


def owner_body(
    fan_two,
    slot_ref, mask_ref, self_table, near_table, degree_ref, bias_ref, seed_table, seed_near_table,
    second_self_ref, second_near_ref, cotangent_ref, grad_ref, seeds_ref,
):
    half = bias_ref.shape[0]
    degree = degree_ref[...].astype(F32)
    table = slot_ref[...] * mask_ref[...]
    own = dot(table, self_table[...], 0, 0)[:half]
    near = dot(table, near_table[...], 0, 0)[half:]
    pre = own + near / degree + bias_ref[...]
    sigma = 1.0 / (1.0 + jnp.exp(-pre))
    active = (pre * sigma).astype(BF16)
    slope = (sigma * (1.0 + pre * (1.0 - sigma))).astype(BF16).astype(F32)
    seeds_ref[:half, :] = dot(active, seed_table[...]).astype(BF16)
    seeds_ref[half:, :] = (dot(active, seed_near_table[...]) / fan_two).astype(BF16)
    back_self = dot(second_self_ref[...], cotangent_ref[...], 1, 1)
    back_near = dot(second_near_ref[...], cotangent_ref[...], 1, 1) / fan_two

    def spread(back, picks):
        high = back.astype(BF16)
        low = (back - high.astype(F32)).astype(BF16)
        both = dot(jnp.concatenate([high, low], axis=0), picks, 1, 1)
        return both[:half] + both[half:]

    grad_active = spread(back_self, seed_table[...]) + spread(back_near, seed_near_table[...])
    grad_pre = grad_active * slope
    nothing = jnp.zeros(grad_pre.shape, BF16)
    for_self = jnp.concatenate([grad_pre.astype(BF16), nothing], axis=0)
    for_near = jnp.concatenate([nothing, (grad_pre / degree).astype(BF16)], axis=0)
    slots = slot_ref.shape[0]
    step = slots // 4
    for piece in range(4):
        span = pl.ds(piece * step, step)
        grad = dot(self_table[span, :], for_self, 1, 1) + dot(near_table[span, :], for_near, 1, 1)
        grad_ref[span, :] = grad.astype(BF16) * mask_ref[span, :]


def seeds_body(seeds_ref, second_self_ref, second_near_ref, cotangent_ref, out_ref, grad_ref):
    slices, both, seeds = seeds_ref.shape
    half = both // 2
    tiles = grad_ref.shape[0] // 2
    per = tiles // slices
    total = jnp.zeros(out_ref.shape, F32)
    cotangent = cotangent_ref[...]
    for at in range(slices):
        rows = pl.ds(at * half, half)
        total = total + dot(seeds_ref[at, :half, :], second_self_ref[rows, :], 0, 0)
        total = total + dot(seeds_ref[at, half:, :], second_near_ref[rows, :], 0, 0)
        grad = dot(seeds_ref[at], cotangent)
        shaped = (per,) + grad_ref.shape[1:]
        grad_ref[pl.ds(at * per, per)] = grad[:half].reshape(shaped).astype(BF16)
        grad_ref[pl.ds(tiles + at * per, per)] = grad[half:].reshape(shaped).astype(BF16)
    out_ref[...] = total.astype(BF16)


def gather_body(returned_ref, spread_ref, out_ref):
    rows = spread_ref.shape[0]
    step = rows // 6
    for piece in range(6):
        span = pl.ds(piece * step, step)
        value = dot(spread_ref[span, :], returned_ref[...]).astype(BF16)
        for at in range(out_ref.shape[0]):
            out_ref[at, span, :] = value


def weight_body(xt_ref, grads_ref, out_ref):
    slices, rows, width = grads_ref.shape
    half = width // 2
    tiles = out_ref.shape[0] // 2
    pieces = [dot(xt_ref[...], grads_ref[at]) for at in range(slices)]
    own = jnp.concatenate([piece[:, :half] for piece in pieces], axis=1)
    near = jnp.concatenate([piece[:, half:] for piece in pieces], axis=1)
    shaped = (tiles,) + out_ref.shape[1:]
    out_ref[pl.ds(0, tiles)] = own.reshape(shaped).astype(BF16)
    out_ref[pl.ds(tiles, tiles)] = near.reshape(shaped).astype(BF16)


def sum_body(first_ref, second_ref, out_ref):
    first = jnp.sum(first_ref[...].astype(F32), axis=0)
    second = jnp.sum(second_ref[...].astype(F32), axis=0)
    both = jnp.concatenate([first, second], axis=0).astype(BF16)
    out_ref[...] = jnp.broadcast_to(both[None], out_ref.shape)


def finish_body(all_ref, first_self_ref, first_near_ref, second_self_ref, second_near_ref):
    peers, tall, width = all_ref.shape
    lines = tall // 2
    tiles = peers // 2
    value = all_ref[...].astype(F32)
    first_self_ref[...] = value[:tiles, :lines].reshape(tiles * lines, width)
    first_near_ref[...] = value[tiles:, :lines].reshape(tiles * lines, width)
    second_self_ref[...] = value[:tiles, lines:].reshape(tiles * lines, width)
    second_near_ref[...] = value[tiles:, lines:].reshape(tiles * lines, width)


def exchange(value, axis):
    return lax.all_to_all(value, axis, split_axis=0, concat_axis=0, tiled=True)


def per_device(
    features,
    first_self,
    first_neighbor,
    first_bias,
    second_self,
    second_neighbor,
    send_rows,
    arrive_count,
    self_slot,
    neighbor_slot,
    degree,
    seed_self,
    seed_neighbor,
    cotangent,
):
    peers = lax.axis_size("dom")
    slices = lax.axis_size("feat")
    rows, slice_cols = features.shape
    hidden = first_self.shape[1]
    half = hidden // slices
    width = 2 * half
    slots = send_rows.shape[1]
    capacity = slots // peers
    mids, fan = neighbor_slot.shape
    seeds, fan_two = seed_neighbor.shape
    out_cols = second_self.shape[1]
    lines = hidden * 2 // peers

    (parts,) = call(
        project_body, [((slices, rows, width), BF16)], (features, first_self, first_neighbor),
        "project", 2 * rows * slice_cols * 2 * hidden, rows * (slice_cols + 2 * hidden) * 2,
    )
    parts = exchange(parts, "feat")

    pick, spread, features_t = call(
        pick_tables_body,
        [((slots, rows), BF16), ((rows, slots), BF16), ((slice_cols, rows), BF16)],
        (send_rows.reshape(slots, 1), send_rows, features), "pick_tables",
        0, 4 * rows * slots, 48 << 20,
    )
    self_table, near_table, seed_table, seed_near_table = call(
        count_tables_body,
        [((slots, mids), BF16), ((slots, mids), BF16), ((mids, seeds), BF16), ((mids, seeds), BF16)],
        (
            self_slot.reshape(1, mids), neighbor_slot.T, degree.reshape(1, mids),
            seed_self.reshape(1, seeds), seed_neighbor.T,
        ),
        "count_tables", 0, 16 * slots * mids, scratch=[pltpu.VMEM((fan, mids), I32)],
    )
    mask = jnp.broadcast_to(
        (
            lax.broadcasted_iota(I32, (peers, capacity, width), 1)
            < arrive_count.reshape(peers, 1, 1)
        ),
        (peers, capacity, width),
    ).astype(BF16).reshape(slots, width)
    mine = lax.axis_index("feat") * half
    bias = lax.dynamic_slice(first_bias.reshape(hidden, 1), (mine, 0), (half, 1))
    second_self_part = lax.dynamic_slice(second_self, (mine, 0), (half, out_cols))
    second_near_part = lax.dynamic_slice(second_neighbor, (mine, 0), (half, out_cols))

    (outgoing,) = call(
        send_body, [((slots, width), BF16)], (parts, pick), "send",
        2 * slots * rows * width, 2 * slots * rows,
    )
    incoming = exchange(outgoing.reshape(peers, capacity, width), "dom").reshape(slots, width)

    grad_table, own_seeds = call(
        lambda *refs: owner_body(fan_two, *refs),
        [((slots, width), BF16), ((width, seeds), BF16)],
        (
            incoming, mask, self_table, near_table, degree.reshape(1, mids), bias, seed_table,
            seed_near_table, second_self_part, second_near_part, cotangent,
        ),
        "owner", 8 * slots * mids * width, 4 * slots * mids,
    )
    returned = exchange(grad_table.reshape(peers, capacity, width), "dom").reshape(slots, width)

    all_seeds = exchange(
        jnp.broadcast_to(own_seeds[None], (slices, width, seeds)), "feat"
    )
    seed_embedding, grad_second = call(
        seeds_body, [((seeds, out_cols), BF16), ((peers, lines, out_cols), BF16)],
        (all_seeds, second_self, second_neighbor, cotangent), "seeds",
        8 * seeds * hidden * out_cols, 2 * slots * width,
    )

    (row_grads,) = call(
        gather_body, [((slices, rows, width), BF16)], (returned, spread), "gather",
        2 * slots * rows * width, 2 * slots * rows,
    )
    row_grads = exchange(row_grads, "feat")
    grad_second = exchange(grad_second, "dom")
    (grad_first,) = call(
        weight_body, [((peers, lines, hidden), BF16)], (features_t, row_grads), "weight",
        2 * rows * slice_cols * 2 * hidden, 2 * rows * (slice_cols + 2 * hidden),
    )
    grad_first = exchange(grad_first, "dom")
    (summed,) = call(
        sum_body, [((peers, 2 * lines, hidden), BF16)], (grad_first, grad_second), "sum",
        0, 4 * peers * lines * hidden,
    )
    summed = exchange(summed, "dom")
    grad_first_self, grad_first_neighbor, grad_second_self, grad_second_neighbor = call(
        finish_body, [((slice_cols, hidden), F32)] * 2 + [((hidden, out_cols), F32)] * 2,
        (summed,), "finish", 0, 8 * peers * lines * hidden,
    )
    return (
        seed_embedding,
        grad_first_self,
        grad_first_neighbor,
        grad_second_self,
        grad_second_neighbor,
    )


def solution(mesh):
    in_specs = (
        P("dom", "feat"),
        P("feat", None),
        P("feat", None),
        P(),
        P(),
        P(),
        P("dom", None),
        P("dom", None),
        P("dom"),
        P("dom", None),
        P("dom"),
        P("dom"),
        P("dom", None),
        P("dom", None),
    )
    out_specs = (P("dom", None), P("feat", None), P("feat", None), P(), P())
    return jax.shard_map(
        per_device, mesh=mesh, in_specs=in_specs, out_specs=out_specs, check_vma=False
    )
```

```python
import functools

import jax
import jax.numpy as jnp
from jax import lax
from jax.experimental import pallas as pl
from jax.experimental.pallas import tpu as pltpu
from jax.sharding import PartitionSpec as P

BF16 = jnp.bfloat16
F32 = jnp.float32
I32 = jnp.int32


def dot(left, right, left_dim=1, right_dim=0):
    return lax.dot_general(
        left, right, (((left_dim,), (right_dim,)), ((), ())), preferred_element_type=F32
    )


def call(body, outs, args, name, flops=0, moved=0, vmem=16, scratch=(), scalars=0):
    specs = [
        pl.BlockSpec(memory_space=pltpu.SMEM if at < scalars else pltpu.VMEM)
        for at in range(len(args))
    ]
    out_specs = [pl.BlockSpec(memory_space=pltpu.VMEM) for _ in outs]
    return pl.pallas_call(
        body,
        out_shape=[jax.ShapeDtypeStruct(shape, dtype) for shape, dtype in outs],
        in_specs=specs,
        out_specs=out_specs,
        scratch_shapes=scratch,
        name=name,
        compiler_params=pltpu.CompilerParams(vmem_limit_bytes=vmem << 20),
        cost_estimate=pl.CostEstimate(flops=flops, bytes_accessed=moved, transcendentals=0),
    )(*args)


def pick_body(row_ref, x_ref, self_ref, near_ref, out_ref, weight_ref, slices):
    rows = x_ref.shape[0]
    half = self_ref.shape[1] // slices
    for at in range(slices):
        span = slice(at * half, (at + 1) * half)
        weight_ref[:, 2 * at * half : 2 * (at + 1) * half] = jnp.concatenate(
            [self_ref[:, span], near_ref[:, span]], axis=1
        )
    step = 128
    lane = lax.broadcasted_iota(I32, (step, step), 1)

    def fill(at, carry):
        start = pl.multiple_of(at * step, step)
        wanted = jnp.broadcast_to(row_ref[:, pl.ds(start, step)], (step, step)).T
        picks = jnp.concatenate(
            [
                jnp.where(wanted == lane + low, 1.0, 0.0).astype(BF16)
                for low in range(0, rows, step)
            ],
            axis=1,
        )
        out_ref[pl.ds(start, step), :] = dot(picks, x_ref[...]).astype(BF16)
        return carry

    lax.fori_loop(0, out_ref.shape[0] // step, fill, 0, unroll=4)


def count_body(
    self_ref, near_ref, degree_ref, seed_ref, seed_near_ref,
    self_table, near_table, seed_table, seed_near_table, live_ref,
    capacity, per,
):
    slots, mids = near_table.shape
    fan = near_ref.shape[0]
    quarter = slots * per // capacity
    deep = capacity.bit_length() - 1
    low = per.bit_length() - 1

    def placed(slot):
        return (
            ((slot >> low) & (capacity // per - 1)) * quarter
            + (slot >> deep) * per
            + (slot & (per - 1))
        )

    step = 32
    live = lax.broadcasted_iota(I32, (fan, mids), 0) < degree_ref[...]
    live_ref[...] = jnp.where(live, placed(near_ref[...]), -1)
    own = placed(self_ref[...])

    def fill(at, carry):
        span = pl.ds(pl.multiple_of(at * step, step), step)
        line = lax.broadcasted_iota(I32, (step, mids), 0) + at * step
        total = jnp.zeros((step, mids), F32)
        for j in range(fan):
            total = total + jnp.where(live_ref[j : j + 1, :] == line, 1.0, 0.0)
        near_table[span, :] = total.astype(BF16)
        self_table[span, :] = jnp.where(own == line, 1.0, 0.0).astype(BF16)
        return carry

    lax.fori_loop(0, slots // step, fill, 0)
    seeds = seed_table.shape[1]
    line = lax.broadcasted_iota(I32, (mids, seeds), 0)
    seed_table[...] = jnp.where(seed_ref[...] == line, 1.0, 0.0).astype(BF16)
    total = jnp.zeros((mids, seeds), F32)
    for j in range(seed_near_ref.shape[0]):
        total = total + jnp.where(seed_near_ref[j : j + 1, :] == line, 1.0, 0.0)
    seed_near_table[...] = total.astype(BF16)


def slot_rows(x_ref, at):
    peers, _, per, cols = x_ref.shape
    return x_ref[:, at].astype(F32).reshape(peers * per, cols).astype(BF16)


def project_body(me_ref, x_ref, *refs):
    weight_refs, out_ref = refs[:-1], refs[-1]
    slices, _, width = out_ref.shape
    total = None
    for shift, weight_ref in enumerate(weight_refs):
        at = lax.rem(me_ref[0] + slices - shift, slices)
        part = dot(slot_rows(x_ref, at), weight_ref[...])
        total = part if total is None else total + part
    total = total.astype(BF16)
    for at in range(slices):
        out_ref[at] = total[:, at * width : (at + 1) * width]


def turn_body(x_ref, out_ref):
    cols = x_ref.shape[3]
    for at in range(x_ref.shape[1]):
        out_ref[at * cols : (at + 1) * cols, :] = slot_rows(x_ref, at).T


def owner_body(
    me_ref, slot_ref, mask_ref, self_table, near_table, degree_ref, bias_ref, seed_table,
    seed_near_table, second_self_ref, second_near_ref, cotangent_ref, grad_ref, seeds_ref,
    fan_two,
):
    slots, width = slot_ref.shape
    half = width // 2
    mine = pl.ds(pl.multiple_of(me_ref[0] * half, half), half)
    degree = degree_ref[...].astype(F32)
    table = slot_ref[...] * mask_ref[...]
    own = dot(table, self_table[...], 0, 0)[:half]
    near = dot(table, near_table[...], 0, 0)[half:]
    pre = own + near / degree + bias_ref[mine, :]
    sigma = 1.0 / (1.0 + jnp.exp(-pre))
    active = (pre * sigma).astype(BF16)
    slope = (sigma * (1.0 + pre * (1.0 - sigma))).astype(BF16).astype(F32)
    seeds_ref[:half, :] = dot(active, seed_table[...]).astype(BF16)
    seeds_ref[half:, :] = (dot(active, seed_near_table[...]) / fan_two).astype(BF16)
    back_self = dot(second_self_ref[mine, :], cotangent_ref[...], 1, 1)
    back_near = dot(second_near_ref[mine, :], cotangent_ref[...], 1, 1) / fan_two

    def spread(back, picks):
        high = back.astype(BF16)
        low = (back - high.astype(F32)).astype(BF16)
        both = dot(jnp.concatenate([high, low], axis=0), picks, 1, 1)
        return both[:half] + both[half:]

    grad_active = spread(back_self, seed_table[...]) + spread(back_near, seed_near_table[...])
    grad_pre = grad_active * slope
    nothing = jnp.zeros(grad_pre.shape, BF16)
    for_self = jnp.concatenate([grad_pre.astype(BF16), nothing], axis=0)
    for_near = jnp.concatenate([nothing, (grad_pre / degree).astype(BF16)], axis=0)
    step = slots // 4
    for piece in range(4):
        span = pl.ds(piece * step, step)
        grad = dot(self_table[span, :], for_self, 1, 1) + dot(near_table[span, :], for_near, 1, 1)
        grad_ref[span, :] = grad.astype(BF16) * mask_ref[span, :]


def seeds_body(me_ref, second_self_ref, second_near_ref, cotangent_ref, *refs):
    seeds_refs, (out_ref, grad_ref) = refs[:-2], refs[-2:]
    slices = len(seeds_refs)
    half = seeds_refs[0].shape[0] // 2
    tiles = grad_ref.shape[0] // 2
    per = tiles // slices
    shaped = (per,) + grad_ref.shape[1:]
    total = jnp.zeros(out_ref.shape, F32)
    cotangent = cotangent_ref[...]
    for shift, seeds_ref in enumerate(seeds_refs):
        at = lax.rem(me_ref[0] + slices - shift, slices)
        rows = pl.ds(pl.multiple_of(at * half, half), half)
        total = total + dot(seeds_ref[:half, :], second_self_ref[rows, :], 0, 0)
        total = total + dot(seeds_ref[half:, :], second_near_ref[rows, :], 0, 0)
        grad = dot(seeds_ref[...], cotangent)
        grad_ref[pl.ds(at * per, per)] = grad[:half].reshape(shaped).astype(BF16)
        grad_ref[pl.ds(tiles + at * per, per)] = grad[half:].reshape(shaped).astype(BF16)
    out_ref[...] = total.astype(BF16)


def weight_body(xt_ref, grads_ref, out_ref):
    slices, step = out_ref.shape[:2]
    grads = jnp.concatenate([grads_ref[at] for at in range(slices)], axis=1)
    for at in range(slices):
        out_ref[at] = dot(xt_ref[pl.ds(at * step, step), :], grads).astype(BF16)


def merge_body(parts_ref, second_ref, out_ref):
    slices, _, cols = parts_ref.shape
    width = cols // slices
    half = width // 2
    tiles = out_ref.shape[0] // 2
    lines = out_ref.shape[1] // 2
    total = jnp.sum(parts_ref[...].astype(F32), axis=0)
    for side in range(2):
        part = jnp.concatenate(
            [
                total[:, at * width + side * half : at * width + (side + 1) * half]
                for at in range(slices)
            ],
            axis=1,
        )
        shaped = (tiles, lines, part.shape[1])
        out_ref[pl.ds(side * tiles, tiles), :lines] = part.reshape(shaped).astype(BF16)
    out_ref[:, lines:] = second_ref[...]


def sum_body(parts_ref, out_ref):
    total = jnp.sum(parts_ref[...].astype(F32), axis=0).astype(BF16)
    out_ref[...] = jnp.broadcast_to(total[None], out_ref.shape)


def finish_body(all_ref, first_self_ref, first_near_ref, second_self_ref, second_near_ref):
    peers, tall, width = all_ref.shape
    lines = tall // 2
    tiles = peers // 2
    value = all_ref[...].astype(F32)
    first_self_ref[...] = value[:tiles, :lines].reshape(tiles * lines, width)
    first_near_ref[...] = value[tiles:, :lines].reshape(tiles * lines, width)
    second_self_ref[...] = value[:tiles, lines:].reshape(tiles * lines, width)
    second_near_ref[...] = value[tiles:, lines:].reshape(tiles * lines, width)


def exchange(value, axis):
    return lax.all_to_all(value, axis, split_axis=0, concat_axis=0, tiled=True)


def per_device(
    features,
    first_self,
    first_neighbor,
    first_bias,
    second_self,
    second_neighbor,
    send_rows,
    arrive_count,
    self_slot,
    neighbor_slot,
    degree,
    seed_self,
    seed_neighbor,
    cotangent,
):
    peers = lax.axis_size("dom")
    slices = lax.axis_size("feat")
    rows, slice_cols = features.shape
    hidden = first_self.shape[1]
    half = hidden // slices
    width = 2 * half
    slots = send_rows.shape[1]
    capacity = slots // peers
    per = capacity // slices
    quarter = slots // slices
    mids, fan = neighbor_slot.shape
    seeds, fan_two = seed_neighbor.shape
    out_cols = second_self.shape[1]
    lines = 2 * hidden // peers
    me = lax.axis_index("feat").astype(I32).reshape(1)

    def around(value):
        return [value] + [
            lax.ppermute(value, "feat", [(at, (at + shift) % slices) for at in range(slices)])
            for shift in range(1, slices)
        ]

    picked, weight = call(
        functools.partial(pick_body, slices=slices),
        [((slots, slice_cols), BF16), ((slice_cols, 2 * hidden), BF16)],
        (send_rows, features, first_self, first_neighbor), "pick",
        2 * slots * rows * slice_cols, 2 * slots * rows,
    )
    routed = exchange(picked.reshape(peers * slices, per, slice_cols), ("dom", "feat"))
    routed = routed.reshape(peers, slices, per, slice_cols)
    weights = around(weight)

    self_table, near_table, seed_table, seed_near_table = call(
        functools.partial(count_body, capacity=capacity, per=per),
        [((slots, mids), BF16), ((slots, mids), BF16), ((mids, seeds), BF16), ((mids, seeds), BF16)],
        (
            self_slot.reshape(1, mids), neighbor_slot.T, degree.reshape(1, mids),
            seed_self.reshape(1, seeds), seed_neighbor.T,
        ),
        "count", 0, 16 * slots * mids, scratch=[pltpu.VMEM((fan, mids), I32)],
    )
    slot_at = lax.broadcasted_iota(I32, (slices, peers, per, width), 0) * per
    slot_at = slot_at + lax.broadcasted_iota(I32, (slices, peers, per, width), 2)
    mask = (slot_at < arrive_count.reshape(1, peers, 1, 1)).astype(BF16).reshape(slots, width)
    bias = first_bias.reshape(hidden, 1)

    routed, seed_table = lax.optimization_barrier((routed, seed_table))

    (projected,) = call(
        project_body, [((slices, quarter, width), BF16)], (me, routed, *weights), "project",
        2 * quarter * slices * slice_cols * 2 * hidden, 4 * quarter * slices * slice_cols,
        scalars=1,
    )
    table = exchange(projected, "feat").reshape(slots, width)
    (turned,) = call(
        turn_body, [((slices * slice_cols, quarter), BF16)], (routed,), "turn",
        0, 8 * quarter * slices * slice_cols,
    )

    grad_table, own_seeds = call(
        functools.partial(owner_body, fan_two=fan_two),
        [((slots, width), BF16), ((width, seeds), BF16)],
        (
            me, table, mask, self_table, near_table, degree.reshape(1, mids), bias, seed_table,
            seed_near_table, second_self, second_neighbor, cotangent,
        ),
        "owner", 8 * slots * mids * width, 4 * slots * mids, scalars=1,
    )
    grads = exchange(grad_table.reshape(slices, quarter, width), "feat")
    seed_embedding, grad_second = call(
        seeds_body, [((seeds, out_cols), BF16), ((peers, lines, out_cols), BF16)],
        (me, second_self, second_neighbor, cotangent, *around(own_seeds)), "seeds",
        8 * seeds * hidden * out_cols, 2 * slots * width, scalars=1,
    )
    (partials,) = call(
        weight_body, [((slices, slice_cols, 2 * hidden), BF16)], (turned, grads), "weight",
        2 * quarter * slices * slice_cols * 2 * hidden, 4 * quarter * slices * slice_cols,
    )
    partials = exchange(partials, "feat")
    (merged,) = call(
        merge_body, [((peers, 2 * lines, hidden), BF16)], (partials, grad_second), "merge",
        0, 8 * peers * lines * hidden,
    )
    merged = exchange(merged, "dom")
    (summed,) = call(
        sum_body, [((peers, 2 * lines, hidden), BF16)], (merged,), "sum",
        0, 8 * peers * lines * hidden,
    )
    summed = exchange(summed, "dom")
    grad_first_self, grad_first_neighbor, grad_second_self, grad_second_neighbor = call(
        finish_body, [((slice_cols, hidden), F32)] * 2 + [((hidden, out_cols), F32)] * 2,
        (summed,), "finish", 0, 8 * peers * lines * hidden,
    )
    return (
        seed_embedding,
        grad_first_self,
        grad_first_neighbor,
        grad_second_self,
        grad_second_neighbor,
    )


def solution(mesh):
    in_specs = (
        P("dom", "feat"),
        P("feat", None),
        P("feat", None),
        P(),
        P(),
        P(),
        P("dom", None),
        P("dom", None),
        P("dom"),
        P("dom", None),
        P("dom"),
        P("dom"),
        P("dom", None),
        P("dom", None),
    )
    out_specs = (P("dom", None), P("feat", None), P("feat", None), P(), P())
    return jax.shard_map(
        per_device, mesh=mesh, in_specs=in_specs, out_specs=out_specs, check_vma=False
    )
```

```python
import functools

import jax
import jax.numpy as jnp
from jax import lax
from jax.experimental import pallas as pl
from jax.experimental.pallas import tpu as pltpu
from jax.sharding import Mesh
from jax.sharding import PartitionSpec as P

BF16 = jnp.bfloat16
F32 = jnp.float32
I32 = jnp.int32
AXES = ("x", "z", "core", "feat")


def dot(left, right, left_dim=1, right_dim=0):
    return lax.dot_general(
        left, right, (((left_dim,), (right_dim,)), ((), ())), preferred_element_type=F32
    )


def call(body, outs, args, name, flops=0, moved=0, vmem=16, scratch=(), scalars=0):
    specs = [
        pl.BlockSpec(memory_space=pltpu.SMEM if at < scalars else pltpu.VMEM)
        for at in range(len(args))
    ]
    out_specs = [pl.BlockSpec(memory_space=pltpu.VMEM) for _ in outs]
    return pl.pallas_call(
        body,
        out_shape=[jax.ShapeDtypeStruct(shape, dtype) for shape, dtype in outs],
        in_specs=specs,
        out_specs=out_specs,
        scratch_shapes=scratch,
        name=name,
        compiler_params=pltpu.CompilerParams(vmem_limit_bytes=vmem << 20),
        cost_estimate=pl.CostEstimate(flops=flops, bytes_accessed=moved, transcendentals=0),
    )(*args)


def pick_body(row_ref, x_ref, self_ref, near_ref, out_ref, weight_ref, slices):
    rows = x_ref.shape[0]
    half = self_ref.shape[1] // slices
    for at in range(slices):
        span = slice(at * half, (at + 1) * half)
        weight_ref[:, 2 * at * half : 2 * (at + 1) * half] = jnp.concatenate(
            [self_ref[:, span], near_ref[:, span]], axis=1
        )
    step = 128
    lane = lax.broadcasted_iota(I32, (step, step), 1)

    def fill(at, carry):
        start = pl.multiple_of(at * step, step)
        wanted = jnp.broadcast_to(row_ref[:, pl.ds(start, step)], (step, step)).T
        picks = jnp.concatenate(
            [
                jnp.where(wanted == lane + low, 1.0, 0.0).astype(BF16)
                for low in range(0, rows, step)
            ],
            axis=1,
        )
        out_ref[pl.ds(start, step), :] = dot(picks, x_ref[...]).astype(BF16)
        return carry

    lax.fori_loop(0, out_ref.shape[0] // step, fill, 0, unroll=4)


def count_body(
    self_ref, near_ref, degree_ref, seed_ref, seed_near_ref,
    self_table, near_table, seed_table, seed_near_table, live_ref,
    capacity, per,
):
    slots, mids = near_table.shape
    fan = near_ref.shape[0]
    quarter = slots * per // capacity
    deep = capacity.bit_length() - 1
    low = per.bit_length() - 1

    def placed(slot):
        return (
            ((slot >> low) & (capacity // per - 1)) * quarter
            + (slot >> deep) * per
            + (slot & (per - 1))
        )

    step = 32
    live = lax.broadcasted_iota(I32, (fan, mids), 0) < degree_ref[...]
    live_ref[...] = jnp.where(live, placed(near_ref[...]), -1)
    own = placed(self_ref[...])

    def fill(at, carry):
        span = pl.ds(pl.multiple_of(at * step, step), step)
        line = lax.broadcasted_iota(I32, (step, mids), 0) + at * step
        total = jnp.zeros((step, mids), F32)
        for j in range(fan):
            total = total + jnp.where(live_ref[j : j + 1, :] == line, 1.0, 0.0)
        near_table[span, :] = total.astype(BF16)
        self_table[span, :] = jnp.where(own == line, 1.0, 0.0).astype(BF16)
        return carry

    lax.fori_loop(0, slots // step, fill, 0)
    seeds = seed_table.shape[1]
    line = lax.broadcasted_iota(I32, (mids, seeds), 0)
    seed_table[...] = jnp.where(seed_ref[...] == line, 1.0, 0.0).astype(BF16)
    total = jnp.zeros((mids, seeds), F32)
    for j in range(seed_near_ref.shape[0]):
        total = total + jnp.where(seed_near_ref[j : j + 1, :] == line, 1.0, 0.0)
    seed_near_table[...] = total.astype(BF16)


def slot_rows(x_ref, at):
    peers, _, per, cols = x_ref.shape
    return x_ref[:, at].astype(F32).reshape(peers * per, cols).astype(BF16)


def project_body(place_ref, x_ref, *refs):
    slices = (len(refs) - 1) // 2
    weight_refs, out_refs, held_ref = refs[:slices], refs[slices:-1], refs[-1]
    width = out_refs[0].shape[1]
    me = place_ref[0]
    total = None
    for shift, weight_ref in enumerate(weight_refs):
        part = dot(slot_rows(x_ref, lax.rem(me + slices - shift, slices)), weight_ref[...])
        total = part if total is None else total + part
    total = total.astype(BF16)
    for at in range(slices):
        held_ref[at] = total[:, at * width : (at + 1) * width]
    for shift, out_ref in enumerate(out_refs):
        out_ref[...] = held_ref[lax.rem(me + shift, slices)]


def turn_body(x_ref, out_ref):
    cols = x_ref.shape[3]
    for at in range(x_ref.shape[1]):
        out_ref[at * cols : (at + 1) * cols, :] = slot_rows(x_ref, at).T


def owner_body(
    place_ref, mask_ref, self_table, near_table, degree_ref, bias_ref, seed_table,
    seed_near_table, second_self_ref, second_near_ref, cotangent_ref, *refs, slices, fan_two
):
    slot_refs, grad_refs, seeds_ref = refs[:slices], refs[slices:-1], refs[-1]
    quarter, width = slot_refs[0].shape
    half = width // 2
    me = place_ref[0]
    mine = pl.ds(pl.multiple_of(me * half, half), half)
    degree = degree_ref[...].astype(F32)
    own, near = 0.0, 0.0
    for shift, slot_ref in enumerate(slot_refs):
        at = lax.rem(me + slices - shift, slices)
        span = pl.ds(pl.multiple_of(at * quarter, quarter), quarter)
        table = slot_ref[...] * mask_ref[span, :]
        own = own + dot(table, self_table[span, :], 0, 0)[:half]
        near = near + dot(table, near_table[span, :], 0, 0)[half:]
    pre = own + near / degree + bias_ref[mine, :]
    sigma = 1.0 / (1.0 + jnp.exp(-pre))
    active = (pre * sigma).astype(BF16)
    slope = (sigma * (1.0 + pre * (1.0 - sigma))).astype(BF16).astype(F32)
    seeds_ref[:half, :] = dot(active, seed_table[...]).astype(BF16)
    seeds_ref[half:, :] = (dot(active, seed_near_table[...]) / fan_two).astype(BF16)
    back_self = dot(second_self_ref[mine, :], cotangent_ref[...], 1, 1)
    back_near = dot(second_near_ref[mine, :], cotangent_ref[...], 1, 1) / fan_two

    def spread(back, picks):
        high = back.astype(BF16)
        low = (back - high.astype(F32)).astype(BF16)
        both = dot(jnp.concatenate([high, low], axis=0), picks, 1, 1)
        return both[:half] + both[half:]

    grad_active = spread(back_self, seed_table[...]) + spread(back_near, seed_near_table[...])
    grad_pre = grad_active * slope
    nothing = jnp.zeros(grad_pre.shape, BF16)
    for_self = jnp.concatenate([grad_pre.astype(BF16), nothing], axis=0)
    for_near = jnp.concatenate([nothing, (grad_pre / degree).astype(BF16)], axis=0)
    for shift, grad_ref in enumerate(grad_refs):
        at = lax.rem(me + shift, slices)
        span = pl.ds(pl.multiple_of(at * quarter, quarter), quarter)
        grad = dot(self_table[span, :], for_self, 1, 1) + dot(near_table[span, :], for_near, 1, 1)
        grad_ref[...] = grad.astype(BF16) * mask_ref[span, :]


def seeds_body(place_ref, second_self_ref, second_near_ref, cotangent_ref, *refs):
    seeds_refs, (out_ref, keep_ref, give_ref, held_ref) = refs[:-4], refs[-4:]
    slices = len(seeds_refs)
    half = seeds_refs[0].shape[0] // 2
    total = jnp.zeros(out_ref.shape, F32)
    cotangent = cotangent_ref[...]
    for shift, seeds_ref in enumerate(seeds_refs):
        at = lax.rem(place_ref[0] + slices - shift, slices)
        rows = pl.ds(pl.multiple_of(at * half, half), half)
        total = total + dot(seeds_ref[:half, :], second_self_ref[rows, :], 0, 0)
        total = total + dot(seeds_ref[half:, :], second_near_ref[rows, :], 0, 0)
        grad = dot(seeds_ref[...], cotangent)
        held_ref[0, rows, :] = grad[:half]
        held_ref[1, rows, :] = grad[half:]
    out_ref[...] = total.astype(BF16)
    keep_ref[...] = held_ref[place_ref[1]]
    give_ref[...] = held_ref[1 - place_ref[1]].astype(BF16)


def weight_body(place_ref, xt_ref, *refs):
    grads_refs, (keep_ref, give_ref, held_ref) = refs[:-3], refs[-3:]
    slices, step, _ = keep_ref.shape
    width = grads_refs[0].shape[1]
    for shift, grads_ref in enumerate(grads_refs):
        at = lax.rem(place_ref[0] + slices - shift, slices)
        held_ref[:, pl.ds(pl.multiple_of(at * width, width), width)] = grads_ref[...]
    grads = held_ref[...]
    for at in range(slices):
        mine = pl.multiple_of((2 * at + place_ref[1]) * step, step)
        other = pl.multiple_of((2 * at + 1 - place_ref[1]) * step, step)
        give_ref[at] = dot(xt_ref[pl.ds(other, step), :], grads).astype(BF16)
        keep_ref[at] = dot(xt_ref[pl.ds(mine, step), :], grads)


def halves_body(keep_ref, got_ref, out_ref):
    slices, step, cols = keep_ref.shape
    peers, deep, _ = out_ref.shape
    for at in range(slices):
        total = (keep_ref[at] + got_ref[at].astype(F32)).astype(BF16)
        for piece in range(peers // slices):
            out_ref[piece * slices + at] = total[piece * deep : (piece + 1) * deep]


def sum_body(parts_ref, out_ref):
    total = jnp.sum(parts_ref[...].astype(F32), axis=0).astype(BF16)
    for at in range(out_ref.shape[0]):
        out_ref[at] = total


def second_split_body(place_ref, keep_ref, got_ref, *out_refs):
    count = len(out_refs)
    step = out_refs[0].shape[0]
    for shift, out_ref in enumerate(out_refs):
        at = lax.rem(place_ref[2] + shift, count)
        span = pl.ds(pl.multiple_of(at * step, step), step)
        out_ref[...] = (keep_ref[span, :] + got_ref[span, :].astype(F32)).astype(BF16)


def add_body(*refs):
    total = refs[0][...].astype(F32)
    for ref in refs[1:-1]:
        total = total + ref[...].astype(F32)
    refs[-1][...] = total.astype(BF16)


def second_pair_body(place_ref, mine_ref, other_ref, out_ref):
    rows = mine_ref.shape[0]
    first = place_ref[1] == 0
    out_ref[:rows, :] = jnp.where(first, mine_ref[...], other_ref[...])
    out_ref[rows:, :] = jnp.where(first, other_ref[...], mine_ref[...])


def second_finish_body(place_ref, *refs):
    parts, (self_ref, near_ref) = refs[:-2], refs[-2:]
    count = len(parts)
    step = parts[0].shape[0] // 2
    for shift, part in enumerate(parts):
        at = lax.rem(place_ref[2] + count - shift, count)
        span = pl.ds(pl.multiple_of(at * step, step), step)
        self_ref[span, :] = part[:step, :].astype(F32)
        near_ref[span, :] = part[step:, :].astype(F32)


def first_finish_body(all_ref, self_ref, near_ref, cores, slices):
    peers, deep, cols = all_ref.shape
    width = cols // slices
    half = width // 2
    for at in range(peers):
        start = (at % cores) * (peers // cores) * deep + (at // cores) * deep
        value = all_ref[at].astype(F32)
        for side, ref in enumerate((self_ref, near_ref)):
            ref[start : start + deep, :] = jnp.concatenate(
                [
                    value[:, f * width + side * half : f * width + (side + 1) * half]
                    for f in range(slices)
                ],
                axis=1,
            )


def exchange(value, axis):
    return lax.all_to_all(value, axis, split_axis=0, concat_axis=0, tiled=True)


def shifted(pieces, axis, count):
    return [
        piece
        if shift == 0
        else lax.ppermute(piece, axis, [(at, (at + shift) % count) for at in range(count)])
        for shift, piece in enumerate(pieces)
    ]


def swapped(value, axis, count, step):
    return lax.ppermute(value, axis, [(at, at ^ step) for at in range(count)])


def per_device(
    features,
    first_self,
    first_neighbor,
    first_bias,
    second_self,
    second_neighbor,
    send_rows,
    arrive_count,
    self_slot,
    neighbor_slot,
    degree,
    seed_self,
    seed_neighbor,
    cotangent,
    sizes,
):
    count_x, count_z, cores, slices = (sizes[axis] for axis in AXES)
    peers = count_x * count_z * cores
    rows, slice_cols = features.shape
    hidden = first_self.shape[1]
    half = hidden // slices
    width = 2 * half
    slots = send_rows.shape[1]
    capacity = slots // peers
    per = capacity // slices
    quarter = slots // slices
    mids, fan = neighbor_slot.shape
    seeds, fan_two = seed_neighbor.shape
    out_cols = second_self.shape[1]
    place = jnp.stack([lax.axis_index(axis) for axis in ("feat", "core", "x")]).astype(I32)

    picked, weight = call(
        functools.partial(pick_body, slices=slices),
        [((slots, slice_cols), BF16), ((slice_cols, 2 * hidden), BF16)],
        (send_rows, features, first_self, first_neighbor), "pick",
        2 * slots * rows * slice_cols, 2 * slots * rows,
    )
    routed = exchange(picked.reshape(peers * slices, per, slice_cols), AXES)
    routed = routed.reshape(peers, slices, per, slice_cols)
    weights = shifted([weight] * slices, "feat", slices)

    self_table, near_table, seed_table, seed_near_table = call(
        functools.partial(count_body, capacity=capacity, per=per),
        [((slots, mids), BF16), ((slots, mids), BF16), ((mids, seeds), BF16), ((mids, seeds), BF16)],
        (
            self_slot.reshape(1, mids), neighbor_slot.T, degree.reshape(1, mids),
            seed_self.reshape(1, seeds), seed_neighbor.T,
        ),
        "count", 0, 16 * slots * mids, scratch=[pltpu.VMEM((fan, mids), I32)],
    )
    slot_at = lax.broadcasted_iota(I32, (slices, peers, per, width), 0) * per
    slot_at = slot_at + lax.broadcasted_iota(I32, (slices, peers, per, width), 2)
    mask = (slot_at < arrive_count.reshape(1, peers, 1, 1)).astype(BF16).reshape(slots, width)
    bias = first_bias.reshape(hidden, 1)
    routed, seed_table, mask, bias = lax.optimization_barrier((routed, seed_table, mask, bias))

    projected = call(
        project_body, [((quarter, width), BF16)] * slices, (place, routed, *weights), "project",
        2 * quarter * slices * slice_cols * 2 * hidden, 4 * quarter * slices * slice_cols,
        scratch=[pltpu.VMEM((slices, quarter, width), BF16)], scalars=1,
    )
    tables = shifted(projected, "feat", slices)
    (turned,) = call(
        turn_body, [((slices * slice_cols, quarter), BF16)], (routed,), "turn",
        0, 8 * quarter * slices * slice_cols,
    )

    *grad_tables, own_seeds = call(
        functools.partial(owner_body, slices=slices, fan_two=fan_two),
        [((quarter, width), BF16)] * slices + [((width, seeds), BF16)],
        (
            place, mask, self_table, near_table, degree.reshape(1, mids), bias, seed_table,
            seed_near_table, second_self, second_neighbor, cotangent, *tables,
        ),
        "owner", 8 * slots * mids * width, 4 * slots * mids, scalars=1,
    )
    grads = shifted(grad_tables, "feat", slices)
    all_seeds = shifted([own_seeds] * slices, "feat", slices)
    grads, all_seeds = lax.optimization_barrier((grads, all_seeds))

    step = slice_cols // cores
    keep, give = call(
        weight_body, [((slices, step, 2 * hidden), F32), ((slices, step, 2 * hidden), BF16)],
        (place, turned, *grads), "weight",
        2 * quarter * slices * slice_cols * 2 * hidden, 4 * quarter * slices * slice_cols,
        scratch=[pltpu.VMEM((quarter, 2 * hidden), BF16)], scalars=1,
    )
    got = swapped(give, "core", cores, 1)
    seed_embedding, second_keep, second_give = call(
        seeds_body,
        [((seeds, out_cols), BF16), ((hidden, out_cols), F32), ((hidden, out_cols), BF16)],
        (place, second_self, second_neighbor, cotangent, *all_seeds), "seeds",
        8 * seeds * hidden * out_cols, 2 * slots * width,
        scratch=[pltpu.VMEM((2, hidden, out_cols), F32)], scalars=1,
    )
    got, second_give = lax.optimization_barrier((got, second_give))
    deep = step // count_x
    (mixed,) = call(
        halves_body, [((count_x * slices, deep, 2 * hidden), BF16)], (keep, got), "halves",
        0, 8 * slices * step * hidden,
    )
    mixed = exchange(mixed, ("x", "feat"))

    second_got = swapped(second_give, "core", cores, 1)
    shard = [((hidden // count_x, out_cols), BF16)]
    second_parts = call(
        second_split_body, shard * count_x, (place, second_keep, second_got), "second_split",
        0, 8 * hidden * out_cols, scalars=1,
    )
    (second,) = call(
        add_body, shard, shifted(second_parts, "x", count_x), "second_add",
        0, 4 * hidden * out_cols,
    )

    def doubled(value, stride):
        (value,) = call(
            add_body, shard, (value, swapped(value, "z", count_z, stride)), "second_add",
            0, 2 * hidden * out_cols,
        )
        return value

    strides = [1 << at for at in range(count_z.bit_length() - 1)]
    second = doubled(second, strides[0])
    mixed, second = lax.optimization_barrier((mixed, second))
    (mixed,) = call(
        sum_body, [((count_z, deep, 2 * hidden), BF16)], (mixed,), "sum", 0, 64 * deep * hidden,
    )
    mixed = exchange(mixed, "z")
    for stride in strides[1:]:
        second = doubled(second, stride)
    mixed, second = lax.optimization_barrier((mixed, second))
    (mixed,) = call(
        sum_body, [((count_x * cores, deep, 2 * hidden), BF16)], (mixed,), "sum",
        0, 64 * deep * hidden,
    )
    mixed = exchange(mixed, ("x", "core"))
    (second,) = call(
        second_pair_body, [((2 * hidden // count_x, out_cols), BF16)],
        (place, second, swapped(second, "core", cores, 1)), "second_pair",
        0, 2 * hidden * out_cols, scalars=1,
    )
    grad_second_self, grad_second_neighbor = call(
        second_finish_body, [((hidden, out_cols), F32)] * 2,
        (place, *shifted([second] * count_x, "x", count_x)), "second_finish",
        0, 12 * hidden * out_cols, scalars=1,
    )

    grad_first_self, grad_first_neighbor = call(
        functools.partial(first_finish_body, cores=cores, slices=slices),
        [((slice_cols, hidden), F32)] * 2, (mixed,), "first_finish", 0, 12 * slice_cols * hidden,
    )
    return (
        seed_embedding,
        grad_first_self,
        grad_first_neighbor,
        grad_second_self,
        grad_second_neighbor,
    )


def solution(mesh):
    shape = (4, 8, 2, mesh.shape["feat"])
    sizes = dict(zip(AXES, shape))
    mesh = Mesh(mesh.devices.reshape(shape), AXES)
    dom = AXES[:3]
    in_specs = (
        P(dom, "feat"),
        P("feat", None),
        P("feat", None),
        P(),
        P(),
        P(),
        P(dom, None),
        P(dom, None),
        P(dom),
        P(dom, None),
        P(dom),
        P(dom),
        P(dom, None),
        P(dom, None),
    )
    out_specs = (P(dom, None), P("feat", None), P("feat", None), P(), P())
    return jax.shard_map(
        functools.partial(per_device, sizes=sizes),
        mesh=mesh,
        in_specs=in_specs,
        out_specs=out_specs,
        check_vma=False,
    )
```

```python
import functools

import jax
import jax.numpy as jnp
from jax import lax
from jax.experimental import pallas as pl
from jax.experimental.pallas import tpu as pltpu
from jax.sharding import Mesh
from jax.sharding import PartitionSpec as P

BF16 = jnp.bfloat16
F32 = jnp.float32
I32 = jnp.int32
AXES = ("x", "z", "core", "feat")


def dot(left, right, left_dim=1, right_dim=0):
    return lax.dot_general(
        left, right, (((left_dim,), (right_dim,)), ((), ())), preferred_element_type=F32
    )


def call(body, outs, args, name, flops=0, moved=0, vmem=16, scratch=(), scalars=0, far=()):
    specs = [
        pl.BlockSpec(
            memory_space=pltpu.SMEM if at < scalars else pltpu.HBM if at in far else pltpu.VMEM
        )
        for at in range(len(args))
    ]
    out_specs = [pl.BlockSpec(memory_space=pltpu.VMEM) for _ in outs]
    return pl.pallas_call(
        body,
        out_shape=[jax.ShapeDtypeStruct(shape, dtype) for shape, dtype in outs],
        in_specs=specs,
        out_specs=out_specs,
        scratch_shapes=scratch,
        name=name,
        compiler_params=pltpu.CompilerParams(vmem_limit_bytes=vmem << 20),
        cost_estimate=pl.CostEstimate(flops=flops, bytes_accessed=moved, transcendentals=0),
    )(*[
        pltpu.with_memory_space_constraint(arg, pltpu.HBM) if at in far else arg
        for at, arg in enumerate(args)
    ])


def pick_body(
    row_far, x_far, self_far, near_far, out_ref, weight_ref, row_ref, x_ref, self_ref, near_ref, sems,
    slices,
):
    copies = [
        pltpu.make_async_copy(far, ref, sems.at[at])
        for at, (far, ref) in enumerate(
            ((row_far, row_ref), (x_far, x_ref), (self_far, self_ref), (near_far, near_ref))
        )
    ]
    for copy in copies:
        copy.start()
    rows = x_ref.shape[0]
    half = self_ref.shape[1] // slices
    copies[0].wait()
    copies[1].wait()
    step = 128
    lane = lax.broadcasted_iota(I32, (step, step), 1)

    def fill(at, carry):
        start = pl.multiple_of(at * step, step)
        wanted = jnp.broadcast_to(row_ref[:, pl.ds(start, step)], (step, step)).T
        picks = jnp.concatenate(
            [
                jnp.where(wanted == lane + low, 1.0, 0.0).astype(BF16)
                for low in range(0, rows, step)
            ],
            axis=1,
        )
        out_ref[pl.ds(start, step), :] = dot(picks, x_ref[...]).astype(BF16)
        return carry

    lax.fori_loop(0, out_ref.shape[0] // step, fill, 0, unroll=4)
    copies[2].wait()
    copies[3].wait()
    for at in range(slices):
        span = slice(at * half, (at + 1) * half)
        weight_ref[:, 2 * at * half : 2 * (at + 1) * half] = jnp.concatenate(
            [self_ref[:, span], near_ref[:, span]], axis=1
        )


def count_body(
    self_ref, near_ref, degree_ref, seed_ref, seed_near_ref,
    self_table, near_table, seed_table, seed_near_table, live_ref,
    capacity, per,
):
    slots, mids = near_table.shape
    fan = near_ref.shape[0]
    quarter = slots * per // capacity
    deep = capacity.bit_length() - 1
    low = per.bit_length() - 1

    def placed(slot):
        return (
            ((slot >> low) & (capacity // per - 1)) * quarter
            + (slot >> deep) * per
            + (slot & (per - 1))
        )

    step = 32
    live = lax.broadcasted_iota(I32, (fan, mids), 0) < degree_ref[...]
    live_ref[...] = jnp.where(live, placed(near_ref[...]), -1)
    own = placed(self_ref[...])

    def fill(at, carry):
        span = pl.ds(pl.multiple_of(at * step, step), step)
        line = lax.broadcasted_iota(I32, (step, mids), 0) + at * step
        total = jnp.zeros((step, mids), F32)
        for j in range(fan):
            total = total + jnp.where(live_ref[j : j + 1, :] == line, 1.0, 0.0)
        near_table[span, :] = total.astype(BF16)
        self_table[span, :] = jnp.where(own == line, 1.0, 0.0).astype(BF16)
        return carry

    lax.fori_loop(0, slots // step, fill, 0)
    seeds = seed_table.shape[1]
    line = lax.broadcasted_iota(I32, (mids, seeds), 0)
    seed_table[...] = jnp.where(seed_ref[...] == line, 1.0, 0.0).astype(BF16)
    total = jnp.zeros((mids, seeds), F32)
    for j in range(seed_near_ref.shape[0]):
        total = total + jnp.where(seed_near_ref[j : j + 1, :] == line, 1.0, 0.0)
    seed_near_table[...] = total.astype(BF16)


def slot_rows(x_ref, at):
    peers, _, per, cols = x_ref.shape
    return x_ref[:, at].astype(F32).reshape(peers * per, cols).astype(BF16)


def project_body(place_ref, x_ref, *refs):
    slices = (len(refs) - 1) // 2
    weight_refs, out_refs, held_ref = refs[:slices], refs[slices:-1], refs[-1]
    width = out_refs[0].shape[1]
    me = place_ref[0]
    total = None
    for shift, weight_ref in enumerate(weight_refs):
        part = dot(slot_rows(x_ref, lax.rem(me + slices - shift, slices)), weight_ref[...])
        total = part if total is None else total + part
    total = total.astype(BF16)
    for at in range(slices):
        held_ref[at] = total[:, at * width : (at + 1) * width]
    for shift, out_ref in enumerate(out_refs):
        out_ref[...] = held_ref[lax.rem(me + shift, slices)]


def turn_body(x_ref, out_ref):
    cols = x_ref.shape[3]
    for at in range(x_ref.shape[1]):
        out_ref[at * cols : (at + 1) * cols, :] = slot_rows(x_ref, at).T


def owner_body(
    place_ref, self_far, near_far, mask_ref, degree_ref, bias_ref, seed_table,
    seed_near_table, second_self_ref, second_near_ref, cotangent_ref, *refs, slices, fan_two
):
    slot_refs, out_refs = refs[:slices], refs[slices : 2 * slices]
    self_table, near_table, sems = refs[2 * slices :]
    _, quarter, width = mask_ref.shape
    half = width // 2
    me = place_ref[0]
    copies = []
    for shift in range(slices):
        at = lax.rem(me + slices - shift, slices)
        for side, (far, ref) in enumerate(((self_far, self_table), (near_far, near_table))):
            copies.append(pltpu.make_async_copy(far.at[at], ref.at[shift], sems.at[side, shift]))
            copies[-1].start()
    mine = pl.ds(pl.multiple_of(me * half, half), half)
    degree = degree_ref[...].astype(F32)
    back_self = dot(second_self_ref[mine, :], cotangent_ref[...], 1, 1)
    back_near = dot(second_near_ref[mine, :], cotangent_ref[...], 1, 1) / fan_two

    def spread(back, picks):
        high = back.astype(BF16)
        low = (back - high.astype(F32)).astype(BF16)
        both = dot(jnp.concatenate([high, low], axis=0), picks, 1, 1)
        return both[:half] + both[half:]

    grad_active = spread(back_self, seed_table[...]) + spread(back_near, seed_near_table[...])
    own, near = 0.0, 0.0
    for shift, slot_ref in enumerate(slot_refs):
        at = lax.rem(me + slices - shift, slices)
        table = slot_ref[...] * mask_ref[at]
        copies[2 * shift].wait()
        own = own + dot(table, self_table[shift], 0, 0)[:half]
        copies[2 * shift + 1].wait()
        near = near + dot(table, near_table[shift], 0, 0)[half:]
    pre = own + near / degree + bias_ref[mine, :]
    sigma = 1.0 / (1.0 + jnp.exp(-pre))
    active = (pre * sigma).astype(BF16)
    slope = (sigma * (1.0 + pre * (1.0 - sigma))).astype(BF16).astype(F32)
    own_seeds = dot(active, seed_table[...]).astype(BF16)
    mean_seeds = (dot(active, seed_near_table[...]) / fan_two).astype(BF16)
    for out_ref in out_refs:
        out_ref[quarter : quarter + half, :] = own_seeds
        out_ref[quarter + half :, :] = mean_seeds
    grad_pre = grad_active * slope
    nothing = jnp.zeros(grad_pre.shape, BF16)
    for_self = jnp.concatenate([grad_pre.astype(BF16), nothing], axis=0)
    for_near = jnp.concatenate([nothing, (grad_pre / degree).astype(BF16)], axis=0)
    for shift, out_ref in enumerate(out_refs):
        held = (slices - shift) % slices
        grad = dot(self_table[held], for_self, 1, 1) + dot(near_table[held], for_near, 1, 1)
        out_ref[:quarter, :] = grad.astype(BF16) * mask_ref[lax.rem(me + shift, slices)]


def seeds_body(place_ref, second_self_ref, second_near_ref, cotangent_ref, *refs):
    seeds_refs, (out_ref, keep_ref, give_ref, held_ref) = refs[:-4], refs[-4:]
    slices = len(seeds_refs)
    half = held_ref.shape[1] // slices
    low = seeds_refs[0].shape[0] - 2 * half
    total = jnp.zeros(out_ref.shape, F32)
    cotangent = cotangent_ref[...]
    for shift, seeds_ref in enumerate(seeds_refs):
        at = lax.rem(place_ref[0] + slices - shift, slices)
        rows = pl.ds(pl.multiple_of(at * half, half), half)
        total = total + dot(seeds_ref[low : low + half, :], second_self_ref[rows, :], 0, 0)
        total = total + dot(seeds_ref[low + half :, :], second_near_ref[rows, :], 0, 0)
        grad = dot(seeds_ref[low:, :], cotangent)
        held_ref[0, rows, :] = grad[:half]
        held_ref[1, rows, :] = grad[half:]
    out_ref[...] = total.astype(BF16)
    keep_ref[...] = held_ref[place_ref[1]]
    give_ref[...] = held_ref[1 - place_ref[1]].astype(BF16)


def weight_body(place_ref, xt_ref, *refs):
    grads_refs, (keep_ref, give_ref, held_ref) = refs[:-3], refs[-3:]
    slices, step, _ = keep_ref.shape
    width = grads_refs[0].shape[1]
    for shift, grads_ref in enumerate(grads_refs):
        at = lax.rem(place_ref[0] + slices - shift, slices)
        held_ref[:, pl.ds(pl.multiple_of(at * width, width), width)] = grads_ref[: held_ref.shape[0], :]
    grads = held_ref[...]
    for at in range(slices):
        mine = pl.multiple_of((2 * at + place_ref[1]) * step, step)
        other = pl.multiple_of((2 * at + 1 - place_ref[1]) * step, step)
        give_ref[at] = dot(xt_ref[pl.ds(other, step), :], grads).astype(BF16)
        keep_ref[at] = dot(xt_ref[pl.ds(mine, step), :], grads)


def halves_body(keep_ref, got_ref, out_ref):
    slices, step, cols = keep_ref.shape
    peers, deep, _ = out_ref.shape
    for at in range(slices):
        total = (keep_ref[at] + got_ref[at].astype(F32)).astype(BF16)
        for piece in range(peers // slices):
            out_ref[piece * slices + at] = total[piece * deep : (piece + 1) * deep]


def sum_body(parts_ref, out_ref):
    total = jnp.sum(parts_ref[...].astype(F32), axis=0).astype(BF16)
    for at in range(out_ref.shape[0]):
        out_ref[at] = total


def second_split_body(place_ref, keep_ref, got_ref, *out_refs):
    count = len(out_refs)
    step = out_refs[0].shape[0]
    for shift, out_ref in enumerate(out_refs):
        at = lax.rem(place_ref[2] + shift, count)
        span = pl.ds(pl.multiple_of(at * step, step), step)
        out_ref[...] = (keep_ref[span, :] + got_ref[span, :].astype(F32)).astype(BF16)


def add_body(*refs):
    total = refs[0][...].astype(F32)
    for ref in refs[1:-1]:
        total = total + ref[...].astype(F32)
    refs[-1][...] = total.astype(BF16)


def join_body(parts_ref, second_ref, out_ref):
    _, deep, cols = parts_ref.shape
    total = jnp.sum(parts_ref[...].astype(F32), axis=0).astype(BF16)
    for at in range(out_ref.shape[0]):
        out_ref[at, :deep] = total
        out_ref[at, deep:, : cols // 2] = second_ref[:deep, :]
        out_ref[at, deep:, cols // 2 :] = second_ref[deep:, :]


def finish_body(all_ref, self_ref, near_ref, second_self_ref, second_near_ref, cores, slices):
    peers, deep, cols = all_ref.shape
    deep = deep // 2
    width = cols // slices
    half = width // 2
    for at in range(peers):
        core, x = at % cores, at // cores
        start = core * (peers // cores) * deep + x * deep
        value = all_ref[at].astype(F32)
        for side, ref in enumerate((self_ref, near_ref)):
            ref[start : start + deep, :] = jnp.concatenate(
                [
                    value[:deep, f * width + side * half : f * width + (side + 1) * half]
                    for f in range(slices)
                ],
                axis=1,
            )
        ref = (second_self_ref, second_near_ref)[core]
        ref[2 * x * deep : (2 * x + 1) * deep, :] = value[deep:, : cols // 2]
        ref[(2 * x + 1) * deep : (2 * x + 2) * deep, :] = value[deep:, cols // 2 :]


def exchange(value, axis):
    return lax.all_to_all(value, axis, split_axis=0, concat_axis=0, tiled=True)


def shifted(pieces, axis, count):
    return [
        piece
        if shift == 0
        else lax.ppermute(piece, axis, [(at, (at + shift) % count) for at in range(count)])
        for shift, piece in enumerate(pieces)
    ]


def swapped(value, axis, count, step):
    return lax.ppermute(value, axis, [(at, at ^ step) for at in range(count)])


def per_device(
    features,
    first_self,
    first_neighbor,
    first_bias,
    second_self,
    second_neighbor,
    send_rows,
    arrive_count,
    self_slot,
    neighbor_slot,
    degree,
    seed_self,
    seed_neighbor,
    cotangent,
    sizes,
):
    count_x, count_z, cores, slices = (sizes[axis] for axis in AXES)
    peers = count_x * count_z * cores
    rows, slice_cols = features.shape
    hidden = first_self.shape[1]
    half = hidden // slices
    width = 2 * half
    slots = send_rows.shape[1]
    capacity = slots // peers
    per = capacity // slices
    quarter = slots // slices
    mids, fan = neighbor_slot.shape
    seeds, fan_two = seed_neighbor.shape
    out_cols = second_self.shape[1]
    place = jnp.stack([lax.axis_index(axis) for axis in ("feat", "core", "x")]).astype(I32)

    picked, weight = call(
        functools.partial(pick_body, slices=slices),
        [((slots, slice_cols), BF16), ((slice_cols, 2 * hidden), BF16)],
        (send_rows, features, first_self, first_neighbor), "pick",
        2 * slots * rows * slice_cols, 2 * slots * rows, far=(0, 1, 2, 3),
        scratch=[
            pltpu.VMEM(send_rows.shape, I32), pltpu.VMEM(features.shape, BF16),
            pltpu.VMEM(first_self.shape, BF16), pltpu.VMEM(first_neighbor.shape, BF16),
            pltpu.SemaphoreType.DMA((4,)),
        ],
    )
    routed = exchange(picked.reshape(peers * slices, per, slice_cols), AXES)
    routed = routed.reshape(peers, slices, per, slice_cols)
    weights = shifted([weight] * slices, "feat", slices)

    self_table, near_table, seed_table, seed_near_table = call(
        functools.partial(count_body, capacity=capacity, per=per),
        [((slots, mids), BF16), ((slots, mids), BF16), ((mids, seeds), BF16), ((mids, seeds), BF16)],
        (
            self_slot.reshape(1, mids), neighbor_slot.T, degree.reshape(1, mids),
            seed_self.reshape(1, seeds), seed_neighbor.T,
        ),
        "count", 0, 16 * slots * mids, scratch=[pltpu.VMEM((fan, mids), I32)],
    )
    slot_at = lax.broadcasted_iota(I32, (slices, peers, per, width), 0) * per
    slot_at = slot_at + lax.broadcasted_iota(I32, (slices, peers, per, width), 2)
    mask = (slot_at < arrive_count.reshape(1, peers, 1, 1)).astype(BF16)
    mask = mask.reshape(slices, quarter, width)
    bias = first_bias.reshape(hidden, 1)
    routed, seed_table, mask, bias = lax.optimization_barrier((routed, seed_table, mask, bias))

    projected = call(
        project_body, [((quarter, width), BF16)] * slices, (place, routed, *weights), "project",
        2 * quarter * slices * slice_cols * 2 * hidden, 4 * quarter * slices * slice_cols,
        scratch=[pltpu.VMEM((slices, quarter, width), BF16)], scalars=1,
    )
    tables = shifted(projected, "feat", slices)
    (turned,) = call(
        turn_body, [((slices * slice_cols, quarter), BF16)], (routed,), "turn",
        0, 8 * quarter * slices * slice_cols,
    )

    grads = call(
        functools.partial(owner_body, slices=slices, fan_two=fan_two),
        [((quarter + width, seeds), BF16)] * slices,
        (
            place, self_table.reshape(slices, quarter, mids), near_table.reshape(slices, quarter, mids),
            mask, degree.reshape(1, mids), bias, seed_table,
            seed_near_table, second_self, second_neighbor, cotangent, *tables,
        ),
        "owner", 8 * slots * mids * width, 4 * slots * mids, scalars=1, far=(1, 2),
        scratch=[
            pltpu.VMEM((slices, quarter, mids), BF16), pltpu.VMEM((slices, quarter, mids), BF16),
            pltpu.SemaphoreType.DMA((2, slices)),
        ],
    )
    grads = shifted(grads, "feat", slices)

    step = slice_cols // cores
    keep, give = call(
        weight_body, [((slices, step, 2 * hidden), F32), ((slices, step, 2 * hidden), BF16)],
        (place, turned, *grads), "weight",
        2 * quarter * slices * slice_cols * 2 * hidden, 4 * quarter * slices * slice_cols,
        scratch=[pltpu.VMEM((quarter, 2 * hidden), BF16)], scalars=1,
    )
    got = swapped(give, "core", cores, 1)
    seed_embedding, second_keep, second_give = call(
        seeds_body,
        [((seeds, out_cols), BF16), ((hidden, out_cols), F32), ((hidden, out_cols), BF16)],
        (place, second_self, second_neighbor, cotangent, *grads), "seeds",
        8 * seeds * hidden * out_cols, 2 * slots * width,
        scratch=[pltpu.VMEM((2, hidden, out_cols), F32)], scalars=1,
    )
    got, second_give = lax.optimization_barrier((got, second_give))
    deep = step // count_x
    (mixed,) = call(
        halves_body, [((count_x * slices, deep, 2 * hidden), BF16)], (keep, got), "halves",
        0, 8 * slices * step * hidden,
    )
    mixed = exchange(mixed, ("x", "feat"))

    second_got = swapped(second_give, "core", cores, 1)
    shard = [((hidden // count_x, out_cols), BF16)]
    second_parts = call(
        second_split_body, shard * count_x, (place, second_keep, second_got), "second_split",
        0, 8 * hidden * out_cols, scalars=1,
    )
    (second,) = call(
        add_body, shard, shifted(second_parts, "x", count_x), "second_add",
        0, 4 * hidden * out_cols,
    )

    def doubled(value, stride):
        (value,) = call(
            add_body, shard, (value, swapped(value, "z", count_z, stride)), "second_add",
            0, 2 * hidden * out_cols,
        )
        return value

    strides = [1 << at for at in range(count_z.bit_length() - 1)]
    second = doubled(second, strides[0])
    mixed, second = lax.optimization_barrier((mixed, second))
    (mixed,) = call(
        sum_body, [((count_z, deep, 2 * hidden), BF16)], (mixed,), "sum", 0, 64 * deep * hidden,
    )
    mixed = exchange(mixed, "z")
    for stride in strides[1:]:
        second = doubled(second, stride)
    (mixed,) = call(
        join_body, [((count_x * cores, 2 * deep, 2 * hidden), BF16)], (mixed, second), "join",
        0, 64 * deep * hidden,
    )
    mixed = exchange(mixed, ("x", "core"))
    grad_first_self, grad_first_neighbor, grad_second_self, grad_second_neighbor = call(
        functools.partial(finish_body, cores=cores, slices=slices),
        [((slice_cols, hidden), F32)] * 2 + [((hidden, out_cols), F32)] * 2, (mixed,), "finish",
        0, 24 * slice_cols * hidden,
    )
    return (
        seed_embedding,
        grad_first_self,
        grad_first_neighbor,
        grad_second_self,
        grad_second_neighbor,
    )


def solution(mesh):
    shape = (4, 8, 2, mesh.shape["feat"])
    sizes = dict(zip(AXES, shape))
    mesh = Mesh(mesh.devices.reshape(shape), AXES)
    dom = AXES[:3]
    in_specs = (
        P(dom, "feat"),
        P("feat", None),
        P("feat", None),
        P(),
        P(),
        P(),
        P(dom, None),
        P(dom, None),
        P(dom),
        P(dom, None),
        P(dom),
        P(dom),
        P(dom, None),
        P(dom, None),
    )
    out_specs = (P(dom, None), P("feat", None), P("feat", None), P(), P())
    return jax.shard_map(
        functools.partial(per_device, sizes=sizes),
        mesh=mesh,
        in_specs=in_specs,
        out_specs=out_specs,
        check_vma=False,
    )
```

```python
import functools

import jax
import jax.numpy as jnp
from jax import lax
from jax.experimental import pallas as pl
from jax.experimental.pallas import tpu as pltpu
from jax.sharding import Mesh
from jax.sharding import PartitionSpec as P

BF16 = jnp.bfloat16
F32 = jnp.float32
I32 = jnp.int32
AXES = ("x", "z", "core", "feat")


def dot(left, right, left_dim=1, right_dim=0):
    return lax.dot_general(
        left, right, (((left_dim,), (right_dim,)), ((), ())), preferred_element_type=F32
    )


def call(body, outs, args, name, flops=0, moved=0, vmem=16, scratch=(), scalars=0, far=()):
    specs = [
        pl.BlockSpec(
            memory_space=pltpu.SMEM if at < scalars else pltpu.HBM if at in far else pltpu.VMEM
        )
        for at in range(len(args))
    ]
    out_specs = [pl.BlockSpec(memory_space=pltpu.VMEM) for _ in outs]
    return pl.pallas_call(
        body,
        out_shape=[jax.ShapeDtypeStruct(shape, dtype) for shape, dtype in outs],
        in_specs=specs,
        out_specs=out_specs,
        scratch_shapes=scratch,
        name=name,
        compiler_params=pltpu.CompilerParams(vmem_limit_bytes=vmem << 20),
        cost_estimate=pl.CostEstimate(flops=flops, bytes_accessed=moved, transcendentals=0),
    )(*[
        pltpu.with_memory_space_constraint(arg, pltpu.HBM) if at in far else arg
        for at, arg in enumerate(args)
    ])


def pick_body(
    row_far, x_far, self_far, near_far, out_ref, weight_ref, row_ref, x_ref, self_ref, near_ref,
    picks_ref, sems, slices,
):
    copies = [
        pltpu.make_async_copy(far, ref, sems.at[at])
        for at, (far, ref) in enumerate(
            ((row_far, row_ref), (x_far, x_ref), (self_far, self_ref), (near_far, near_ref))
        )
    ]
    for copy in copies:
        copy.start()
    rows = x_ref.shape[0]
    half = self_ref.shape[1] // slices
    copies[0].wait()
    copies[1].wait()
    step = 128
    tall = 4 * step
    lane = lax.broadcasted_iota(I32, (step, step), 1)

    def fill(at, carry):
        for piece in range(tall // step):
            start = pl.multiple_of(at * tall + piece * step, step)
            wanted = jnp.broadcast_to(row_ref[:, pl.ds(start, step)], (step, step)).T
            for low in range(0, rows, step):
                picks_ref[pl.ds(start, step), low : low + step] = jnp.where(
                    wanted == lane + low, 1.0, 0.0
                ).astype(BF16)
        span = pl.ds(pl.multiple_of(at * tall, tall), tall)
        out_ref[span, :] = dot(picks_ref[span, :], x_ref[...]).astype(BF16)
        return carry

    lax.fori_loop(0, out_ref.shape[0] // tall, fill, 0, unroll=2)
    copies[2].wait()
    copies[3].wait()
    for at in range(slices):
        span = slice(at * half, (at + 1) * half)
        weight_ref[:, 2 * at * half : 2 * (at + 1) * half] = jnp.concatenate(
            [self_ref[:, span], near_ref[:, span]], axis=1
        )


def count_body(
    self_ref, near_ref, degree_ref, seed_ref, seed_near_ref,
    self_table, near_table, seed_table, seed_near_table, live_ref,
    capacity, per,
):
    slots, mids = near_table.shape
    fan = near_ref.shape[0]
    quarter = slots * per // capacity
    deep = capacity.bit_length() - 1
    low = per.bit_length() - 1

    def placed(slot):
        return (
            ((slot >> low) & (capacity // per - 1)) * quarter
            + (slot >> deep) * per
            + (slot & (per - 1))
        )

    step = 32
    live = lax.broadcasted_iota(I32, (fan, mids), 0) < degree_ref[...]
    live_ref[...] = jnp.where(live, placed(near_ref[...]), -1)
    own = placed(self_ref[...])

    def fill(at, carry):
        span = pl.ds(pl.multiple_of(at * step, step), step)
        line = lax.broadcasted_iota(I32, (step, mids), 0) + at * step
        total = jnp.zeros((step, mids), F32)
        for j in range(fan):
            total = total + jnp.where(live_ref[j : j + 1, :] == line, 1.0, 0.0)
        near_table[span, :] = total.astype(BF16)
        self_table[span, :] = jnp.where(own == line, 1.0, 0.0).astype(BF16)
        return carry

    lax.fori_loop(0, slots // step, fill, 0)
    seeds = seed_table.shape[1]
    line = lax.broadcasted_iota(I32, (mids, seeds), 0)
    seed_table[...] = jnp.where(seed_ref[...] == line, 1.0, 0.0).astype(BF16)
    total = jnp.zeros((mids, seeds), F32)
    for j in range(seed_near_ref.shape[0]):
        total = total + jnp.where(seed_near_ref[j : j + 1, :] == line, 1.0, 0.0)
    seed_near_table[...] = total.astype(BF16)


def slot_rows(x_ref, at):
    peers, _, per, cols = x_ref.shape
    return x_ref[:, at].reshape(peers * per, cols)


def project_body(place_ref, x_ref, *refs):
    slices = (len(refs) - 1) // 2
    weight_refs, out_refs, held_ref = refs[:slices], refs[slices:-1], refs[-1]
    width = out_refs[0].shape[1]
    me = place_ref[0]
    total = None
    for shift, weight_ref in enumerate(weight_refs):
        part = dot(slot_rows(x_ref, lax.rem(me + slices - shift, slices)), weight_ref[...])
        total = part if total is None else total + part
    total = total.astype(BF16)
    for at in range(slices):
        held_ref[at] = total[:, at * width : (at + 1) * width]
    for shift, out_ref in enumerate(out_refs):
        out_ref[...] = held_ref[lax.rem(me + shift, slices)]


def turn_body(x_ref, out_ref):
    cols = x_ref.shape[3]
    for at in range(x_ref.shape[1]):
        out_ref[at * cols : (at + 1) * cols, :] = slot_rows(x_ref, at).T


def owner_body(
    place_ref, self_far, near_far, mask_ref, degree_ref, bias_ref, seed_table,
    seed_near_table, second_self_ref, second_near_ref, cotangent_ref, *refs, slices, fan_two
):
    slot_refs, out_refs = refs[:slices], refs[slices : 2 * slices]
    self_table, near_table, sems = refs[2 * slices :]
    _, quarter, width = mask_ref.shape
    half = width // 2
    me = place_ref[0]
    copies = []
    for shift in range(slices):
        at = lax.rem(me + slices - shift, slices)
        for side, (far, ref) in enumerate(((self_far, self_table), (near_far, near_table))):
            copies.append(pltpu.make_async_copy(far.at[at], ref.at[shift], sems.at[side, shift]))
            copies[-1].start()
    mine = pl.ds(pl.multiple_of(me * half, half), half)
    degree = degree_ref[...].astype(F32)
    back_self = dot(second_self_ref[mine, :], cotangent_ref[...], 1, 1)
    back_near = dot(second_near_ref[mine, :], cotangent_ref[...], 1, 1) / fan_two

    def spread(back, picks):
        high = back.astype(BF16)
        low = (back - high.astype(F32)).astype(BF16)
        both = dot(jnp.concatenate([high, low], axis=0), picks, 1, 1)
        return both[:half] + both[half:]

    grad_active = spread(back_self, seed_table[...]) + spread(back_near, seed_near_table[...])
    own, near = 0.0, 0.0
    for shift, slot_ref in enumerate(slot_refs):
        at = lax.rem(me + slices - shift, slices)
        table = slot_ref[...] * mask_ref[at]
        copies[2 * shift].wait()
        own = own + dot(table, self_table[shift], 0, 0)[:half]
        copies[2 * shift + 1].wait()
        near = near + dot(table, near_table[shift], 0, 0)[half:]
    pre = own + near / degree + bias_ref[mine, :]
    sigma = 1.0 / (1.0 + jnp.exp(-pre))
    active = (pre * sigma).astype(BF16)
    slope = (sigma * (1.0 + pre * (1.0 - sigma))).astype(BF16).astype(F32)
    own_seeds = dot(active, seed_table[...]).astype(BF16)
    mean_seeds = (dot(active, seed_near_table[...]) / fan_two).astype(BF16)
    for out_ref in out_refs:
        out_ref[quarter : quarter + half, :] = own_seeds
        out_ref[quarter + half :, :] = mean_seeds
    grad_pre = grad_active * slope
    nothing = jnp.zeros(grad_pre.shape, BF16)
    for_self = jnp.concatenate([grad_pre.astype(BF16), nothing], axis=0)
    for_near = jnp.concatenate([nothing, (grad_pre / degree).astype(BF16)], axis=0)
    for shift, out_ref in enumerate(out_refs):
        held = (slices - shift) % slices
        grad = dot(self_table[held], for_self, 1, 1) + dot(near_table[held], for_near, 1, 1)
        out_ref[:quarter, :] = grad.astype(BF16) * mask_ref[lax.rem(me + shift, slices)]


def seeds_body(place_ref, second_self_ref, second_near_ref, cotangent_ref, *refs):
    seeds_refs, (out_ref, keep_ref, give_ref, held_ref) = refs[:-4], refs[-4:]
    slices = len(seeds_refs)
    half = held_ref.shape[1] // slices
    low = seeds_refs[0].shape[0] - 2 * half
    total = jnp.zeros(out_ref.shape, F32)
    cotangent = cotangent_ref[...]
    for shift, seeds_ref in enumerate(seeds_refs):
        at = lax.rem(place_ref[0] + slices - shift, slices)
        rows = pl.ds(pl.multiple_of(at * half, half), half)
        total = total + dot(seeds_ref[low : low + half, :], second_self_ref[rows, :], 0, 0)
        total = total + dot(seeds_ref[low + half :, :], second_near_ref[rows, :], 0, 0)
        grad = dot(seeds_ref[low:, :], cotangent)
        held_ref[0, rows, :] = grad[:half]
        held_ref[1, rows, :] = grad[half:]
    out_ref[...] = total.astype(BF16)
    keep_ref[...] = held_ref[place_ref[1]]
    give_ref[...] = held_ref[1 - place_ref[1]].astype(BF16)


def weight_body(place_ref, xt_ref, *refs):
    grads_refs, (keep_ref, give_ref, held_ref) = refs[:-3], refs[-3:]
    slices, step, _ = keep_ref.shape
    width = grads_refs[0].shape[1]
    for shift, grads_ref in enumerate(grads_refs):
        at = lax.rem(place_ref[0] + slices - shift, slices)
        held_ref[:, pl.ds(pl.multiple_of(at * width, width), width)] = grads_ref[: held_ref.shape[0], :]
    grads = held_ref[...]
    for at in range(slices):
        mine = pl.multiple_of((2 * at + place_ref[1]) * step, step)
        other = pl.multiple_of((2 * at + 1 - place_ref[1]) * step, step)
        give_ref[at] = dot(xt_ref[pl.ds(other, step), :], grads).astype(BF16)
        keep_ref[at] = dot(xt_ref[pl.ds(mine, step), :], grads)


def halves_body(keep_ref, got_ref, out_ref):
    slices, step, cols = keep_ref.shape
    peers, deep, _ = out_ref.shape
    for at in range(slices):
        total = (keep_ref[at] + got_ref[at].astype(F32)).astype(BF16)
        for piece in range(peers // slices):
            out_ref[piece * slices + at] = total[piece * deep : (piece + 1) * deep]


def sum_body(parts_ref, out_ref):
    total = jnp.sum(parts_ref[...].astype(F32), axis=0).astype(BF16)
    for at in range(out_ref.shape[0]):
        out_ref[at] = total


def second_split_body(place_ref, keep_ref, got_ref, *out_refs):
    count = len(out_refs)
    step = out_refs[0].shape[0]
    for shift, out_ref in enumerate(out_refs):
        at = lax.rem(place_ref[2] + shift, count)
        span = pl.ds(pl.multiple_of(at * step, step), step)
        out_ref[...] = (keep_ref[span, :] + got_ref[span, :].astype(F32)).astype(BF16)


def add_body(*refs):
    total = refs[0][...].astype(F32)
    for ref in refs[1:-1]:
        total = total + ref[...].astype(F32)
    refs[-1][...] = total.astype(BF16)


def join_body(parts_ref, second_ref, out_ref):
    _, deep, cols = parts_ref.shape
    out_ref[:deep] = jnp.sum(parts_ref[...].astype(F32), axis=0).astype(BF16)
    out_ref[deep:, : cols // 2] = second_ref[:deep, :]
    out_ref[deep:, cols // 2 :] = second_ref[deep:, :]


def pair_body(place_ref, mine_ref, other_ref, out_ref):
    rows = mine_ref.shape[0]
    first = place_ref[1] == 0
    out_ref[:rows, :] = jnp.where(first, mine_ref[...], other_ref[...])
    out_ref[rows:, :] = jnp.where(first, other_ref[...], mine_ref[...])


def finish_body(place_ref, *refs, cores, slices):
    parts, (self_ref, near_ref, second_self_ref, second_near_ref) = refs[:-4], refs[-4:]
    count = len(parts)
    cols = parts[0].shape[1]
    deep = parts[0].shape[0] // (2 * cores)
    width = cols // slices
    half = width // 2
    for shift, part in enumerate(parts):
        x = lax.rem(place_ref[2] + count - shift, count)
        for core in range(cores):
            low = 2 * core * deep
            value = part[low : low + deep, :].astype(F32)
            span = pl.ds(pl.multiple_of((core * count + x) * deep, deep), deep)
            for side, ref in enumerate((self_ref, near_ref)):
                ref[span, :] = jnp.concatenate(
                    [
                        value[:, f * width + side * half : f * width + (side + 1) * half]
                        for f in range(slices)
                    ],
                    axis=1,
                )
            value = part[low + deep : low + 2 * deep, :].astype(F32)
            ref = (second_self_ref, second_near_ref)[core]
            for side in range(2):
                span = pl.ds(pl.multiple_of((2 * x + side) * deep, deep), deep)
                ref[span, :] = value[:, side * cols // 2 : (side + 1) * cols // 2]


def exchange(value, axis):
    return lax.all_to_all(value, axis, split_axis=0, concat_axis=0, tiled=True)


def shifted(pieces, axis, count):
    return [
        piece
        if shift == 0
        else lax.ppermute(piece, axis, [(at, (at + shift) % count) for at in range(count)])
        for shift, piece in enumerate(pieces)
    ]


def swapped(value, axis, count, step):
    return lax.ppermute(value, axis, [(at, at ^ step) for at in range(count)])


def per_device(
    features,
    first_self,
    first_neighbor,
    first_bias,
    second_self,
    second_neighbor,
    send_rows,
    arrive_count,
    self_slot,
    neighbor_slot,
    degree,
    seed_self,
    seed_neighbor,
    cotangent,
    sizes,
):
    count_x, count_z, cores, slices = (sizes[axis] for axis in AXES)
    peers = count_x * count_z * cores
    rows, slice_cols = features.shape
    hidden = first_self.shape[1]
    half = hidden // slices
    width = 2 * half
    slots = send_rows.shape[1]
    capacity = slots // peers
    per = capacity // slices
    quarter = slots // slices
    mids, fan = neighbor_slot.shape
    seeds, fan_two = seed_neighbor.shape
    out_cols = second_self.shape[1]
    place = jnp.stack([lax.axis_index(axis) for axis in ("feat", "core", "x")]).astype(I32)

    picked, weight = call(
        functools.partial(pick_body, slices=slices),
        [((slots, slice_cols), BF16), ((slice_cols, 2 * hidden), BF16)],
        (send_rows, features, first_self, first_neighbor), "pick",
        2 * slots * rows * slice_cols, 2 * slots * rows, far=(0, 1, 2, 3),
        scratch=[
            pltpu.VMEM(send_rows.shape, I32), pltpu.VMEM(features.shape, BF16),
            pltpu.VMEM(first_self.shape, BF16), pltpu.VMEM(first_neighbor.shape, BF16),
            pltpu.VMEM((slots, rows), BF16), pltpu.SemaphoreType.DMA((4,)),
        ],
    )
    routed = exchange(picked.reshape(peers * slices, per, slice_cols), AXES)
    routed = routed.reshape(peers, slices, per, slice_cols)
    weights = shifted([weight] * slices, "feat", slices)

    self_table, near_table, seed_table, seed_near_table = call(
        functools.partial(count_body, capacity=capacity, per=per),
        [((slots, mids), BF16), ((slots, mids), BF16), ((mids, seeds), BF16), ((mids, seeds), BF16)],
        (
            self_slot.reshape(1, mids), neighbor_slot.T, degree.reshape(1, mids),
            seed_self.reshape(1, seeds), seed_neighbor.T,
        ),
        "count", 0, 16 * slots * mids, scratch=[pltpu.VMEM((fan, mids), I32)],
    )
    slot_at = lax.broadcasted_iota(I32, (slices, peers, per, width), 0) * per
    slot_at = slot_at + lax.broadcasted_iota(I32, (slices, peers, per, width), 2)
    mask = (slot_at < arrive_count.reshape(1, peers, 1, 1)).astype(BF16)
    mask = mask.reshape(slices, quarter, width)
    bias = first_bias.reshape(hidden, 1)
    routed, seed_table, mask, bias = lax.optimization_barrier((routed, seed_table, mask, bias))

    projected = call(
        project_body, [((quarter, width), BF16)] * slices, (place, routed, *weights), "project",
        2 * quarter * slices * slice_cols * 2 * hidden, 4 * quarter * slices * slice_cols,
        scratch=[pltpu.VMEM((slices, quarter, width), BF16)], scalars=1,
    )
    tables = shifted(projected, "feat", slices)
    (turned,) = call(
        turn_body, [((slices * slice_cols, quarter), BF16)], (routed,), "turn",
        0, 8 * quarter * slices * slice_cols,
    )

    grads = call(
        functools.partial(owner_body, slices=slices, fan_two=fan_two),
        [((quarter + width, seeds), BF16)] * slices,
        (
            place, self_table.reshape(slices, quarter, mids), near_table.reshape(slices, quarter, mids),
            mask, degree.reshape(1, mids), bias, seed_table,
            seed_near_table, second_self, second_neighbor, cotangent, *tables,
        ),
        "owner", 8 * slots * mids * width, 4 * slots * mids, scalars=1, far=(1, 2),
        scratch=[
            pltpu.VMEM((slices, quarter, mids), BF16), pltpu.VMEM((slices, quarter, mids), BF16),
            pltpu.SemaphoreType.DMA((2, slices)),
        ],
    )
    grads = shifted(grads, "feat", slices)

    step = slice_cols // cores
    keep, give = call(
        weight_body, [((slices, step, 2 * hidden), F32), ((slices, step, 2 * hidden), BF16)],
        (place, turned, *grads), "weight",
        2 * quarter * slices * slice_cols * 2 * hidden, 4 * quarter * slices * slice_cols,
        scratch=[pltpu.VMEM((quarter, 2 * hidden), BF16)], scalars=1,
    )
    got = swapped(give, "core", cores, 1)
    seed_embedding, second_keep, second_give = call(
        seeds_body,
        [((seeds, out_cols), BF16), ((hidden, out_cols), F32), ((hidden, out_cols), BF16)],
        (place, second_self, second_neighbor, cotangent, *grads), "seeds",
        8 * seeds * hidden * out_cols, 2 * slots * width,
        scratch=[pltpu.VMEM((2, hidden, out_cols), F32)], scalars=1,
    )
    got, second_give = lax.optimization_barrier((got, second_give))
    deep = step // count_x
    (mixed,) = call(
        halves_body, [((count_x * slices, deep, 2 * hidden), BF16)], (keep, got), "halves",
        0, 8 * slices * step * hidden,
    )
    mixed = exchange(mixed, ("x", "feat"))

    second_got = swapped(second_give, "core", cores, 1)
    shard = [((hidden // count_x, out_cols), BF16)]
    second_parts = call(
        second_split_body, shard * count_x, (place, second_keep, second_got), "second_split",
        0, 8 * hidden * out_cols, scalars=1,
    )
    (second,) = call(
        add_body, shard, shifted(second_parts, "x", count_x), "second_add",
        0, 4 * hidden * out_cols,
    )

    def doubled(value, stride):
        (value,) = call(
            add_body, shard, (value, swapped(value, "z", count_z, stride)), "second_add",
            0, 2 * hidden * out_cols,
        )
        return value

    strides = [1 << at for at in range(count_z.bit_length() - 1)]
    second = doubled(second, strides[0])
    mixed, second = lax.optimization_barrier((mixed, second))
    (mixed,) = call(
        sum_body, [((count_z, deep, 2 * hidden), BF16)], (mixed,), "sum", 0, 64 * deep * hidden,
    )
    mixed = exchange(mixed, "z")
    for stride in strides[1:]:
        second = doubled(second, stride)
    (mixed,) = call(
        join_body, [((2 * deep, 2 * hidden), BF16)], (mixed, second), "join",
        0, 64 * deep * hidden,
    )
    (mixed,) = call(
        pair_body, [((4 * deep, 2 * hidden), BF16)],
        (place, mixed, swapped(mixed, "core", cores, 1)), "pair", 0, 32 * deep * hidden, scalars=1,
    )
    grad_first_self, grad_first_neighbor, grad_second_self, grad_second_neighbor = call(
        functools.partial(finish_body, cores=cores, slices=slices),
        [((slice_cols, hidden), F32)] * 2 + [((hidden, out_cols), F32)] * 2,
        (place, *shifted([mixed] * count_x, "x", count_x)), "finish",
        0, 24 * slice_cols * hidden, scalars=1,
    )
    return (
        seed_embedding,
        grad_first_self,
        grad_first_neighbor,
        grad_second_self,
        grad_second_neighbor,
    )


def solution(mesh):
    shape = (4, 8, 2, mesh.shape["feat"])
    sizes = dict(zip(AXES, shape))
    mesh = Mesh(mesh.devices.reshape(shape), AXES)
    dom = AXES[:3]
    in_specs = (
        P(dom, "feat"),
        P("feat", None),
        P("feat", None),
        P(),
        P(),
        P(),
        P(dom, None),
        P(dom, None),
        P(dom),
        P(dom, None),
        P(dom),
        P(dom),
        P(dom, None),
        P(dom, None),
    )
    out_specs = (P(dom, None), P("feat", None), P("feat", None), P(), P())
    return jax.shard_map(
        functools.partial(per_device, sizes=sizes),
        mesh=mesh,
        in_specs=in_specs,
        out_specs=out_specs,
        check_vma=False,
    )
```

```python
import functools

import jax
import jax.numpy as jnp
from jax import lax
from jax.experimental import pallas as pl
from jax.experimental.pallas import tpu as pltpu
from jax.sharding import PartitionSpec as P

BF16 = jnp.bfloat16
F32 = jnp.float32
I32 = jnp.int32


def dot(left, right, left_dim=1, right_dim=0):
    return lax.dot_general(
        left, right, (((left_dim,), (right_dim,)), ((), ())), preferred_element_type=F32
    )


def call(body, outs, args, name, flops=0, moved=0, vmem=16, scratch=(), scalars=0, far=()):
    specs = [
        pl.BlockSpec(
            memory_space=pltpu.SMEM if at < scalars else pltpu.HBM if at in far else pltpu.VMEM
        )
        for at in range(len(args))
    ]
    out_specs = [pl.BlockSpec(memory_space=pltpu.VMEM) for _ in outs]
    return pl.pallas_call(
        body,
        out_shape=[jax.ShapeDtypeStruct(shape, dtype) for shape, dtype in outs],
        in_specs=specs,
        out_specs=out_specs,
        scratch_shapes=scratch,
        name=name,
        compiler_params=pltpu.CompilerParams(vmem_limit_bytes=vmem << 20),
        cost_estimate=pl.CostEstimate(flops=flops, bytes_accessed=moved, transcendentals=0),
    )(*[
        pltpu.with_memory_space_constraint(arg, pltpu.HBM) if at in far else arg
        for at, arg in enumerate(args)
    ])


def pick_body(row_far, x_far, out_ref, row_ref, x_ref, sems):
    copies = [
        pltpu.make_async_copy(row_far, row_ref, sems.at[0]),
        pltpu.make_async_copy(x_far, x_ref, sems.at[1]),
    ]
    for copy in copies:
        copy.start()
    for copy in copies:
        copy.wait()
    rows = x_ref.shape[0]
    step = 128
    lane = lax.broadcasted_iota(I32, (step, step), 1)

    def fill(at, carry):
        start = pl.multiple_of(at * step, step)
        wanted = jnp.broadcast_to(row_ref[:, pl.ds(start, step)], (step, step)).T
        picks = jnp.concatenate(
            [
                jnp.where(wanted == lane + low, 1.0, 0.0).astype(BF16)
                for low in range(0, rows, step)
            ],
            axis=1,
        )
        out_ref[pl.ds(start, step), :] = dot(picks, x_ref[...]).astype(BF16)
        return carry

    lax.fori_loop(0, out_ref.shape[0] // step, fill, 0, unroll=4)


def count_body(
    self_ref, near_ref, degree_ref, mask_ref, seed_ref, seed_near_ref,
    self_table, near_table, seed_table, seed_near_table, live_ref,
):
    slots, mids = near_table.shape
    fan = near_ref.shape[0]
    step = 32
    live = lax.broadcasted_iota(I32, (fan, mids), 0) < degree_ref[...]
    live_ref[...] = jnp.where(live, near_ref[...], -1)
    own = self_ref[...]

    def fill(at, carry):
        span = pl.ds(pl.multiple_of(at * step, step), step)
        line = lax.broadcasted_iota(I32, (step, mids), 0) + at * step
        total = jnp.zeros((step, mids), F32)
        for j in range(fan):
            total = total + jnp.where(live_ref[j : j + 1, :] == line, 1.0, 0.0)
        filled = mask_ref[span, :].astype(F32)
        filled = jnp.concatenate([filled] * (mids // filled.shape[1]), axis=1)
        near_table[span, :] = (total * filled).astype(BF16)
        self_table[span, :] = jnp.where(own == line, filled, 0.0).astype(BF16)
        return carry

    lax.fori_loop(0, slots // step, fill, 0)
    seeds = seed_table.shape[1]
    line = lax.broadcasted_iota(I32, (mids, seeds), 0)
    seed_table[...] = jnp.where(seed_ref[...] == line, 1.0, 0.0).astype(BF16)
    total = jnp.zeros((mids, seeds), F32)
    for j in range(seed_near_ref.shape[0]):
        total = total + jnp.where(seed_near_ref[j : j + 1, :] == line, 1.0, 0.0)
    seed_near_table[...] = total.astype(BF16)


def gather_body(
    place_ref, x_ref, self_far, near_far, degree_ref, weight_self_ref, weight_near_ref, *refs, slices
):
    own_ref, near_ref = refs[:2]
    out_refs = refs[2 : 2 + slices]
    self_table, near_table, held_ref, sems = refs[2 + slices :]
    pieces, step, _ = self_table.shape
    copies = []
    for piece in range(pieces):
        for side, (far, ref) in enumerate(((self_far, self_table), (near_far, near_table))):
            copy = pltpu.make_async_copy(far.at[piece], ref.at[piece], sems.at[side, piece])
            copy.start()
            copies.append(copy)
    own, near = 0.0, 0.0
    for piece in range(pieces):
        turned = x_ref[pl.ds(piece * step, step), :].T
        copies[2 * piece].wait()
        own = own + dot(turned, self_table[piece])
        copies[2 * piece + 1].wait()
        near = near + dot(turned, near_table[piece])
    own = own.astype(BF16)
    near = (near / degree_ref[...].astype(F32)).astype(BF16)
    own_ref[...] = own
    near_ref[...] = near
    pre = dot(weight_self_ref[...], own, 0, 0) + dot(weight_near_ref[...], near, 0, 0)
    half = held_ref.shape[1]
    for at in range(slices):
        held_ref[at] = pre[at * half : (at + 1) * half].astype(BF16)
    for shift, out_ref in enumerate(out_refs):
        out_ref[...] = held_ref[lax.rem(place_ref[0] + shift, slices)]


def owner_body(
    place_ref, bias_ref, seed_table, seed_near_table, second_self_ref, second_near_ref,
    cotangent_ref, *refs, fan_two
):
    pre_refs, out_ref = refs[:-1], refs[-1]
    half = pre_refs[0].shape[0]
    mine = pl.ds(pl.multiple_of(place_ref[0] * half, half), half)
    back_self = dot(second_self_ref[mine, :], cotangent_ref[...], 1, 1)
    back_near = dot(second_near_ref[mine, :], cotangent_ref[...], 1, 1) / fan_two

    def spread(back, picks):
        high = back.astype(BF16)
        low = (back - high.astype(F32)).astype(BF16)
        both = dot(jnp.concatenate([high, low], axis=0), picks, 1, 1)
        return both[:half] + both[half:]

    grad_active = spread(back_self, seed_table[...]) + spread(back_near, seed_near_table[...])
    pre = bias_ref[mine, :]
    for pre_ref in pre_refs:
        pre = pre + pre_ref[...].astype(F32)
    sigma = 1.0 / (1.0 + jnp.exp(-pre))
    active = (pre * sigma).astype(BF16)
    slope = (sigma * (1.0 + pre * (1.0 - sigma))).astype(BF16).astype(F32)
    out_ref[:half, :] = (grad_active * slope).astype(BF16)
    own_seeds = dot(active, seed_table[...]).astype(BF16)
    mean_seeds = (dot(active, seed_near_table[...]) / fan_two).astype(BF16)
    seeds = jnp.concatenate([own_seeds, mean_seeds], axis=0)
    width = seeds.shape[1]
    tall = out_ref.shape[0] - half
    for at in range(seeds.shape[0] // tall):
        out_ref[half:, at * width : (at + 1) * width] = seeds[at * tall : (at + 1) * tall]


def unpacked_seeds(ref, half, width):
    return jnp.concatenate(
        [ref[half:, at : at + width] for at in range(0, ref.shape[1], width)], axis=0
    )


def weight_body(place_ref, own_ref, near_ref, cotangent_ref, *refs, half):
    grads_refs, (out_ref, held_ref) = refs[:-2], refs[-2:]
    slices = len(grads_refs)
    tiles = out_ref.shape[0] // 2
    lines = out_ref.shape[1] // 2
    per = half // lines
    cotangent = cotangent_ref[...]
    for shift, grads_ref in enumerate(grads_refs):
        at = lax.rem(place_ref[0] + slices - shift, slices)
        held_ref[pl.ds(pl.multiple_of(at * half, half), half), :] = grads_ref[:half, :]
        second = dot(unpacked_seeds(grads_ref, half, cotangent.shape[0]), cotangent)
        for side in range(2):
            part = second[side * half : (side + 1) * half].reshape(per, lines, second.shape[1])
            out_ref[pl.ds(side * tiles + at * per, per), lines:] = part.astype(BF16)
    grads = held_ref[...]
    for side, ref in enumerate((own_ref, near_ref)):
        part = dot(ref[...], grads, 1, 1)
        part = part.reshape(tiles, lines, part.shape[1])
        out_ref[pl.ds(side * tiles, tiles), :lines] = part.astype(BF16)


def embed_body(place_ref, second_self_ref, second_near_ref, *refs, half):
    grads_refs, out_ref = refs[:-1], refs[-1]
    slices = len(grads_refs)
    total = jnp.zeros(out_ref.shape, F32)
    for shift, grads_ref in enumerate(grads_refs):
        at = lax.rem(place_ref[0] + slices - shift, slices)
        rows = pl.ds(pl.multiple_of(at * half, half), half)
        seeds = unpacked_seeds(grads_ref, half, out_ref.shape[0])
        total = total + dot(seeds[:half], second_self_ref[rows, :], 0, 0)
        total = total + dot(seeds[half:], second_near_ref[rows, :], 0, 0)
    out_ref[...] = total.astype(BF16)


def sum_body(parts_ref, out_ref):
    total = jnp.sum(parts_ref[...].astype(F32), axis=0).astype(BF16)
    for at in range(out_ref.shape[0]):
        out_ref[at] = total


def finish_body(all_ref, first_self_ref, first_near_ref, second_self_ref, second_near_ref):
    peers, tall, width = all_ref.shape
    lines = tall // 2
    tiles = peers // 2
    value = all_ref[...].astype(F32)
    first_self_ref[...] = value[:tiles, :lines].reshape(tiles * lines, width)
    first_near_ref[...] = value[tiles:, :lines].reshape(tiles * lines, width)
    second_self_ref[...] = value[:tiles, lines:].reshape(tiles * lines, width)
    second_near_ref[...] = value[tiles:, lines:].reshape(tiles * lines, width)


def exchange(value, axis):
    return lax.all_to_all(value, axis, split_axis=0, concat_axis=0, tiled=True)


def shifted(pieces, axis, count):
    return [
        piece
        if shift == 0
        else lax.ppermute(piece, axis, [(at, (at + shift) % count) for at in range(count)])
        for shift, piece in enumerate(pieces)
    ]


def per_device(
    features,
    first_self,
    first_neighbor,
    first_bias,
    second_self,
    second_neighbor,
    send_rows,
    arrive_count,
    self_slot,
    neighbor_slot,
    degree,
    seed_self,
    seed_neighbor,
    cotangent,
):
    peers = lax.axis_size("dom")
    slices = lax.axis_size("feat")
    rows, slice_cols = features.shape
    hidden = first_self.shape[1]
    half = hidden // slices
    slots = send_rows.shape[1]
    capacity = slots // peers
    mids, fan = neighbor_slot.shape
    seeds, fan_two = seed_neighbor.shape
    out_cols = second_self.shape[1]
    lines = 2 * hidden // peers
    pieces = 4
    place = lax.axis_index("feat").astype(I32).reshape(1)

    (picked,) = call(
        pick_body, [((slots, slice_cols), BF16)], (send_rows, features), "pick",
        2 * slots * rows * slice_cols, 2 * slots * rows, far=(0, 1),
        scratch=[
            pltpu.VMEM(send_rows.shape, I32), pltpu.VMEM(features.shape, BF16),
            pltpu.SemaphoreType.DMA((2,)),
        ],
    )
    routed = exchange(picked.reshape(peers, capacity, slice_cols), "dom").reshape(slots, slice_cols)

    slot_at = lax.broadcasted_iota(I32, (peers, capacity, 128), 1)
    mask = (slot_at < arrive_count.reshape(peers, 1, 1)).astype(BF16).reshape(slots, 128)
    self_table, near_table, seed_table, seed_near_table = call(
        count_body,
        [((slots, mids), BF16), ((slots, mids), BF16), ((mids, seeds), BF16), ((mids, seeds), BF16)],
        (
            self_slot.reshape(1, mids), neighbor_slot.T, degree.reshape(1, mids), mask,
            seed_self.reshape(1, seeds), seed_neighbor.T,
        ),
        "count", 0, 16 * slots * mids, scratch=[pltpu.VMEM((fan, mids), I32)],
    )
    bias = first_bias.reshape(hidden, 1)
    routed, seed_table, bias = lax.optimization_barrier((routed, seed_table, bias))

    own_rows, near_rows, *pre = call(
        functools.partial(gather_body, slices=slices),
        [((slice_cols, mids), BF16)] * 2 + [((half, mids), BF16)] * slices,
        (
            place, routed, self_table.reshape(pieces, slots // pieces, mids),
            near_table.reshape(pieces, slots // pieces, mids), degree.reshape(1, mids),
            first_self, first_neighbor,
        ),
        "gather", 4 * slots * slice_cols * mids, 4 * slots * mids, scalars=1, far=(2, 3),
        scratch=[
            pltpu.VMEM((pieces, slots // pieces, mids), BF16),
            pltpu.VMEM((pieces, slots // pieces, mids), BF16),
            pltpu.VMEM((slices, half, mids), BF16), pltpu.SemaphoreType.DMA((2, pieces)),
        ],
    )
    pre = shifted(pre, "feat", slices)
    tall = 2 * half * seeds // mids
    (grads,) = call(
        functools.partial(owner_body, fan_two=fan_two), [((half + tall, mids), BF16)],
        (
            place, bias, seed_table, seed_near_table, second_self, second_neighbor, cotangent, *pre,
        ),
        "owner", 16 * half * seeds * mids, 8 * half * mids, scalars=1,
    )
    grads = shifted([grads] * slices, "feat", slices)
    (merged,) = call(
        functools.partial(weight_body, half=half), [((peers, 2 * lines, hidden), BF16)],
        (place, own_rows, near_rows, cotangent, *grads), "weight",
        4 * slice_cols * mids * hidden, 8 * slice_cols * mids,
        scratch=[pltpu.VMEM((hidden, mids), BF16)], scalars=1,
    )
    merged = exchange(merged, "dom")
    (seed_embedding,) = call(
        functools.partial(embed_body, half=half), [((seeds, out_cols), BF16)],
        (place, second_self, second_neighbor, *grads), "embed",
        4 * seeds * hidden * out_cols, 8 * seeds * hidden, scalars=1,
    )
    (summed,) = call(
        sum_body, [((peers, 2 * lines, hidden), BF16)], (merged,), "sum",
        0, 8 * peers * lines * hidden,
    )
    summed = exchange(summed, "dom")
    grad_first_self, grad_first_neighbor, grad_second_self, grad_second_neighbor = call(
        finish_body, [((slice_cols, hidden), F32)] * 2 + [((hidden, out_cols), F32)] * 2,
        (summed,), "finish", 0, 8 * peers * lines * hidden,
    )
    return (
        seed_embedding,
        grad_first_self,
        grad_first_neighbor,
        grad_second_self,
        grad_second_neighbor,
    )


def solution(mesh):
    in_specs = (
        P("dom", "feat"),
        P("feat", None),
        P("feat", None),
        P(),
        P(),
        P(),
        P("dom", None),
        P("dom", None),
        P("dom"),
        P("dom", None),
        P("dom"),
        P("dom"),
        P("dom", None),
        P("dom", None),
    )
    out_specs = (P("dom", None), P("feat", None), P("feat", None), P(), P())
    return jax.shard_map(
        per_device, mesh=mesh, in_specs=in_specs, out_specs=out_specs, check_vma=False
    )
```

```python
import functools

import jax
import jax.numpy as jnp
from jax import lax
from jax.experimental import pallas as pl
from jax.experimental.pallas import tpu as pltpu
from jax.sharding import Mesh
from jax.sharding import PartitionSpec as P

BF16 = jnp.bfloat16
F32 = jnp.float32
I32 = jnp.int32
AXES = ("x", "z", "core", "feat")


def dot(left, right, left_dim=1, right_dim=0):
    return lax.dot_general(
        left, right, (((left_dim,), (right_dim,)), ((), ())), preferred_element_type=F32
    )


def call(body, outs, args, name, flops=0, moved=0, vmem=16, scratch=(), scalars=0, far=()):
    specs = [
        pl.BlockSpec(
            memory_space=pltpu.SMEM if at < scalars else pltpu.HBM if at in far else pltpu.VMEM
        )
        for at in range(len(args))
    ]
    out_specs = [pl.BlockSpec(memory_space=pltpu.VMEM) for _ in outs]
    return pl.pallas_call(
        body,
        out_shape=[jax.ShapeDtypeStruct(shape, dtype) for shape, dtype in outs],
        in_specs=specs,
        out_specs=out_specs,
        scratch_shapes=scratch,
        name=name,
        compiler_params=pltpu.CompilerParams(vmem_limit_bytes=vmem << 20),
        cost_estimate=pl.CostEstimate(flops=flops, bytes_accessed=moved, transcendentals=0),
    )(*[
        pltpu.with_memory_space_constraint(arg, pltpu.HBM) if at in far else arg
        for at, arg in enumerate(args)
    ])


def pick_body(row_far, x_far, out_ref, row_ref, x_ref, sems):
    copies = [
        pltpu.make_async_copy(row_far, row_ref, sems.at[0]),
        pltpu.make_async_copy(x_far, x_ref, sems.at[1]),
    ]
    for copy in copies:
        copy.start()
    for copy in copies:
        copy.wait()
    rows = x_ref.shape[0]
    step = 128
    lane = lax.broadcasted_iota(I32, (step, step), 1)

    def fill(at, carry):
        start = pl.multiple_of(at * step, step)
        wanted = jnp.broadcast_to(row_ref[:, pl.ds(start, step)], (step, step)).T
        picks = jnp.concatenate(
            [
                jnp.where(wanted == lane + low, 1.0, 0.0).astype(BF16)
                for low in range(0, rows, step)
            ],
            axis=1,
        )
        out_ref[pl.ds(start, step), :] = dot(picks, x_ref[...]).astype(BF16)
        return carry

    lax.fori_loop(0, out_ref.shape[0] // step, fill, 0, unroll=4)


def count_body(
    self_ref, near_ref, degree_ref, mask_ref, seed_ref, seed_near_ref,
    self_table, near_table, seed_table, seed_near_table, live_ref,
):
    slots, mids = near_table.shape
    fan = near_ref.shape[0]
    step = 32
    live = lax.broadcasted_iota(I32, (fan, mids), 0) < degree_ref[...]
    live_ref[...] = jnp.where(live, near_ref[...], -1)
    own = self_ref[...]

    def fill(at, carry):
        span = pl.ds(pl.multiple_of(at * step, step), step)
        line = lax.broadcasted_iota(I32, (step, mids), 0) + at * step
        total = jnp.zeros((step, mids), F32)
        for j in range(fan):
            total = total + jnp.where(live_ref[j : j + 1, :] == line, 1.0, 0.0)
        filled = mask_ref[span, :].astype(F32)
        filled = jnp.concatenate([filled] * (mids // filled.shape[1]), axis=1)
        near_table[span, :] = (total * filled).astype(BF16)
        self_table[span, :] = jnp.where(own == line, filled, 0.0).astype(BF16)
        return carry

    lax.fori_loop(0, slots // step, fill, 0)
    seeds = seed_table.shape[1]
    line = lax.broadcasted_iota(I32, (mids, seeds), 0)
    seed_table[...] = jnp.where(seed_ref[...] == line, 1.0, 0.0).astype(BF16)
    total = jnp.zeros((mids, seeds), F32)
    for j in range(seed_near_ref.shape[0]):
        total = total + jnp.where(seed_near_ref[j : j + 1, :] == line, 1.0, 0.0)
    seed_near_table[...] = total.astype(BF16)


def gather_body(
    place_ref, x_ref, self_far, near_far, degree_ref, weight_self_ref, weight_near_ref, *refs, slices
):
    own_ref, near_ref = refs[:2]
    out_refs = refs[2 : 2 + slices]
    self_table, near_table, held_ref, sems = refs[2 + slices :]
    pieces, step, _ = self_table.shape
    copies = []
    for piece in range(pieces):
        for side, (far, ref) in enumerate(((self_far, self_table), (near_far, near_table))):
            copy = pltpu.make_async_copy(far.at[piece], ref.at[piece], sems.at[side, piece])
            copy.start()
            copies.append(copy)
    own, near = 0.0, 0.0
    for piece in range(pieces):
        turned = x_ref[pl.ds(piece * step, step), :].T
        copies[2 * piece].wait()
        own = own + dot(turned, self_table[piece])
        copies[2 * piece + 1].wait()
        near = near + dot(turned, near_table[piece])
    own = own.astype(BF16)
    near = (near / degree_ref[...].astype(F32)).astype(BF16)
    own_ref[...] = own
    near_ref[...] = near
    pre = dot(weight_self_ref[...], own, 0, 0) + dot(weight_near_ref[...], near, 0, 0)
    half = held_ref.shape[1]
    for at in range(slices):
        held_ref[at] = pre[at * half : (at + 1) * half].astype(BF16)
    for shift, out_ref in enumerate(out_refs):
        out_ref[...] = held_ref[lax.rem(place_ref[0] + shift, slices)]


def owner_body(
    place_ref, bias_ref, seed_table, seed_near_table, second_self_ref, second_near_ref,
    cotangent_ref, *refs, fan_two
):
    pre_refs, out_ref = refs[:-1], refs[-1]
    half = pre_refs[0].shape[0]
    mine = pl.ds(pl.multiple_of(place_ref[0] * half, half), half)
    back_self = dot(second_self_ref[mine, :], cotangent_ref[...], 1, 1)
    back_near = dot(second_near_ref[mine, :], cotangent_ref[...], 1, 1) / fan_two

    def spread(back, picks):
        high = back.astype(BF16)
        low = (back - high.astype(F32)).astype(BF16)
        both = dot(jnp.concatenate([high, low], axis=0), picks, 1, 1)
        return both[:half] + both[half:]

    grad_active = spread(back_self, seed_table[...]) + spread(back_near, seed_near_table[...])
    pre = bias_ref[mine, :]
    for pre_ref in pre_refs:
        pre = pre + pre_ref[...].astype(F32)
    sigma = 1.0 / (1.0 + jnp.exp(-pre))
    active = (pre * sigma).astype(BF16)
    slope = (sigma * (1.0 + pre * (1.0 - sigma))).astype(BF16).astype(F32)
    out_ref[:half, :] = (grad_active * slope).astype(BF16)
    own_seeds = dot(active, seed_table[...]).astype(BF16)
    mean_seeds = (dot(active, seed_near_table[...]) / fan_two).astype(BF16)
    seeds = jnp.concatenate([own_seeds, mean_seeds], axis=0)
    width = seeds.shape[1]
    tall = out_ref.shape[0] - half
    for at in range(seeds.shape[0] // tall):
        out_ref[half:, at * width : (at + 1) * width] = seeds[at * tall : (at + 1) * tall]


def unpacked_seeds(ref, half, width):
    return jnp.concatenate(
        [ref[half:, at : at + width] for at in range(0, ref.shape[1], width)], axis=0
    )


def weight_body(place_ref, own_ref, near_ref, cotangent_ref, *refs, half, count):
    grads_refs, (keep_ref, give_ref, grads_held, held_ref) = refs[:-4], refs[-4:]
    slices = len(grads_refs)
    cores, tall, cols = held_ref.shape
    hidden = cols // 2
    deep = tall // (2 * count)
    cotangent = cotangent_ref[...]
    for shift, grads_ref in enumerate(grads_refs):
        at = lax.rem(place_ref[0] + slices - shift, slices)
        grads_held[pl.ds(pl.multiple_of(at * half, half), half), :] = grads_ref[:half, :]
        second = dot(unpacked_seeds(grads_ref, half, cotangent.shape[0]), cotangent)
        for piece in range(half // deep):
            index = at * (half // deep) + piece
            core = lax.div(index, count)
            x = lax.rem(index, count)
            span = pl.ds(pl.multiple_of((2 * x + 1) * deep, deep), deep)
            for side in range(2):
                held_ref[core, span, side * hidden : (side + 1) * hidden] = second[
                    side * half + piece * deep : side * half + (piece + 1) * deep
                ]
    grads = grads_held[...]
    for side, ref in enumerate((own_ref, near_ref)):
        part = dot(ref[...], grads, 1, 1)
        for core in range(cores):
            for x in range(count):
                low = (core * count + x) * deep
                held_ref[
                    core, 2 * x * deep : (2 * x + 1) * deep, side * hidden : (side + 1) * hidden
                ] = part[low : low + deep]
    keep_ref[...] = held_ref[place_ref[1]]
    give_ref[...] = held_ref[1 - place_ref[1]].astype(BF16)


def split_body(place_ref, keep_ref, got_ref, *out_refs):
    count = len(out_refs)
    step = out_refs[0].shape[0]
    for shift, out_ref in enumerate(out_refs):
        at = lax.rem(place_ref[2] + shift, count)
        span = pl.ds(pl.multiple_of(at * step, step), step)
        out_ref[...] = (keep_ref[span, :] + got_ref[span, :].astype(F32)).astype(BF16)


def spread_body(*refs):
    parts, out_ref = refs[:-1], refs[-1]
    total = parts[0][...].astype(F32)
    for part in parts[1:]:
        total = total + part[...].astype(F32)
    total = total.astype(BF16)
    for at in range(out_ref.shape[0]):
        out_ref[at] = total


def sum_body(parts_ref, out_ref):
    out_ref[...] = jnp.sum(parts_ref[...].astype(F32), axis=0).astype(BF16)


def stack_body(place_ref, *refs):
    parts, out_ref = refs[:-1], refs[-1]
    count = len(parts)
    step = parts[0].shape[0]
    for shift, part in enumerate(parts):
        at = lax.rem(place_ref[2] + count - shift, count)
        out_ref[pl.ds(pl.multiple_of(at * step, step), step), :] = part[...]


def finish_body(
    place_ref, mine_ref, other_ref, first_self_ref, first_near_ref, second_self_ref, second_near_ref,
    count, cores,
):
    hidden = first_self_ref.shape[0]
    deep = hidden // (count * cores)
    mine, other = mine_ref[...].astype(F32), other_ref[...].astype(F32)
    refs = ((first_self_ref, first_near_ref), (second_self_ref, second_near_ref))
    for core in range(cores):
        value = jnp.where(place_ref[1] == core, mine, other)
        for x in range(count):
            low = (core * count + x) * deep
            for layer in range(2):
                start = (2 * x + layer) * deep
                for side in range(2):
                    refs[layer][side][low : low + deep, :] = value[
                        start : start + deep, side * hidden : (side + 1) * hidden
                    ]


def embed_body(place_ref, second_self_ref, second_near_ref, *refs, half):
    grads_refs, out_ref = refs[:-1], refs[-1]
    slices = len(grads_refs)
    total = jnp.zeros(out_ref.shape, F32)
    for shift, grads_ref in enumerate(grads_refs):
        at = lax.rem(place_ref[0] + slices - shift, slices)
        rows = pl.ds(pl.multiple_of(at * half, half), half)
        seeds = unpacked_seeds(grads_ref, half, out_ref.shape[0])
        total = total + dot(seeds[:half], second_self_ref[rows, :], 0, 0)
        total = total + dot(seeds[half:], second_near_ref[rows, :], 0, 0)
    out_ref[...] = total.astype(BF16)


def exchange(value, axis):
    return lax.all_to_all(value, axis, split_axis=0, concat_axis=0, tiled=True)


def shifted(pieces, axis, count):
    return [
        piece
        if shift == 0
        else lax.ppermute(piece, axis, [(at, (at + shift) % count) for at in range(count)])
        for shift, piece in enumerate(pieces)
    ]


def swapped(value, axis, count, step):
    return lax.ppermute(value, axis, [(at, at ^ step) for at in range(count)])


def per_device(
    features,
    first_self,
    first_neighbor,
    first_bias,
    second_self,
    second_neighbor,
    send_rows,
    arrive_count,
    self_slot,
    neighbor_slot,
    degree,
    seed_self,
    seed_neighbor,
    cotangent,
    sizes,
):
    count_x, count_z, cores, slices = (sizes[axis] for axis in AXES)
    peers = count_x * count_z * cores
    rows, slice_cols = features.shape
    hidden = first_self.shape[1]
    half = hidden // slices
    slots = send_rows.shape[1]
    capacity = slots // peers
    mids, fan = neighbor_slot.shape
    seeds, fan_two = seed_neighbor.shape
    out_cols = second_self.shape[1]
    pieces = 4
    place = jnp.stack([lax.axis_index(axis) for axis in ("feat", "core", "x")]).astype(I32)

    (picked,) = call(
        pick_body, [((slots, slice_cols), BF16)], (send_rows, features), "pick",
        2 * slots * rows * slice_cols, 2 * slots * rows, far=(0, 1),
        scratch=[
            pltpu.VMEM(send_rows.shape, I32), pltpu.VMEM(features.shape, BF16),
            pltpu.SemaphoreType.DMA((2,)),
        ],
    )
    routed = exchange(picked.reshape(peers, capacity, slice_cols), AXES[:3]).reshape(slots, slice_cols)

    slot_at = lax.broadcasted_iota(I32, (peers, capacity, 128), 1)
    mask = (slot_at < arrive_count.reshape(peers, 1, 1)).astype(BF16).reshape(slots, 128)
    self_table, near_table, seed_table, seed_near_table = call(
        count_body,
        [((slots, mids), BF16), ((slots, mids), BF16), ((mids, seeds), BF16), ((mids, seeds), BF16)],
        (
            self_slot.reshape(1, mids), neighbor_slot.T, degree.reshape(1, mids), mask,
            seed_self.reshape(1, seeds), seed_neighbor.T,
        ),
        "count", 0, 16 * slots * mids, scratch=[pltpu.VMEM((fan, mids), I32)],
    )
    bias = first_bias.reshape(hidden, 1)
    routed, seed_table, bias = lax.optimization_barrier((routed, seed_table, bias))

    own_rows, near_rows, *pre = call(
        functools.partial(gather_body, slices=slices),
        [((slice_cols, mids), BF16)] * 2 + [((half, mids), BF16)] * slices,
        (
            place, routed, self_table.reshape(pieces, slots // pieces, mids),
            near_table.reshape(pieces, slots // pieces, mids), degree.reshape(1, mids),
            first_self, first_neighbor,
        ),
        "gather", 4 * slots * slice_cols * mids, 4 * slots * mids, scalars=1, far=(2, 3),
        scratch=[
            pltpu.VMEM((pieces, slots // pieces, mids), BF16),
            pltpu.VMEM((pieces, slots // pieces, mids), BF16),
            pltpu.VMEM((slices, half, mids), BF16), pltpu.SemaphoreType.DMA((2, pieces)),
        ],
    )
    pre = shifted(pre, "feat", slices)
    tall = 2 * half * seeds // mids
    (grads,) = call(
        functools.partial(owner_body, fan_two=fan_two), [((half + tall, mids), BF16)],
        (
            place, bias, seed_table, seed_near_table, second_self, second_neighbor, cotangent, *pre,
        ),
        "owner", 16 * half * seeds * mids, 8 * half * mids, scalars=1,
    )
    grads = shifted([grads] * slices, "feat", slices)
    tall = 2 * hidden // cores
    keep, give = call(
        functools.partial(weight_body, half=half, count=count_x),
        [((tall, 2 * hidden), F32), ((tall, 2 * hidden), BF16)],
        (place, own_rows, near_rows, cotangent, *grads), "weight",
        4 * slice_cols * mids * hidden, 8 * slice_cols * mids,
        scratch=[pltpu.VMEM((hidden, mids), BF16), pltpu.VMEM((cores, tall, 2 * hidden), F32)],
        scalars=1,
    )
    got = swapped(give, "core", cores, 1)
    shard = (tall // count_x, 2 * hidden)
    parts = call(
        split_body, [(shard, BF16)] * count_x, (place, keep, got), "split", 0, 16 * tall * hidden,
        scalars=1,
    )
    (mixed,) = call(
        spread_body, [((count_z,) + shard, BF16)], shifted(parts, "x", count_x), "spread",
        0, 4 * tall * hidden,
    )
    mixed = exchange(mixed, "z")
    (seed_embedding,) = call(
        functools.partial(embed_body, half=half), [((seeds, out_cols), BF16)],
        (place, second_self, second_neighbor, *grads), "embed",
        4 * seeds * hidden * out_cols, 8 * seeds * hidden, scalars=1,
    )
    mixed, seed_embedding = lax.optimization_barrier((mixed, seed_embedding))
    (mixed,) = call(sum_body, [(shard, BF16)], (mixed,), "sum", 0, 8 * tall * hidden)
    (mixed,) = call(
        stack_body, [((tall, 2 * hidden), BF16)],
        (place, *shifted([mixed] * count_x, "x", count_x)), "stack", 0, 8 * tall * hidden, scalars=1,
    )
    grad_first_self, grad_first_neighbor, grad_second_self, grad_second_neighbor = call(
        functools.partial(finish_body, count=count_x, cores=cores),
        [((slice_cols, hidden), F32)] * 2 + [((hidden, out_cols), F32)] * 2,
        (place, mixed, swapped(mixed, "core", cores, 1)), "finish", 0, 24 * tall * hidden, scalars=1,
    )
    return (
        seed_embedding,
        grad_first_self,
        grad_first_neighbor,
        grad_second_self,
        grad_second_neighbor,
    )


def solution(mesh):
    shape = (4, 8, 2, mesh.shape["feat"])
    sizes = dict(zip(AXES, shape))
    mesh = Mesh(mesh.devices.reshape(shape), AXES)
    dom = AXES[:3]
    in_specs = (
        P(dom, "feat"),
        P("feat", None),
        P("feat", None),
        P(),
        P(),
        P(),
        P(dom, None),
        P(dom, None),
        P(dom),
        P(dom, None),
        P(dom),
        P(dom),
        P(dom, None),
        P(dom, None),
    )
    out_specs = (P(dom, None), P("feat", None), P("feat", None), P(), P())
    return jax.shard_map(
        functools.partial(per_device, sizes=sizes),
        mesh=mesh,
        in_specs=in_specs,
        out_specs=out_specs,
        check_vma=False,
    )
```

```python
import functools

import jax
import jax.numpy as jnp
from jax import lax
from jax.experimental import pallas as pl
from jax.experimental.pallas import tpu as pltpu
from jax.sharding import Mesh
from jax.sharding import PartitionSpec as P

BF16 = jnp.bfloat16
F32 = jnp.float32
I32 = jnp.int32
AXES = ("x", "z", "core", "feat")


def dot(left, right, left_dim=1, right_dim=0):
    return lax.dot_general(
        left, right, (((left_dim,), (right_dim,)), ((), ())), preferred_element_type=F32
    )


def call(body, outs, args, name, flops=0, moved=0, vmem=16, scratch=(), scalars=0, far=()):
    specs = [
        pl.BlockSpec(
            memory_space=pltpu.SMEM if at < scalars else pltpu.HBM if at in far else pltpu.VMEM
        )
        for at in range(len(args))
    ]
    out_specs = [pl.BlockSpec(memory_space=pltpu.VMEM) for _ in outs]
    return pl.pallas_call(
        body,
        out_shape=[jax.ShapeDtypeStruct(shape, dtype) for shape, dtype in outs],
        in_specs=specs,
        out_specs=out_specs,
        scratch_shapes=scratch,
        name=name,
        compiler_params=pltpu.CompilerParams(vmem_limit_bytes=vmem << 20),
        cost_estimate=pl.CostEstimate(flops=flops, bytes_accessed=moved, transcendentals=0),
    )(*[
        pltpu.with_memory_space_constraint(arg, pltpu.HBM) if at in far else arg
        for at, arg in enumerate(args)
    ])


def pick_body(row_far, x_far, out_ref, row_ref, x_ref, sems):
    copies = [
        pltpu.make_async_copy(row_far, row_ref, sems.at[0]),
        pltpu.make_async_copy(x_far, x_ref, sems.at[1]),
    ]
    for copy in copies:
        copy.start()
    for copy in copies:
        copy.wait()
    rows = x_ref.shape[0]
    step = 128
    lane = lax.broadcasted_iota(I32, (step, step), 1)

    def fill(at, carry):
        start = pl.multiple_of(at * step, step)
        wanted = jnp.broadcast_to(row_ref[:, pl.ds(start, step)], (step, step)).T
        within = jnp.where((wanted & (step - 1)) == lane, 1.0, 0.0).astype(BF16)
        block = (wanted >> (step.bit_length() - 1)).astype(F32).astype(BF16)
        nothing = jnp.zeros_like(within)
        picks = jnp.concatenate(
            [jnp.where(block == BF16(at), within, nothing) for at in range(rows // step)], axis=1
        )
        out_ref[pl.ds(start, step), :] = dot(picks, x_ref[...]).astype(BF16)
        return carry

    lax.fori_loop(0, out_ref.shape[0] // step, fill, 0, unroll=8)


def count_body(
    self_ref, near_ref, degree_ref, mask_ref, seed_ref, seed_near_ref, seed_table, seed_near_table,
    *refs,
):
    tables, live_ref = refs[:-1], refs[-1]
    tall, mids = tables[0].shape
    fan = near_ref.shape[0]
    step = 32
    live = lax.broadcasted_iota(I32, (fan, mids), 0) < degree_ref[...]
    live_ref[...] = jnp.where(live, near_ref[...], -1)
    own = self_ref[...]

    for index in range(len(tables) // 2):
        self_table, near_table = tables[2 * index], tables[2 * index + 1]
        low = index * tall

        def fill(at, carry, self_table=self_table, near_table=near_table, low=low):
            start = pl.multiple_of(at * step, step)
            span = pl.ds(start, step)
            line = lax.broadcasted_iota(I32, (step, mids), 0) + (low + start)
            total = jnp.zeros((step, mids), F32)
            for j in range(fan):
                total = total + jnp.where(live_ref[j : j + 1, :] == line, 1.0, 0.0)
            filled = mask_ref[pl.ds(low + start, step), :].astype(F32)
            filled = jnp.concatenate([filled] * (mids // filled.shape[1]), axis=1)
            near_table[span, :] = (total * filled).astype(BF16)
            self_table[span, :] = jnp.where(own == line, filled, 0.0).astype(BF16)
            return carry

        lax.fori_loop(0, tall // step, fill, 0)
    seeds = seed_table.shape[1]
    line = lax.broadcasted_iota(I32, (mids, seeds), 0)
    seed_table[...] = jnp.where(seed_ref[...] == line, 1.0, 0.0).astype(BF16)
    total = jnp.zeros((mids, seeds), F32)
    for j in range(seed_near_ref.shape[0]):
        total = total + jnp.where(seed_near_ref[j : j + 1, :] == line, 1.0, 0.0)
    seed_near_table[...] = total.astype(BF16)


def gather_body(
    place_ref, x_ref, degree_ref, weight_self_ref, weight_near_ref, *refs, slices, pieces
):
    tables, fars = refs[:pieces], refs[pieces : 2 * pieces]
    own_ref, near_ref = refs[2 * pieces : 2 * pieces + 2]
    out_refs = refs[2 * pieces + 2 : 2 * pieces + 2 + slices]
    held_ref, table_ref, sems = refs[2 * pieces + 2 + slices :]
    copies = [
        pltpu.make_async_copy(far, table_ref.at[at], sems.at[at]) for at, far in enumerate(fars)
    ]
    for copy in copies:
        copy.start()
    step = tables[0].shape[0]
    own, near = 0.0, 0.0
    for piece in range(pieces):
        turned = x_ref[pl.ds(piece * step, step), :].T
        if 2 * piece < pieces:
            own = own + dot(turned, tables[2 * piece][...])
            near = near + dot(turned, tables[2 * piece + 1][...])
        else:
            at = 2 * piece - pieces
            copies[at].wait()
            own = own + dot(turned, table_ref[at])
            copies[at + 1].wait()
            near = near + dot(turned, table_ref[at + 1])
    own = own.astype(BF16)
    near = (near / degree_ref[...].astype(F32)).astype(BF16)
    own_ref[...] = own
    near_ref[...] = near
    pre = dot(weight_self_ref[...], own, 0, 0) + dot(weight_near_ref[...], near, 0, 0)
    half = held_ref.shape[1]
    for at in range(slices):
        held_ref[at] = pre[at * half : (at + 1) * half].astype(BF16)
    for shift, out_ref in enumerate(out_refs):
        out_ref[...] = held_ref[lax.rem(place_ref[0] + shift, slices)]


def owner_body(
    place_ref, bias_ref, seed_table, seed_near_table, second_self_ref, second_near_ref,
    cotangent_ref, *refs, fan_two
):
    pre_refs, out_ref = refs[:-1], refs[-1]
    half = pre_refs[0].shape[0]
    mine = pl.ds(pl.multiple_of(place_ref[0] * half, half), half)
    back_self = dot(second_self_ref[mine, :], cotangent_ref[...], 1, 1)
    back_near = dot(second_near_ref[mine, :], cotangent_ref[...], 1, 1) / fan_two

    def spread(back, picks):
        high = back.astype(BF16)
        low = (back - high.astype(F32)).astype(BF16)
        both = dot(jnp.concatenate([high, low], axis=0), picks, 1, 1)
        return both[:half] + both[half:]

    grad_active = spread(back_self, seed_table[...]) + spread(back_near, seed_near_table[...])
    pre = bias_ref[mine, :]
    for pre_ref in pre_refs:
        pre = pre + pre_ref[...].astype(F32)
    sigma = 1.0 / (1.0 + jnp.exp(-pre))
    active = (pre * sigma).astype(BF16)
    slope = (sigma * (1.0 + pre * (1.0 - sigma))).astype(BF16).astype(F32)
    out_ref[:half, :] = (grad_active * slope).astype(BF16)
    own_seeds = dot(active, seed_table[...]).astype(BF16)
    mean_seeds = (dot(active, seed_near_table[...]) / fan_two).astype(BF16)
    seeds = jnp.concatenate([own_seeds, mean_seeds], axis=0)
    width = seeds.shape[1]
    tall = out_ref.shape[0] - half
    for at in range(seeds.shape[0] // tall):
        out_ref[half:, at * width : (at + 1) * width] = seeds[at * tall : (at + 1) * tall]


def unpacked_seeds(ref, half, width):
    return jnp.concatenate(
        [ref[half:, at : at + width] for at in range(0, ref.shape[1], width)], axis=0
    )


def weight_body(place_ref, core_ref, own_ref, near_ref, cotangent_ref, *refs, half, count):
    grads_refs, (keep_ref, give_ref, grads_held, held_ref) = refs[:-4], refs[-4:]
    slices = len(grads_refs)
    cores, tall, cols = held_ref.shape
    hidden = cols // 2
    deep = tall // (2 * count)
    cotangent = cotangent_ref[...]
    for shift, grads_ref in enumerate(grads_refs):
        at = lax.rem(place_ref[0] + slices - shift, slices)
        grads_held[pl.ds(pl.multiple_of(at * half, half), half), :] = grads_ref[:half, :]
        second = dot(unpacked_seeds(grads_ref, half, cotangent.shape[0]), cotangent)
        for piece in range(half // deep):
            index = at * (half // deep) + piece
            core = lax.div(index, count)
            x = lax.rem(index, count)
            span = pl.ds(pl.multiple_of((2 * x + 1) * deep, deep), deep)
            for side in range(2):
                held_ref[core, span, side * hidden : (side + 1) * hidden] = second[
                    side * half + piece * deep : side * half + (piece + 1) * deep
                ]
    grads = grads_held[...]
    for side, ref in enumerate((own_ref, near_ref)):
        part = dot(ref[...], grads, 1, 1)
        for core in range(cores):
            for x in range(count):
                low = (core * count + x) * deep
                held_ref[
                    core, 2 * x * deep : (2 * x + 1) * deep, side * hidden : (side + 1) * hidden
                ] = part[low : low + deep]
    keep_ref[...] = held_ref[core_ref[0]]
    give_ref[...] = held_ref[1 - core_ref[0]].astype(BF16)


def split_body(place_ref, keep_ref, got_ref, *out_refs):
    count = len(out_refs)
    step = out_refs[0].shape[0]
    for shift, out_ref in enumerate(out_refs):
        at = lax.rem(place_ref[0] + shift, count)
        span = pl.ds(pl.multiple_of(at * step, step), step)
        out_ref[...] = (keep_ref[span, :] + got_ref[span, :].astype(F32)).astype(BF16)


def spread_body(*refs):
    parts, out_ref = refs[:-1], refs[-1]
    total = parts[0][...].astype(F32)
    for part in parts[1:]:
        total = total + part[...].astype(F32)
    total = total.astype(BF16)
    for at in range(out_ref.shape[0]):
        out_ref[at] = total


def sum_body(parts_ref, out_ref):
    out_ref[...] = jnp.sum(parts_ref[...].astype(F32), axis=0).astype(BF16)


def stack_body(place_ref, *refs):
    parts, out_ref = refs[:-1], refs[-1]
    count = len(parts)
    step = parts[0].shape[0]
    for shift, part in enumerate(parts):
        at = lax.rem(place_ref[0] + count - shift, count)
        out_ref[pl.ds(pl.multiple_of(at * step, step), step), :] = part[...]


def finish_body(
    place_ref, mine_ref, other_ref, first_self_ref, first_near_ref, second_self_ref, second_near_ref,
    count, cores,
):
    hidden = first_self_ref.shape[0]
    deep = hidden // (count * cores)
    mine, other = mine_ref[...].astype(F32), other_ref[...].astype(F32)
    refs = ((first_self_ref, first_near_ref), (second_self_ref, second_near_ref))
    for core in range(cores):
        value = jnp.where(place_ref[0] == core, mine, other)
        for x in range(count):
            low = (core * count + x) * deep
            for layer in range(2):
                start = (2 * x + layer) * deep
                for side in range(2):
                    refs[layer][side][low : low + deep, :] = value[
                        start : start + deep, side * hidden : (side + 1) * hidden
                    ]


def embed_body(place_ref, second_self_ref, second_near_ref, *refs, half):
    grads_refs, out_ref = refs[:-1], refs[-1]
    slices = len(grads_refs)
    total = jnp.zeros(out_ref.shape, F32)
    for shift, grads_ref in enumerate(grads_refs):
        at = lax.rem(place_ref[0] + slices - shift, slices)
        rows = pl.ds(pl.multiple_of(at * half, half), half)
        seeds = unpacked_seeds(grads_ref, half, out_ref.shape[0])
        total = total + dot(seeds[:half], second_self_ref[rows, :], 0, 0)
        total = total + dot(seeds[half:], second_near_ref[rows, :], 0, 0)
    out_ref[...] = total.astype(BF16)


def exchange(value, axis):
    return lax.all_to_all(value, axis, split_axis=0, concat_axis=0, tiled=True)


def shifted(pieces, axis, count):
    return [
        piece
        if shift == 0
        else lax.ppermute(piece, axis, [(at, (at + shift) % count) for at in range(count)])
        for shift, piece in enumerate(pieces)
    ]


def swapped(value, axis, count, step):
    return lax.ppermute(value, axis, [(at, at ^ step) for at in range(count)])


def per_device(
    features,
    first_self,
    first_neighbor,
    first_bias,
    second_self,
    second_neighbor,
    send_rows,
    arrive_count,
    self_slot,
    neighbor_slot,
    degree,
    seed_self,
    seed_neighbor,
    cotangent,
    sizes,
):
    count_x, count_z, cores, slices = (sizes[axis] for axis in AXES)
    peers = count_x * count_z * cores
    rows, slice_cols = features.shape
    hidden = first_self.shape[1]
    half = hidden // slices
    slots = send_rows.shape[1]
    capacity = slots // peers
    mids, fan = neighbor_slot.shape
    seeds, fan_two = seed_neighbor.shape
    out_cols = second_self.shape[1]
    pieces = 4
    at_feat, at_core, at_x = (
        lax.axis_index(axis).astype(I32).reshape(1) for axis in ("feat", "core", "x")
    )

    (picked,) = call(
        pick_body, [((slots, slice_cols), BF16)], (send_rows, features), "pick",
        2 * slots * rows * slice_cols, 2 * slots * rows, far=(0, 1),
        scratch=[
            pltpu.VMEM(send_rows.shape, I32), pltpu.VMEM(features.shape, BF16),
            pltpu.SemaphoreType.DMA((2,)),
        ],
    )
    routed = exchange(picked.reshape(peers, capacity, slice_cols), AXES[:3]).reshape(slots, slice_cols)

    slot_at = lax.broadcasted_iota(I32, (peers, capacity, 128), 1)
    mask = (slot_at < arrive_count.reshape(peers, 1, 1)).astype(BF16).reshape(slots, 128)
    seed_table, seed_near_table, *tables = call(
        count_body,
        [((mids, seeds), BF16)] * 2 + [((slots // pieces, mids), BF16)] * (2 * pieces),
        (
            self_slot.reshape(1, mids), neighbor_slot.T, degree.reshape(1, mids), mask,
            seed_self.reshape(1, seeds), seed_neighbor.T,
        ),
        "count", 0, 16 * slots * mids, scratch=[pltpu.VMEM((fan, mids), I32)],
    )
    bias = first_bias.reshape(hidden, 1)
    routed, seed_table, bias = lax.optimization_barrier((routed, seed_table, bias))

    own_rows, near_rows, *pre = call(
        functools.partial(gather_body, slices=slices, pieces=pieces),
        [((slice_cols, mids), BF16)] * 2 + [((half, mids), BF16)] * slices,
        (at_feat, routed, degree.reshape(1, mids), first_self, first_neighbor, *tables),
        "gather", 4 * slots * slice_cols * mids, 4 * slots * mids, scalars=1,
        far=range(5 + pieces, 5 + 2 * pieces),
        scratch=[
            pltpu.VMEM((slices, half, mids), BF16),
            pltpu.VMEM((pieces, slots // pieces, mids), BF16), pltpu.SemaphoreType.DMA((pieces,)),
        ],
    )
    pre = shifted(pre, "feat", slices)
    tall = 2 * half * seeds // mids
    (grads,) = call(
        functools.partial(owner_body, fan_two=fan_two), [((half + tall, mids), BF16)],
        (
            at_feat, bias, seed_table, seed_near_table, second_self, second_neighbor, cotangent, *pre,
        ),
        "owner", 16 * half * seeds * mids, 8 * half * mids, scalars=1,
    )
    grads = shifted([grads] * slices, "feat", slices)
    tall = 2 * hidden // cores
    keep, give = call(
        functools.partial(weight_body, half=half, count=count_x),
        [((tall, 2 * hidden), F32), ((tall, 2 * hidden), BF16)],
        (at_feat, at_core, own_rows, near_rows, cotangent, *grads), "weight",
        4 * slice_cols * mids * hidden, 8 * slice_cols * mids,
        scratch=[pltpu.VMEM((hidden, mids), BF16), pltpu.VMEM((cores, tall, 2 * hidden), F32)],
        scalars=2,
    )
    got = swapped(give, "core", cores, 1)
    shard = (tall // count_x, 2 * hidden)
    parts = call(
        split_body, [(shard, BF16)] * count_x, (at_x, keep, got), "split", 0, 16 * tall * hidden,
        scalars=1,
    )
    (mixed,) = call(
        spread_body, [((count_z,) + shard, BF16)], shifted(parts, "x", count_x), "spread",
        0, 4 * tall * hidden,
    )
    mixed = exchange(mixed, "z")
    (seed_embedding,) = call(
        functools.partial(embed_body, half=half), [((seeds, out_cols), BF16)],
        (at_feat, second_self, second_neighbor, *grads), "embed",
        4 * seeds * hidden * out_cols, 8 * seeds * hidden, scalars=1,
    )
    mixed, seed_embedding = lax.optimization_barrier((mixed, seed_embedding))
    (mixed,) = call(sum_body, [(shard, BF16)], (mixed,), "sum", 0, 8 * tall * hidden)
    (mixed,) = call(
        stack_body, [((tall, 2 * hidden), BF16)],
        (at_x, *shifted([mixed] * count_x, "x", count_x)), "stack", 0, 8 * tall * hidden, scalars=1,
    )
    grad_first_self, grad_first_neighbor, grad_second_self, grad_second_neighbor = call(
        functools.partial(finish_body, count=count_x, cores=cores),
        [((slice_cols, hidden), F32)] * 2 + [((hidden, out_cols), F32)] * 2,
        (at_core, mixed, swapped(mixed, "core", cores, 1)), "finish", 0, 24 * tall * hidden, scalars=1,
    )
    return (
        seed_embedding,
        grad_first_self,
        grad_first_neighbor,
        grad_second_self,
        grad_second_neighbor,
    )


def solution(mesh):
    shape = (4, 8, 2, mesh.shape["feat"])
    sizes = dict(zip(AXES, shape))
    mesh = Mesh(mesh.devices.reshape(shape), AXES)
    dom = AXES[:3]
    in_specs = (
        P(dom, "feat"),
        P("feat", None),
        P("feat", None),
        P(),
        P(),
        P(),
        P(dom, None),
        P(dom, None),
        P(dom),
        P(dom, None),
        P(dom),
        P(dom),
        P(dom, None),
        P(dom, None),
    )
    out_specs = (P(dom, None), P("feat", None), P("feat", None), P(), P())
    return jax.shard_map(
        functools.partial(per_device, sizes=sizes),
        mesh=mesh,
        in_specs=in_specs,
        out_specs=out_specs,
        check_vma=False,
    )
```

```python
import functools

import jax
import jax.numpy as jnp
from jax import lax
from jax.experimental import pallas as pl
from jax.experimental.pallas import tpu as pltpu
from jax.sharding import Mesh
from jax.sharding import PartitionSpec as P

BF16 = jnp.bfloat16
F32 = jnp.float32
I32 = jnp.int32
AXES = ("x", "z", "core", "feat")


def dot(left, right, left_dim=1, right_dim=0):
    return lax.dot_general(
        left, right, (((left_dim,), (right_dim,)), ((), ())), preferred_element_type=F32
    )


def call(body, outs, args, name, flops=0, moved=0, vmem=16, scratch=(), scalars=0, far=()):
    specs = [
        pl.BlockSpec(
            memory_space=pltpu.SMEM if at < scalars else pltpu.HBM if at in far else pltpu.VMEM
        )
        for at in range(len(args))
    ]
    out_specs = [pl.BlockSpec(memory_space=pltpu.VMEM) for _ in outs]
    return pl.pallas_call(
        body,
        out_shape=[jax.ShapeDtypeStruct(shape, dtype) for shape, dtype in outs],
        in_specs=specs,
        out_specs=out_specs,
        scratch_shapes=scratch,
        name=name,
        compiler_params=pltpu.CompilerParams(vmem_limit_bytes=vmem << 20),
        cost_estimate=pl.CostEstimate(flops=flops, bytes_accessed=moved, transcendentals=0),
    )(*[
        pltpu.with_memory_space_constraint(arg, pltpu.HBM) if at in far else arg
        for at, arg in enumerate(args)
    ])


def pick_body(row_far, x_far, out_ref, row_ref, x_ref, sems):
    copies = [
        pltpu.make_async_copy(row_far, row_ref, sems.at[0]),
        pltpu.make_async_copy(x_far, x_ref, sems.at[1]),
    ]
    for copy in copies:
        copy.start()
    for copy in copies:
        copy.wait()
    rows = x_ref.shape[0]
    step = 128
    lane = lax.broadcasted_iota(I32, (step, step), 1)

    def fill(at, carry):
        start = pl.multiple_of(at * step, step)
        wanted = jnp.broadcast_to(row_ref[:, pl.ds(start, step)], (step, step)).T
        within = jnp.where((wanted & (step - 1)) == lane, 1.0, 0.0).astype(BF16)
        block = (wanted >> (step.bit_length() - 1)).astype(F32).astype(BF16)
        nothing = jnp.zeros_like(within)
        picks = jnp.concatenate(
            [jnp.where(block == BF16(at), within, nothing) for at in range(rows // step)], axis=1
        )
        out_ref[pl.ds(start, step), :] = dot(picks, x_ref[...]).astype(BF16)
        return carry

    lax.fori_loop(0, out_ref.shape[0] // step, fill, 0, unroll=8)


def count_body(
    self_ref, near_ref, degree_ref, mask_ref, seed_ref, seed_near_ref,
    self_table, near_table, seed_table, seed_near_table, live_ref,
):
    slots, mids = near_table.shape
    fan = near_ref.shape[0]
    step = 32
    live = lax.broadcasted_iota(I32, (fan, mids), 0) < degree_ref[...]
    live_ref[...] = jnp.where(live, near_ref[...], -1)
    own = self_ref[...]

    def fill(at, carry):
        span = pl.ds(pl.multiple_of(at * step, step), step)
        line = lax.broadcasted_iota(I32, (step, mids), 0) + at * step
        total = jnp.zeros((step, mids), F32)
        for j in range(fan):
            total = total + jnp.where(live_ref[j : j + 1, :] == line, 1.0, 0.0)
        filled = mask_ref[span, :].astype(F32)
        filled = jnp.concatenate([filled] * (mids // filled.shape[1]), axis=1)
        near_table[span, :] = (total * filled).astype(BF16)
        self_table[span, :] = jnp.where(own == line, filled, 0.0).astype(BF16)
        return carry

    lax.fori_loop(0, slots // step, fill, 0)
    seeds = seed_table.shape[1]
    line = lax.broadcasted_iota(I32, (mids, seeds), 0)
    seed_table[...] = jnp.where(seed_ref[...] == line, 1.0, 0.0).astype(BF16)
    total = jnp.zeros((mids, seeds), F32)
    for j in range(seed_near_ref.shape[0]):
        total = total + jnp.where(seed_near_ref[j : j + 1, :] == line, 1.0, 0.0)
    seed_near_table[...] = total.astype(BF16)


def gather_body(
    place_ref, x_ref, self_far, near_far, degree_ref, weight_self_ref, weight_near_ref, *refs, slices
):
    own_ref, near_ref = refs[:2]
    out_refs = refs[2 : 2 + slices]
    self_table, near_table, held_ref, sems = refs[2 + slices :]
    pieces, step, _ = self_table.shape
    copies = []
    for piece in range(pieces):
        for side, (far, ref) in enumerate(((self_far, self_table), (near_far, near_table))):
            copy = pltpu.make_async_copy(far.at[piece], ref.at[piece], sems.at[side, piece])
            copy.start()
            copies.append(copy)
    own, near = 0.0, 0.0
    for piece in range(pieces):
        turned = x_ref[pl.ds(piece * step, step), :].T
        copies[2 * piece].wait()
        own = own + dot(turned, self_table[piece])
        copies[2 * piece + 1].wait()
        near = near + dot(turned, near_table[piece])
    own = own.astype(BF16)
    near = (near / degree_ref[...].astype(F32)).astype(BF16)
    own_ref[...] = own
    near_ref[...] = near
    pre = dot(weight_self_ref[...], own, 0, 0) + dot(weight_near_ref[...], near, 0, 0)
    half = held_ref.shape[1]
    for at in range(slices):
        held_ref[at] = pre[at * half : (at + 1) * half].astype(BF16)
    for shift, out_ref in enumerate(out_refs):
        out_ref[...] = held_ref[lax.rem(place_ref[0] + shift, slices)]


def owner_body(
    place_ref, bias_ref, seed_table, seed_near_table, second_self_ref, second_near_ref,
    cotangent_ref, *refs, fan_two
):
    pre_refs, out_ref = refs[:-1], refs[-1]
    half = pre_refs[0].shape[0]
    mine = pl.ds(pl.multiple_of(place_ref[0] * half, half), half)
    back_self = dot(second_self_ref[mine, :], cotangent_ref[...], 1, 1)
    back_near = dot(second_near_ref[mine, :], cotangent_ref[...], 1, 1) / fan_two

    def spread(back, picks):
        high = back.astype(BF16)
        low = (back - high.astype(F32)).astype(BF16)
        both = dot(jnp.concatenate([high, low], axis=0), picks, 1, 1)
        return both[:half] + both[half:]

    grad_active = spread(back_self, seed_table[...]) + spread(back_near, seed_near_table[...])
    pre = bias_ref[mine, :]
    for pre_ref in pre_refs:
        pre = pre + pre_ref[...].astype(F32)
    sigma = 1.0 / (1.0 + jnp.exp(-pre))
    active = (pre * sigma).astype(BF16)
    slope = (sigma * (1.0 + pre * (1.0 - sigma))).astype(BF16).astype(F32)
    out_ref[:half, :] = (grad_active * slope).astype(BF16)
    own_seeds = dot(active, seed_table[...]).astype(BF16)
    mean_seeds = (dot(active, seed_near_table[...]) / fan_two).astype(BF16)
    seeds = jnp.concatenate([own_seeds, mean_seeds], axis=0)
    width = seeds.shape[1]
    tall = out_ref.shape[0] - half
    for at in range(seeds.shape[0] // tall):
        out_ref[half:, at * width : (at + 1) * width] = seeds[at * tall : (at + 1) * tall]


def unpacked_seeds(ref, half, width):
    return jnp.concatenate(
        [ref[half:, at : at + width] for at in range(0, ref.shape[1], width)], axis=0
    )


def weight_body(place_ref, core_ref, own_ref, near_ref, cotangent_ref, *refs, half, count):
    grads_refs, (keep_ref, give_ref, grads_held, held_ref) = refs[:-4], refs[-4:]
    slices = len(grads_refs)
    cores, tall, cols = held_ref.shape
    hidden = cols // 2
    deep = tall // (2 * count)
    cotangent = cotangent_ref[...]
    for shift, grads_ref in enumerate(grads_refs):
        at = lax.rem(place_ref[0] + slices - shift, slices)
        grads_held[pl.ds(pl.multiple_of(at * half, half), half), :] = grads_ref[:half, :]
        second = dot(unpacked_seeds(grads_ref, half, cotangent.shape[0]), cotangent)
        for piece in range(half // deep):
            index = at * (half // deep) + piece
            core = lax.div(index, count)
            x = lax.rem(index, count)
            span = pl.ds(pl.multiple_of((2 * x + 1) * deep, deep), deep)
            for side in range(2):
                held_ref[core, span, side * hidden : (side + 1) * hidden] = second[
                    side * half + piece * deep : side * half + (piece + 1) * deep
                ]
    grads = grads_held[...]
    for side, ref in enumerate((own_ref, near_ref)):
        part = dot(ref[...], grads, 1, 1)
        for core in range(cores):
            for x in range(count):
                low = (core * count + x) * deep
                held_ref[
                    core, 2 * x * deep : (2 * x + 1) * deep, side * hidden : (side + 1) * hidden
                ] = part[low : low + deep]
    keep_ref[...] = held_ref[core_ref[0]]
    give_ref[...] = held_ref[1 - core_ref[0]].astype(BF16)


def split_body(place_ref, keep_ref, got_ref, *out_refs):
    count = len(out_refs)
    step = out_refs[0].shape[0]
    for shift, out_ref in enumerate(out_refs):
        at = lax.rem(place_ref[0] + shift, count)
        span = pl.ds(pl.multiple_of(at * step, step), step)
        out_ref[...] = (keep_ref[span, :] + got_ref[span, :].astype(F32)).astype(BF16)


def spread_body(*refs):
    parts, out_ref = refs[:-1], refs[-1]
    total = parts[0][...].astype(F32)
    for part in parts[1:]:
        total = total + part[...].astype(F32)
    total = total.astype(BF16)
    for at in range(out_ref.shape[0]):
        out_ref[at] = total


def sum_body(parts_ref, out_ref):
    out_ref[...] = jnp.sum(parts_ref[...].astype(F32), axis=0).astype(BF16)


def stack_body(place_ref, *refs):
    parts, out_ref = refs[:-1], refs[-1]
    count = len(parts)
    step = parts[0].shape[0]
    for shift, part in enumerate(parts):
        at = lax.rem(place_ref[0] + count - shift, count)
        out_ref[pl.ds(pl.multiple_of(at * step, step), step), :] = part[...]


def finish_body(
    place_ref, mine_ref, other_ref, first_self_ref, first_near_ref, second_self_ref, second_near_ref,
    count, cores,
):
    hidden = first_self_ref.shape[0]
    deep = hidden // (count * cores)
    mine, other = mine_ref[...].astype(F32), other_ref[...].astype(F32)
    refs = ((first_self_ref, first_near_ref), (second_self_ref, second_near_ref))
    for core in range(cores):
        value = jnp.where(place_ref[0] == core, mine, other)
        for x in range(count):
            low = (core * count + x) * deep
            for layer in range(2):
                start = (2 * x + layer) * deep
                for side in range(2):
                    refs[layer][side][low : low + deep, :] = value[
                        start : start + deep, side * hidden : (side + 1) * hidden
                    ]


def embed_body(place_ref, second_self_ref, second_near_ref, *refs, half):
    grads_refs, out_ref = refs[:-1], refs[-1]
    slices = len(grads_refs)
    total = jnp.zeros(out_ref.shape, F32)
    for shift, grads_ref in enumerate(grads_refs):
        at = lax.rem(place_ref[0] + slices - shift, slices)
        rows = pl.ds(pl.multiple_of(at * half, half), half)
        seeds = unpacked_seeds(grads_ref, half, out_ref.shape[0])
        total = total + dot(seeds[:half], second_self_ref[rows, :], 0, 0)
        total = total + dot(seeds[half:], second_near_ref[rows, :], 0, 0)
    out_ref[...] = total.astype(BF16)


def exchange(value, axis):
    return lax.all_to_all(value, axis, split_axis=0, concat_axis=0, tiled=True)


def shifted(pieces, axis, count):
    return [
        piece
        if shift == 0
        else lax.ppermute(piece, axis, [(at, (at + shift) % count) for at in range(count)])
        for shift, piece in enumerate(pieces)
    ]


def swapped(value, axis, count, step):
    return lax.ppermute(value, axis, [(at, at ^ step) for at in range(count)])


def per_device(
    features,
    first_self,
    first_neighbor,
    first_bias,
    second_self,
    second_neighbor,
    send_rows,
    arrive_count,
    self_slot,
    neighbor_slot,
    degree,
    seed_self,
    seed_neighbor,
    cotangent,
    sizes,
):
    count_x, count_z, cores, slices = (sizes[axis] for axis in AXES)
    peers = count_x * count_z * cores
    rows, slice_cols = features.shape
    hidden = first_self.shape[1]
    half = hidden // slices
    slots = send_rows.shape[1]
    capacity = slots // peers
    mids, fan = neighbor_slot.shape
    seeds, fan_two = seed_neighbor.shape
    out_cols = second_self.shape[1]
    pieces = 4
    at_feat, at_core, at_x = (
        lax.axis_index(axis).astype(I32).reshape(1) for axis in ("feat", "core", "x")
    )

    (picked,) = call(
        pick_body, [((slots, slice_cols), BF16)], (send_rows, features), "pick",
        2 * slots * rows * slice_cols, 2 * slots * rows, far=(0, 1),
        scratch=[
            pltpu.VMEM(send_rows.shape, I32), pltpu.VMEM(features.shape, BF16),
            pltpu.SemaphoreType.DMA((2,)),
        ],
    )
    routed = exchange(picked.reshape(peers, capacity, slice_cols), AXES[:3]).reshape(slots, slice_cols)

    slot_at = lax.broadcasted_iota(I32, (peers, capacity, 128), 1)
    mask = (slot_at < arrive_count.reshape(peers, 1, 1)).astype(BF16).reshape(slots, 128)
    self_table, near_table, seed_table, seed_near_table = call(
        count_body,
        [((slots, mids), BF16), ((slots, mids), BF16), ((mids, seeds), BF16), ((mids, seeds), BF16)],
        (
            self_slot.reshape(1, mids), neighbor_slot.T, degree.reshape(1, mids), mask,
            seed_self.reshape(1, seeds), seed_neighbor.T,
        ),
        "count", 0, 16 * slots * mids, scratch=[pltpu.VMEM((fan, mids), I32)],
    )
    bias = first_bias.reshape(hidden, 1)
    routed, seed_table, bias = lax.optimization_barrier((routed, seed_table, bias))

    own_rows, near_rows, *pre = call(
        functools.partial(gather_body, slices=slices),
        [((slice_cols, mids), BF16)] * 2 + [((half, mids), BF16)] * slices,
        (
            at_feat, routed, self_table.reshape(pieces, slots // pieces, mids),
            near_table.reshape(pieces, slots // pieces, mids), degree.reshape(1, mids),
            first_self, first_neighbor,
        ),
        "gather", 4 * slots * slice_cols * mids, 4 * slots * mids, scalars=1, far=(2, 3),
        scratch=[
            pltpu.VMEM((pieces, slots // pieces, mids), BF16),
            pltpu.VMEM((pieces, slots // pieces, mids), BF16),
            pltpu.VMEM((slices, half, mids), BF16), pltpu.SemaphoreType.DMA((2, pieces)),
        ],
    )
    pre = shifted(pre, "feat", slices)
    tall = 2 * half * seeds // mids
    (grads,) = call(
        functools.partial(owner_body, fan_two=fan_two), [((half + tall, mids), BF16)],
        (
            at_feat, bias, seed_table, seed_near_table, second_self, second_neighbor, cotangent, *pre,
        ),
        "owner", 16 * half * seeds * mids, 8 * half * mids, scalars=1,
    )
    grads = shifted([grads] * slices, "feat", slices)
    tall = 2 * hidden // cores
    keep, give = call(
        functools.partial(weight_body, half=half, count=count_x),
        [((tall, 2 * hidden), F32), ((tall, 2 * hidden), BF16)],
        (at_feat, at_core, own_rows, near_rows, cotangent, *grads), "weight",
        4 * slice_cols * mids * hidden, 8 * slice_cols * mids,
        scratch=[pltpu.VMEM((hidden, mids), BF16), pltpu.VMEM((cores, tall, 2 * hidden), F32)],
        scalars=2,
    )
    got = swapped(give, "core", cores, 1)
    shard = (tall // count_x, 2 * hidden)
    parts = call(
        split_body, [(shard, BF16)] * count_x, (at_x, keep, got), "split", 0, 16 * tall * hidden,
        scalars=1,
    )
    (mixed,) = call(
        spread_body, [((count_z,) + shard, BF16)], shifted(parts, "x", count_x), "spread",
        0, 4 * tall * hidden,
    )
    mixed = exchange(mixed, "z")
    (seed_embedding,) = call(
        functools.partial(embed_body, half=half), [((seeds, out_cols), BF16)],
        (at_feat, second_self, second_neighbor, *grads), "embed",
        4 * seeds * hidden * out_cols, 8 * seeds * hidden, scalars=1,
    )
    mixed, seed_embedding = lax.optimization_barrier((mixed, seed_embedding))
    (mixed,) = call(sum_body, [(shard, BF16)], (mixed,), "sum", 0, 8 * tall * hidden)
    (mixed,) = call(
        stack_body, [((tall, 2 * hidden), BF16)],
        (at_x, *shifted([mixed] * count_x, "x", count_x)), "stack", 0, 8 * tall * hidden, scalars=1,
    )
    grad_first_self, grad_first_neighbor, grad_second_self, grad_second_neighbor = call(
        functools.partial(finish_body, count=count_x, cores=cores),
        [((slice_cols, hidden), F32)] * 2 + [((hidden, out_cols), F32)] * 2,
        (at_core, mixed, swapped(mixed, "core", cores, 1)), "finish", 0, 24 * tall * hidden, scalars=1,
    )
    return (
        seed_embedding,
        grad_first_self,
        grad_first_neighbor,
        grad_second_self,
        grad_second_neighbor,
    )


def solution(mesh):
    shape = (4, 8, 2, mesh.shape["feat"])
    sizes = dict(zip(AXES, shape))
    mesh = Mesh(mesh.devices.reshape(shape), AXES)
    dom = AXES[:3]
    in_specs = (
        P(dom, "feat"),
        P("feat", None),
        P("feat", None),
        P(),
        P(),
        P(),
        P(dom, None),
        P(dom, None),
        P(dom),
        P(dom, None),
        P(dom),
        P(dom),
        P(dom, None),
        P(dom, None),
    )
    out_specs = (P(dom, None), P("feat", None), P("feat", None), P(), P())
    return jax.shard_map(
        functools.partial(per_device, sizes=sizes),
        mesh=mesh,
        in_specs=in_specs,
        out_specs=out_specs,
        check_vma=False,
    )
```

```python
import functools

import jax
import jax.numpy as jnp
from jax import lax
from jax.experimental import pallas as pl
from jax.experimental.pallas import tpu as pltpu
from jax.sharding import Mesh
from jax.sharding import PartitionSpec as P

BF16 = jnp.bfloat16
F32 = jnp.float32
I32 = jnp.int32
AXES = ("x", "z", "core", "feat")


def dot(left, right, left_dim=1, right_dim=0):
    return lax.dot_general(
        left, right, (((left_dim,), (right_dim,)), ((), ())), preferred_element_type=F32
    )


def call(body, outs, args, name, flops=0, moved=0, vmem=16, scratch=(), scalars=0, far=()):
    specs = [
        pl.BlockSpec(
            memory_space=pltpu.SMEM if at < scalars else pltpu.HBM if at in far else pltpu.VMEM
        )
        for at in range(len(args))
    ]
    out_specs = [pl.BlockSpec(memory_space=pltpu.VMEM) for _ in outs]
    return pl.pallas_call(
        body,
        out_shape=[jax.ShapeDtypeStruct(shape, dtype) for shape, dtype in outs],
        in_specs=specs,
        out_specs=out_specs,
        scratch_shapes=scratch,
        name=name,
        compiler_params=pltpu.CompilerParams(vmem_limit_bytes=vmem << 20),
        cost_estimate=pl.CostEstimate(flops=flops, bytes_accessed=moved, transcendentals=0),
    )(*[
        pltpu.with_memory_space_constraint(arg, pltpu.HBM) if at in far else arg
        for at, arg in enumerate(args)
    ])


def pick_body(row_far, x_far, out_ref, row_ref, x_ref, sems):
    copies = [
        pltpu.make_async_copy(row_far, row_ref, sems.at[0]),
        pltpu.make_async_copy(x_far, x_ref, sems.at[1]),
    ]
    for copy in copies:
        copy.start()
    for copy in copies:
        copy.wait()
    rows = x_ref.shape[0]
    step = 128
    lane = lax.broadcasted_iota(I32, (step, step), 1)

    def fill(at, carry):
        start = pl.multiple_of(at * step, step)
        wanted = jnp.broadcast_to(row_ref[:, pl.ds(start, step)], (step, step)).T
        within = jnp.where((wanted & (step - 1)) == lane, 1.0, 0.0).astype(BF16)
        block = (wanted >> (step.bit_length() - 1)).astype(F32).astype(BF16)
        nothing = jnp.zeros_like(within)
        picks = jnp.concatenate(
            [jnp.where(block == BF16(at), within, nothing) for at in range(rows // step)], axis=1
        )
        out_ref[pl.ds(start, step), :] = dot(picks, x_ref[...]).astype(BF16)
        return carry

    lax.fori_loop(0, out_ref.shape[0] // step, fill, 0, unroll=8)


def count_body(
    near_ref, degree_ref, mask_ref, seed_ref, seed_near_ref, near_table,
    seed_table, seed_near_table, live_ref,
):
    slots, mids = near_table.shape
    fan = near_ref.shape[0]
    step = 32
    live = lax.broadcasted_iota(I32, (fan, mids), 0) < degree_ref[...]
    live_ref[...] = jnp.where(live, near_ref[...], -1)

    def fill(at, carry):
        span = pl.ds(pl.multiple_of(at * step, step), step)
        line = lax.broadcasted_iota(I32, (step, mids), 0) + at * step
        total = jnp.zeros((step, mids), F32)
        for j in range(fan):
            total = total + jnp.where(live_ref[j : j + 1, :] == line, 1.0, 0.0)
        filled = mask_ref[span, :].astype(F32)
        filled = jnp.concatenate([filled] * (mids // filled.shape[1]), axis=1)
        near_table[span, :] = (total * filled).astype(BF16)
        return carry

    lax.fori_loop(0, slots // step, fill, 0)
    seeds = seed_table.shape[1]
    line = lax.broadcasted_iota(I32, (mids, seeds), 0)
    seed_table[...] = jnp.where(seed_ref[...] == line, 1.0, 0.0).astype(BF16)
    total = jnp.zeros((mids, seeds), F32)
    for j in range(seed_near_ref.shape[0]):
        total = total + jnp.where(seed_near_ref[j : j + 1, :] == line, 1.0, 0.0)
    seed_near_table[...] = total.astype(BF16)


def gather_body(
    place_ref, x_ref, slot_ref, mask_ref, near_far, degree_ref, weight_self_ref, weight_near_ref,
    *refs, slices
):
    own_ref, near_ref = refs[:2]
    out_refs = refs[2 : 2 + slices]
    near_table, held_ref, sems = refs[2 + slices :]
    pieces, step, mids = near_table.shape
    copies = [
        pltpu.make_async_copy(near_far.at[at], near_table.at[at], sems.at[at])
        for at in range(pieces)
    ]
    for copy in copies:
        copy.start()
    own, near = 0.0, 0.0
    for piece in range(pieces):
        span = pl.ds(piece * step, step)
        turned = x_ref[span, :].T
        line = lax.broadcasted_iota(I32, (step, mids), 0) + piece * step
        filled = mask_ref[span, :].astype(F32)
        filled = jnp.concatenate([filled] * (mids // filled.shape[1]), axis=1)
        own = own + dot(turned, jnp.where(slot_ref[...] == line, filled, 0.0).astype(BF16))
        copies[piece].wait()
        near = near + dot(turned, near_table[piece])
    own = own.astype(BF16)
    near = (near / degree_ref[...].astype(F32)).astype(BF16)
    own_ref[...] = own
    near_ref[...] = near
    pre = dot(weight_self_ref[...], own, 0, 0) + dot(weight_near_ref[...], near, 0, 0)
    half = held_ref.shape[1]
    for at in range(slices):
        held_ref[at] = pre[at * half : (at + 1) * half].astype(BF16)
    for shift, out_ref in enumerate(out_refs):
        out_ref[...] = held_ref[lax.rem(place_ref[0] + shift, slices)]


def owner_body(
    place_ref, bias_ref, seed_table, seed_near_table, second_self_ref, second_near_ref,
    cotangent_ref, *refs, fan_two
):
    pre_refs, out_ref = refs[:-1], refs[-1]
    half = pre_refs[0].shape[0]
    mine = pl.ds(pl.multiple_of(place_ref[0] * half, half), half)
    back_self = dot(second_self_ref[mine, :], cotangent_ref[...], 1, 1)
    back_near = dot(second_near_ref[mine, :], cotangent_ref[...], 1, 1) / fan_two

    def spread(back, picks):
        high = back.astype(BF16)
        low = (back - high.astype(F32)).astype(BF16)
        both = dot(jnp.concatenate([high, low], axis=0), picks, 1, 1)
        return both[:half] + both[half:]

    grad_active = spread(back_self, seed_table[...]) + spread(back_near, seed_near_table[...])
    pre = bias_ref[mine, :]
    for pre_ref in pre_refs:
        pre = pre + pre_ref[...].astype(F32)
    sigma = 1.0 / (1.0 + jnp.exp(-pre))
    active = (pre * sigma).astype(BF16)
    slope = (sigma * (1.0 + pre * (1.0 - sigma))).astype(BF16).astype(F32)
    out_ref[:half, :] = (grad_active * slope).astype(BF16)
    own_seeds = dot(active, seed_table[...]).astype(BF16)
    mean_seeds = (dot(active, seed_near_table[...]) / fan_two).astype(BF16)
    seeds = jnp.concatenate([own_seeds, mean_seeds], axis=0)
    width = seeds.shape[1]
    tall = out_ref.shape[0] - half
    for at in range(seeds.shape[0] // tall):
        out_ref[half:, at * width : (at + 1) * width] = seeds[at * tall : (at + 1) * tall]


def unpacked_seeds(ref, half, width):
    return jnp.concatenate(
        [ref[half:, at : at + width] for at in range(0, ref.shape[1], width)], axis=0
    )


def weight_body(place_ref, core_ref, own_ref, near_ref, cotangent_ref, *refs, half, count):
    grads_refs, (keep_ref, give_ref, grads_held, held_ref) = refs[:-4], refs[-4:]
    slices = len(grads_refs)
    cores, tall, cols = held_ref.shape
    hidden = cols // 2
    deep = tall // (2 * count)
    cotangent = cotangent_ref[...]
    for shift, grads_ref in enumerate(grads_refs):
        at = lax.rem(place_ref[0] + slices - shift, slices)
        grads_held[pl.ds(pl.multiple_of(at * half, half), half), :] = grads_ref[:half, :]
        second = dot(unpacked_seeds(grads_ref, half, cotangent.shape[0]), cotangent)
        for piece in range(half // deep):
            index = at * (half // deep) + piece
            core = lax.div(index, count)
            x = lax.rem(index, count)
            span = pl.ds(pl.multiple_of((2 * x + 1) * deep, deep), deep)
            for side in range(2):
                held_ref[core, span, side * hidden : (side + 1) * hidden] = second[
                    side * half + piece * deep : side * half + (piece + 1) * deep
                ]
    grads = grads_held[...]
    for side, ref in enumerate((own_ref, near_ref)):
        part = dot(ref[...], grads, 1, 1)
        for core in range(cores):
            for x in range(count):
                low = (core * count + x) * deep
                held_ref[
                    core, 2 * x * deep : (2 * x + 1) * deep, side * hidden : (side + 1) * hidden
                ] = part[low : low + deep]
    keep_ref[...] = held_ref[core_ref[0]]
    give_ref[...] = held_ref[1 - core_ref[0]].astype(BF16)


def split_body(place_ref, keep_ref, got_ref, *out_refs):
    count = len(out_refs)
    step = out_refs[0].shape[0]
    for shift, out_ref in enumerate(out_refs):
        at = lax.rem(place_ref[0] + shift, count)
        span = pl.ds(pl.multiple_of(at * step, step), step)
        out_ref[...] = (keep_ref[span, :] + got_ref[span, :].astype(F32)).astype(BF16)


def spread_body(*refs):
    parts, out_ref = refs[:-1], refs[-1]
    total = parts[0][...].astype(F32)
    for part in parts[1:]:
        total = total + part[...].astype(F32)
    total = total.astype(BF16)
    for at in range(out_ref.shape[0]):
        out_ref[at] = total


def sum_body(parts_ref, out_ref):
    out_ref[...] = jnp.sum(parts_ref[...].astype(F32), axis=0).astype(BF16)


def finish_body(core_ref, x_ref, *refs, count, cores):
    mine, other, outs = refs[:count], refs[count : 2 * count], refs[2 * count :]
    deep = mine[0].shape[0] // 2
    hidden = outs[0].shape[1]
    for shift in range(count):
        x = lax.rem(x_ref[0] + count - shift, count)
        own, got = mine[shift][...].astype(F32), other[shift][...].astype(F32)
        for core in range(cores):
            value = jnp.where(core_ref[0] == core, own, got)
            span = pl.ds(pl.multiple_of((core * count + x) * deep, deep), deep)
            for at, out_ref in enumerate(outs):
                layer, side = at // 2, at % 2
                out_ref[span, :] = value[
                    layer * deep : (layer + 1) * deep, side * hidden : (side + 1) * hidden
                ]


def embed_body(place_ref, second_self_ref, second_near_ref, *refs, half):
    grads_refs, out_ref = refs[:-1], refs[-1]
    slices = len(grads_refs)
    total = jnp.zeros(out_ref.shape, F32)
    for shift, grads_ref in enumerate(grads_refs):
        at = lax.rem(place_ref[0] + slices - shift, slices)
        rows = pl.ds(pl.multiple_of(at * half, half), half)
        seeds = unpacked_seeds(grads_ref, half, out_ref.shape[0])
        total = total + dot(seeds[:half], second_self_ref[rows, :], 0, 0)
        total = total + dot(seeds[half:], second_near_ref[rows, :], 0, 0)
    out_ref[...] = total.astype(BF16)


def exchange(value, axis):
    return lax.all_to_all(value, axis, split_axis=0, concat_axis=0, tiled=True)


def shifted(pieces, axis, count):
    return [
        piece
        if shift == 0
        else lax.ppermute(piece, axis, [(at, (at + shift) % count) for at in range(count)])
        for shift, piece in enumerate(pieces)
    ]


def swapped(value, axis, count, step):
    return lax.ppermute(value, axis, [(at, at ^ step) for at in range(count)])


def per_device(
    features,
    first_self,
    first_neighbor,
    first_bias,
    second_self,
    second_neighbor,
    send_rows,
    arrive_count,
    self_slot,
    neighbor_slot,
    degree,
    seed_self,
    seed_neighbor,
    cotangent,
    sizes,
):
    count_x, count_z, cores, slices = (sizes[axis] for axis in AXES)
    peers = count_x * count_z * cores
    rows, slice_cols = features.shape
    hidden = first_self.shape[1]
    half = hidden // slices
    slots = send_rows.shape[1]
    capacity = slots // peers
    mids, fan = neighbor_slot.shape
    seeds, fan_two = seed_neighbor.shape
    out_cols = second_self.shape[1]
    pieces = 4
    at_feat, at_core, at_x = (
        lax.axis_index(axis).astype(I32).reshape(1) for axis in ("feat", "core", "x")
    )

    (picked,) = call(
        pick_body, [((slots, slice_cols), BF16)], (send_rows, features), "pick",
        2 * slots * rows * slice_cols, 2 * slots * rows, far=(0, 1),
        scratch=[
            pltpu.VMEM(send_rows.shape, I32), pltpu.VMEM(features.shape, BF16),
            pltpu.SemaphoreType.DMA((2,)),
        ],
    )
    routed = exchange(picked.reshape(peers, capacity, slice_cols), AXES[:3]).reshape(slots, slice_cols)

    slot_at = lax.broadcasted_iota(I32, (peers, capacity, 128), 1)
    mask = (slot_at < arrive_count.reshape(peers, 1, 1)).astype(BF16).reshape(slots, 128)
    near_table, seed_table, seed_near_table = call(
        count_body,
        [((slots, mids), BF16), ((mids, seeds), BF16), ((mids, seeds), BF16)],
        (
            neighbor_slot.T, degree.reshape(1, mids), mask,
            seed_self.reshape(1, seeds), seed_neighbor.T,
        ),
        "count", 0, 16 * slots * mids, scratch=[pltpu.VMEM((fan, mids), I32)],
    )
    bias = first_bias.reshape(hidden, 1)
    routed, seed_table, bias = lax.optimization_barrier((routed, seed_table, bias))

    own_rows, near_rows, *pre = call(
        functools.partial(gather_body, slices=slices),
        [((slice_cols, mids), BF16)] * 2 + [((half, mids), BF16)] * slices,
        (
            at_feat, routed, self_slot.reshape(1, mids), mask,
            near_table.reshape(pieces, slots // pieces, mids), degree.reshape(1, mids),
            first_self, first_neighbor,
        ),
        "gather", 4 * slots * slice_cols * mids, 4 * slots * mids, scalars=1, far=(4,),
        scratch=[
            pltpu.VMEM((pieces, slots // pieces, mids), BF16),
            pltpu.VMEM((slices, half, mids), BF16), pltpu.SemaphoreType.DMA((pieces,)),
        ],
    )
    pre = shifted(pre, "feat", slices)
    tall = 2 * half * seeds // mids
    (grads,) = call(
        functools.partial(owner_body, fan_two=fan_two), [((half + tall, mids), BF16)],
        (
            at_feat, bias, seed_table, seed_near_table, second_self, second_neighbor, cotangent, *pre,
        ),
        "owner", 16 * half * seeds * mids, 8 * half * mids, scalars=1,
    )
    grads = shifted([grads] * slices, "feat", slices)
    tall = 2 * hidden // cores
    keep, give = call(
        functools.partial(weight_body, half=half, count=count_x),
        [((tall, 2 * hidden), F32), ((tall, 2 * hidden), BF16)],
        (at_feat, at_core, own_rows, near_rows, cotangent, *grads), "weight",
        4 * slice_cols * mids * hidden, 8 * slice_cols * mids,
        scratch=[pltpu.VMEM((hidden, mids), BF16), pltpu.VMEM((cores, tall, 2 * hidden), F32)],
        scalars=2,
    )
    got = swapped(give, "core", cores, 1)
    shard = (tall // count_x, 2 * hidden)
    parts = call(
        split_body, [(shard, BF16)] * count_x, (at_x, keep, got), "split", 0, 16 * tall * hidden,
        scalars=1,
    )
    (mixed,) = call(
        spread_body, [((count_z,) + shard, BF16)], shifted(parts, "x", count_x), "spread",
        0, 4 * tall * hidden,
    )
    mixed = exchange(mixed, "z")
    (seed_embedding,) = call(
        functools.partial(embed_body, half=half), [((seeds, out_cols), BF16)],
        (at_feat, second_self, second_neighbor, *grads), "embed",
        4 * seeds * hidden * out_cols, 8 * seeds * hidden, scalars=1,
    )
    mixed, seed_embedding = lax.optimization_barrier((mixed, seed_embedding))
    (mixed,) = call(sum_body, [(shard, BF16)], (mixed,), "sum", 0, 8 * tall * hidden)
    mine = shifted([mixed] * count_x, "x", count_x)
    other = [swapped(piece, "core", cores, 1) for piece in mine]
    grad_first_self, grad_first_neighbor, grad_second_self, grad_second_neighbor = call(
        functools.partial(finish_body, count=count_x, cores=cores),
        [((slice_cols, hidden), F32)] * 2 + [((hidden, out_cols), F32)] * 2,
        (at_core, at_x, *mine, *other), "finish", 0, 24 * tall * hidden, scalars=2,
    )
    return (
        seed_embedding,
        grad_first_self,
        grad_first_neighbor,
        grad_second_self,
        grad_second_neighbor,
    )


def solution(mesh):
    shape = (4, 8, 2, mesh.shape["feat"])
    sizes = dict(zip(AXES, shape))
    mesh = Mesh(mesh.devices.reshape(shape), AXES)
    dom = AXES[:3]
    in_specs = (
        P(dom, "feat"),
        P("feat", None),
        P("feat", None),
        P(),
        P(),
        P(),
        P(dom, None),
        P(dom, None),
        P(dom),
        P(dom, None),
        P(dom),
        P(dom),
        P(dom, None),
        P(dom, None),
    )
    out_specs = (P(dom, None), P("feat", None), P("feat", None), P(), P())
    return jax.shard_map(
        functools.partial(per_device, sizes=sizes),
        mesh=mesh,
        in_specs=in_specs,
        out_specs=out_specs,
        check_vma=False,
    )
```

```python
import functools

import jax
import jax.numpy as jnp
from jax import lax
from jax.experimental import pallas as pl
from jax.experimental.pallas import tpu as pltpu
from jax.sharding import Mesh
from jax.sharding import PartitionSpec as P

BF16 = jnp.bfloat16
F32 = jnp.float32
I32 = jnp.int32
AXES = ("x", "z", "core", "feat")


def dot(left, right, left_dim=1, right_dim=0):
    return lax.dot_general(
        left, right, (((left_dim,), (right_dim,)), ((), ())), preferred_element_type=F32
    )


def call(body, outs, args, name, flops=0, moved=0, vmem=16, scratch=(), scalars=0, far=()):
    specs = [
        pl.BlockSpec(
            memory_space=pltpu.SMEM if at < scalars else pltpu.HBM if at in far else pltpu.VMEM
        )
        for at in range(len(args))
    ]
    out_specs = [pl.BlockSpec(memory_space=pltpu.VMEM) for _ in outs]
    return pl.pallas_call(
        body,
        out_shape=[jax.ShapeDtypeStruct(shape, dtype) for shape, dtype in outs],
        in_specs=specs,
        out_specs=out_specs,
        scratch_shapes=scratch,
        name=name,
        compiler_params=pltpu.CompilerParams(vmem_limit_bytes=vmem << 20),
        cost_estimate=pl.CostEstimate(flops=flops, bytes_accessed=moved, transcendentals=0),
    )(*[
        pltpu.with_memory_space_constraint(arg, pltpu.HBM) if at in far else arg
        for at, arg in enumerate(args)
    ])


def pick_body(row_far, x_far, out_ref, row_ref, x_ref, sems):
    copies = [
        pltpu.make_async_copy(row_far, row_ref, sems.at[0]),
        pltpu.make_async_copy(x_far, x_ref, sems.at[1]),
    ]
    for copy in copies:
        copy.start()
    for copy in copies:
        copy.wait()
    rows = x_ref.shape[0]
    step = 128
    lane = lax.broadcasted_iota(I32, (step, step), 1)

    def fill(at, carry):
        start = pl.multiple_of(at * step, step)
        wanted = jnp.broadcast_to(row_ref[:, pl.ds(start, step)], (step, step)).T
        within = jnp.where((wanted & (step - 1)) == lane, 1.0, 0.0).astype(BF16)
        block = (wanted >> (step.bit_length() - 1)).astype(F32).astype(BF16)
        nothing = jnp.zeros_like(within)
        picks = jnp.concatenate(
            [jnp.where(block == BF16(at), within, nothing) for at in range(rows // step)], axis=1
        )
        out_ref[pl.ds(start, step), :] = dot(picks, x_ref[...]).astype(BF16)
        return carry

    lax.fori_loop(0, out_ref.shape[0] // step, fill, 0, unroll=True)


def count_body(
    near_ref, degree_ref, mask_ref, seed_ref, seed_near_ref, near_table,
    seed_table, seed_near_table, live_ref,
):
    slots, mids = near_table.shape
    fan = near_ref.shape[0]
    step = 32
    live = lax.broadcasted_iota(I32, (fan, mids), 0) < degree_ref[...]
    live_ref[...] = jnp.where(live, near_ref[...], -1)

    def fill(at, carry):
        span = pl.ds(pl.multiple_of(at * step, step), step)
        line = lax.broadcasted_iota(I32, (step, mids), 0) + at * step
        total = jnp.zeros((step, mids), F32)
        for j in range(fan):
            total = total + jnp.where(live_ref[j : j + 1, :] == line, 1.0, 0.0)
        filled = mask_ref[span, :].astype(F32)
        filled = jnp.concatenate([filled] * (mids // filled.shape[1]), axis=1)
        near_table[span, :] = (total * filled).astype(BF16)
        return carry

    lax.fori_loop(0, slots // step, fill, 0)
    seeds = seed_table.shape[1]
    line = lax.broadcasted_iota(I32, (mids, seeds), 0)
    seed_table[...] = jnp.where(seed_ref[...] == line, 1.0, 0.0).astype(BF16)
    total = jnp.zeros((mids, seeds), F32)
    for j in range(seed_near_ref.shape[0]):
        total = total + jnp.where(seed_near_ref[j : j + 1, :] == line, 1.0, 0.0)
    seed_near_table[...] = total.astype(BF16)


def gather_body(
    place_ref, x_ref, slot_ref, mask_ref, near_far, degree_ref, weight_self_ref, weight_near_ref,
    *refs, slices
):
    own_ref, near_ref = refs[:2]
    out_refs = refs[2 : 2 + slices]
    near_table, held_ref, sems = refs[2 + slices :]
    pieces, step, mids = near_table.shape
    copies = [
        pltpu.make_async_copy(near_far.at[at], near_table.at[at], sems.at[at])
        for at in range(pieces)
    ]
    for copy in copies:
        copy.start()
    own, near = 0.0, 0.0
    for piece in range(pieces):
        span = pl.ds(piece * step, step)
        turned = x_ref[span, :].T
        line = lax.broadcasted_iota(I32, (step, mids), 0) + piece * step
        filled = mask_ref[span, :].astype(F32)
        filled = jnp.concatenate([filled] * (mids // filled.shape[1]), axis=1)
        own = own + dot(turned, jnp.where(slot_ref[...] == line, filled, 0.0).astype(BF16))
        copies[piece].wait()
        near = near + dot(turned, near_table[piece])
    own = own.astype(BF16)
    near = (near / degree_ref[...].astype(F32)).astype(BF16)
    own_ref[...] = own
    near_ref[...] = near
    pre = dot(weight_self_ref[...], own, 0, 0) + dot(weight_near_ref[...], near, 0, 0)
    half = held_ref.shape[1]
    for at in range(slices):
        held_ref[at] = pre[at * half : (at + 1) * half].astype(BF16)
    for shift, out_ref in enumerate(out_refs):
        out_ref[...] = held_ref[lax.rem(place_ref[0] + shift, slices)]


def owner_body(
    place_ref, bias_ref, seed_table, seed_near_table, second_self_ref, second_near_ref,
    cotangent_ref, *refs, fan_two
):
    pre_refs, out_ref = refs[:-1], refs[-1]
    half = pre_refs[0].shape[0]
    mine = pl.ds(pl.multiple_of(place_ref[0] * half, half), half)
    back_self = dot(second_self_ref[mine, :], cotangent_ref[...], 1, 1)
    back_near = dot(second_near_ref[mine, :], cotangent_ref[...], 1, 1) / fan_two

    def spread(back, picks):
        high = back.astype(BF16)
        low = (back - high.astype(F32)).astype(BF16)
        both = dot(jnp.concatenate([high, low], axis=0), picks, 1, 1)
        return both[:half] + both[half:]

    grad_active = spread(back_self, seed_table[...]) + spread(back_near, seed_near_table[...])
    pre = bias_ref[mine, :]
    for pre_ref in pre_refs:
        pre = pre + pre_ref[...].astype(F32)
    sigma = 1.0 / (1.0 + jnp.exp(-pre))
    active = (pre * sigma).astype(BF16)
    slope = (sigma * (1.0 + pre * (1.0 - sigma))).astype(BF16).astype(F32)
    out_ref[:half, :] = (grad_active * slope).astype(BF16)
    own_seeds = dot(active, seed_table[...]).astype(BF16)
    mean_seeds = (dot(active, seed_near_table[...]) / fan_two).astype(BF16)
    seeds = jnp.concatenate([own_seeds, mean_seeds], axis=0)
    width = seeds.shape[1]
    tall = out_ref.shape[0] - half
    for at in range(seeds.shape[0] // tall):
        out_ref[half:, at * width : (at + 1) * width] = seeds[at * tall : (at + 1) * tall]


def unpacked_seeds(ref, half, width):
    return jnp.concatenate(
        [ref[half:, at : at + width] for at in range(0, ref.shape[1], width)], axis=0
    )


def weight_body(place_ref, core_ref, own_ref, near_ref, cotangent_ref, *refs, half, count):
    grads_refs, (keep_ref, give_ref, grads_held, held_ref) = refs[:-4], refs[-4:]
    slices = len(grads_refs)
    cores, tall, cols = held_ref.shape
    hidden = cols // 2
    deep = tall // (2 * count)
    cotangent = cotangent_ref[...]
    for shift, grads_ref in enumerate(grads_refs):
        at = lax.rem(place_ref[0] + slices - shift, slices)
        grads_held[pl.ds(pl.multiple_of(at * half, half), half), :] = grads_ref[:half, :]
        second = dot(unpacked_seeds(grads_ref, half, cotangent.shape[0]), cotangent)
        for piece in range(half // deep):
            index = at * (half // deep) + piece
            core = lax.div(index, count)
            x = lax.rem(index, count)
            span = pl.ds(pl.multiple_of((2 * x + 1) * deep, deep), deep)
            for side in range(2):
                held_ref[core, span, side * hidden : (side + 1) * hidden] = second[
                    side * half + piece * deep : side * half + (piece + 1) * deep
                ]
    grads = grads_held[...]
    for side, ref in enumerate((own_ref, near_ref)):
        part = dot(ref[...], grads, 1, 1)
        for core in range(cores):
            for x in range(count):
                low = (core * count + x) * deep
                held_ref[
                    core, 2 * x * deep : (2 * x + 1) * deep, side * hidden : (side + 1) * hidden
                ] = part[low : low + deep]
    keep_ref[...] = held_ref[core_ref[0]]
    give_ref[...] = held_ref[1 - core_ref[0]].astype(BF16)


def split_body(place_ref, keep_ref, got_ref, *out_refs):
    count = len(out_refs)
    step = out_refs[0].shape[0]
    for shift, out_ref in enumerate(out_refs):
        at = lax.rem(place_ref[0] + shift, count)
        span = pl.ds(pl.multiple_of(at * step, step), step)
        out_ref[...] = (keep_ref[span, :] + got_ref[span, :].astype(F32)).astype(BF16)


def add_body(*refs):
    total = refs[0][...].astype(F32)
    for ref in refs[1:-1]:
        total = total + ref[...].astype(F32)
    refs[-1][...] = total.astype(BF16)


def finish_body(core_ref, x_ref, *refs, count, cores):
    mine, other, outs = refs[:count], refs[count : 2 * count], refs[2 * count :]
    deep = mine[0].shape[0] // 2
    hidden = outs[0].shape[1]
    for shift in range(count):
        x = lax.rem(x_ref[0] + count - shift, count)
        own, got = mine[shift][...].astype(F32), other[shift][...].astype(F32)
        for core in range(cores):
            value = jnp.where(core_ref[0] == core, own, got)
            span = pl.ds(pl.multiple_of((core * count + x) * deep, deep), deep)
            for at, out_ref in enumerate(outs):
                layer, side = at // 2, at % 2
                out_ref[span, :] = value[
                    layer * deep : (layer + 1) * deep, side * hidden : (side + 1) * hidden
                ]


def embed_body(place_ref, second_self_ref, second_near_ref, *refs, half):
    grads_refs, out_ref = refs[:-1], refs[-1]
    slices = len(grads_refs)
    total = jnp.zeros(out_ref.shape, F32)
    for shift, grads_ref in enumerate(grads_refs):
        at = lax.rem(place_ref[0] + slices - shift, slices)
        rows = pl.ds(pl.multiple_of(at * half, half), half)
        seeds = unpacked_seeds(grads_ref, half, out_ref.shape[0])
        total = total + dot(seeds[:half], second_self_ref[rows, :], 0, 0)
        total = total + dot(seeds[half:], second_near_ref[rows, :], 0, 0)
    out_ref[...] = total.astype(BF16)


def exchange(value, axis):
    return lax.all_to_all(value, axis, split_axis=0, concat_axis=0, tiled=True)


def shifted(pieces, axis, count):
    return [
        piece
        if shift == 0
        else lax.ppermute(piece, axis, [(at, (at + shift) % count) for at in range(count)])
        for shift, piece in enumerate(pieces)
    ]


def swapped(value, axis, count, step):
    return lax.ppermute(value, axis, [(at, at ^ step) for at in range(count)])


def per_device(
    features,
    first_self,
    first_neighbor,
    first_bias,
    second_self,
    second_neighbor,
    send_rows,
    arrive_count,
    self_slot,
    neighbor_slot,
    degree,
    seed_self,
    seed_neighbor,
    cotangent,
    sizes,
):
    count_x, count_z, cores, slices = (sizes[axis] for axis in AXES)
    peers = count_x * count_z * cores
    rows, slice_cols = features.shape
    hidden = first_self.shape[1]
    half = hidden // slices
    slots = send_rows.shape[1]
    capacity = slots // peers
    mids, fan = neighbor_slot.shape
    seeds, fan_two = seed_neighbor.shape
    out_cols = second_self.shape[1]
    pieces = 4
    at_feat, at_core, at_x = (
        lax.axis_index(axis).astype(I32).reshape(1) for axis in ("feat", "core", "x")
    )

    (picked,) = call(
        pick_body, [((slots, slice_cols), BF16)], (send_rows, features), "pick",
        2 * slots * rows * slice_cols, 2 * slots * rows, far=(0, 1),
        scratch=[
            pltpu.VMEM(send_rows.shape, I32), pltpu.VMEM(features.shape, BF16),
            pltpu.SemaphoreType.DMA((2,)),
        ],
    )
    routed = exchange(picked.reshape(peers, capacity, slice_cols), AXES[:3]).reshape(slots, slice_cols)

    slot_at = lax.broadcasted_iota(I32, (peers, capacity, 128), 1)
    mask = (slot_at < arrive_count.reshape(peers, 1, 1)).astype(BF16).reshape(slots, 128)
    near_table, seed_table, seed_near_table = call(
        count_body,
        [((slots, mids), BF16), ((mids, seeds), BF16), ((mids, seeds), BF16)],
        (
            neighbor_slot.T, degree.reshape(1, mids), mask,
            seed_self.reshape(1, seeds), seed_neighbor.T,
        ),
        "count", 0, 16 * slots * mids, scratch=[pltpu.VMEM((fan, mids), I32)],
    )
    bias = first_bias.reshape(hidden, 1)
    routed, seed_table, bias = lax.optimization_barrier((routed, seed_table, bias))

    own_rows, near_rows, *pre = call(
        functools.partial(gather_body, slices=slices),
        [((slice_cols, mids), BF16)] * 2 + [((half, mids), BF16)] * slices,
        (
            at_feat, routed, self_slot.reshape(1, mids), mask,
            near_table.reshape(pieces, slots // pieces, mids), degree.reshape(1, mids),
            first_self, first_neighbor,
        ),
        "gather", 4 * slots * slice_cols * mids, 4 * slots * mids, scalars=1, far=(4,),
        scratch=[
            pltpu.VMEM((pieces, slots // pieces, mids), BF16),
            pltpu.VMEM((slices, half, mids), BF16), pltpu.SemaphoreType.DMA((pieces,)),
        ],
    )
    pre = shifted(pre, "feat", slices)
    tall = 2 * half * seeds // mids
    (grads,) = call(
        functools.partial(owner_body, fan_two=fan_two), [((half + tall, mids), BF16)],
        (
            at_feat, bias, seed_table, seed_near_table, second_self, second_neighbor, cotangent, *pre,
        ),
        "owner", 16 * half * seeds * mids, 8 * half * mids, scalars=1,
    )
    grads = shifted([grads] * slices, "feat", slices)
    tall = 2 * hidden // cores
    keep, give = call(
        functools.partial(weight_body, half=half, count=count_x),
        [((tall, 2 * hidden), F32), ((tall, 2 * hidden), BF16)],
        (at_feat, at_core, own_rows, near_rows, cotangent, *grads), "weight",
        4 * slice_cols * mids * hidden, 8 * slice_cols * mids,
        scratch=[pltpu.VMEM((hidden, mids), BF16), pltpu.VMEM((cores, tall, 2 * hidden), F32)],
        scalars=2,
    )
    got = swapped(give, "core", cores, 1)
    shard = (tall // count_x, 2 * hidden)
    parts = call(
        split_body, [(shard, BF16)] * count_x, (at_x, keep, got), "split", 0, 16 * tall * hidden,
        scalars=1,
    )
    (mixed,) = call(
        add_body, [(shard, BF16)], shifted(parts, "x", count_x), "add", 0, 4 * tall * hidden
    )
    stride = 1
    while stride < count_z:
        (mixed,) = call(
            add_body, [(shard, BF16)], (mixed, swapped(mixed, "z", count_z, stride)), "add",
            0, 2 * tall * hidden,
        )
        stride *= 2
    (seed_embedding,) = call(
        functools.partial(embed_body, half=half), [((seeds, out_cols), BF16)],
        (at_feat, second_self, second_neighbor, *grads), "embed",
        4 * seeds * hidden * out_cols, 8 * seeds * hidden, scalars=1,
    )
    mine = shifted([mixed] * count_x, "x", count_x)
    other = [swapped(piece, "core", cores, 1) for piece in mine]
    grad_first_self, grad_first_neighbor, grad_second_self, grad_second_neighbor = call(
        functools.partial(finish_body, count=count_x, cores=cores),
        [((slice_cols, hidden), F32)] * 2 + [((hidden, out_cols), F32)] * 2,
        (at_core, at_x, *mine, *other), "finish", 0, 24 * tall * hidden, scalars=2,
    )
    return (
        seed_embedding,
        grad_first_self,
        grad_first_neighbor,
        grad_second_self,
        grad_second_neighbor,
    )


def solution(mesh):
    shape = (4, 8, 2, mesh.shape["feat"])
    sizes = dict(zip(AXES, shape))
    mesh = Mesh(mesh.devices.reshape(shape), AXES)
    dom = AXES[:3]
    in_specs = (
        P(dom, "feat"),
        P("feat", None),
        P("feat", None),
        P(),
        P(),
        P(),
        P(dom, None),
        P(dom, None),
        P(dom),
        P(dom, None),
        P(dom),
        P(dom),
        P(dom, None),
        P(dom, None),
    )
    out_specs = (P(dom, None), P("feat", None), P("feat", None), P(), P())
    return jax.shard_map(
        functools.partial(per_device, sizes=sizes),
        mesh=mesh,
        in_specs=in_specs,
        out_specs=out_specs,
        check_vma=False,
    )
```

```python
import functools

import jax
import jax.numpy as jnp
from jax import lax
from jax.experimental import pallas as pl
from jax.experimental.pallas import tpu as pltpu
from jax.sharding import Mesh
from jax.sharding import PartitionSpec as P

BF16 = jnp.bfloat16
F32 = jnp.float32
I32 = jnp.int32
AXES = ("x", "z", "core", "feat")


def dot(left, right, left_dim=1, right_dim=0):
    return lax.dot_general(
        left, right, (((left_dim,), (right_dim,)), ((), ())), preferred_element_type=F32
    )


def call(body, outs, args, name, flops=0, moved=0, vmem=16, scratch=(), scalars=0, far=()):
    specs = [
        pl.BlockSpec(
            memory_space=pltpu.SMEM if at < scalars else pltpu.HBM if at in far else pltpu.VMEM
        )
        for at in range(len(args))
    ]
    out_specs = [pl.BlockSpec(memory_space=pltpu.VMEM) for _ in outs]
    return pl.pallas_call(
        body,
        out_shape=[jax.ShapeDtypeStruct(shape, dtype) for shape, dtype in outs],
        in_specs=specs,
        out_specs=out_specs,
        scratch_shapes=scratch,
        name=name,
        compiler_params=pltpu.CompilerParams(vmem_limit_bytes=vmem << 20),
        cost_estimate=pl.CostEstimate(flops=flops, bytes_accessed=moved, transcendentals=0),
    )(*[
        pltpu.with_memory_space_constraint(arg, pltpu.HBM) if at in far else arg
        for at, arg in enumerate(args)
    ])


def pick_body(row_far, x_far, out_ref, row_ref, x_ref, sems):
    copies = [
        pltpu.make_async_copy(row_far, row_ref, sems.at[0]),
        pltpu.make_async_copy(x_far, x_ref, sems.at[1]),
    ]
    for copy in copies:
        copy.start()
    for copy in copies:
        copy.wait()
    rows = x_ref.shape[0]
    step = 128
    lane = lax.broadcasted_iota(I32, (step, step), 1)

    def fill(at, carry):
        start = pl.multiple_of(at * step, step)
        wanted = jnp.broadcast_to(row_ref[:, pl.ds(start, step)], (step, step)).T
        within = jnp.where((wanted & (step - 1)) == lane, 1.0, 0.0).astype(BF16)
        block = (wanted >> (step.bit_length() - 1)).astype(F32).astype(BF16)
        nothing = jnp.zeros_like(within)
        picks = jnp.concatenate(
            [jnp.where(block == BF16(at), within, nothing) for at in range(rows // step)], axis=1
        )
        out_ref[pl.ds(start, step), :] = dot(picks, x_ref[...]).astype(BF16)
        return carry

    lax.fori_loop(0, out_ref.shape[0] // step, fill, 0, unroll=True)


def count_body(
    near_ref, degree_ref, mask_ref, seed_ref, seed_near_ref, near_table,
    seed_table, seed_near_table, live_ref,
):
    slots, mids = near_table.shape
    fan = near_ref.shape[0]
    step = 32
    live = lax.broadcasted_iota(I32, (fan, mids), 0) < degree_ref[...]
    live_ref[...] = jnp.where(live, near_ref[...], -1)

    def fill(at, carry):
        span = pl.ds(pl.multiple_of(at * step, step), step)
        line = lax.broadcasted_iota(I32, (step, mids), 0) + at * step
        total = jnp.zeros((step, mids), F32)
        for j in range(fan):
            total = total + jnp.where(live_ref[j : j + 1, :] == line, 1.0, 0.0)
        filled = mask_ref[span, :].astype(F32)
        filled = jnp.concatenate([filled] * (mids // filled.shape[1]), axis=1)
        near_table[span, :] = (total * filled).astype(BF16)
        return carry

    lax.fori_loop(0, slots // step, fill, 0)
    seeds = seed_table.shape[1]
    line = lax.broadcasted_iota(I32, (mids, seeds), 0)
    seed_table[...] = jnp.where(seed_ref[...] == line, 1.0, 0.0).astype(BF16)
    total = jnp.zeros((mids, seeds), F32)
    for j in range(seed_near_ref.shape[0]):
        total = total + jnp.where(seed_near_ref[j : j + 1, :] == line, 1.0, 0.0)
    seed_near_table[...] = total.astype(BF16)


def gather_body(
    place_ref, x_ref, slot_ref, mask_ref, near_far, degree_ref, weight_self_ref, weight_near_ref,
    *refs, slices
):
    own_ref, near_ref = refs[:2]
    out_refs = refs[2 : 2 + slices]
    near_table, held_ref, sems = refs[2 + slices :]
    pieces, step, mids = near_table.shape
    copies = [
        pltpu.make_async_copy(near_far.at[at], near_table.at[at], sems.at[at])
        for at in range(pieces)
    ]
    for copy in copies:
        copy.start()
    own, near = 0.0, 0.0
    for piece in range(pieces):
        span = pl.ds(piece * step, step)
        turned = x_ref[span, :].T
        line = lax.broadcasted_iota(I32, (step, mids), 0) + piece * step
        filled = mask_ref[span, :].astype(F32)
        filled = jnp.concatenate([filled] * (mids // filled.shape[1]), axis=1)
        own = own + dot(turned, jnp.where(slot_ref[...] == line, filled, 0.0).astype(BF16))
        copies[piece].wait()
        near = near + dot(turned, near_table[piece])
    own = own.astype(BF16)
    near = (near / degree_ref[...].astype(F32)).astype(BF16)
    own_ref[...] = own
    near_ref[...] = near
    pre = dot(weight_self_ref[...], own, 0, 0) + dot(weight_near_ref[...], near, 0, 0)
    half = held_ref.shape[1]
    for at in range(slices):
        held_ref[at] = pre[at * half : (at + 1) * half].astype(BF16)
    for shift, out_ref in enumerate(out_refs):
        out_ref[...] = held_ref[lax.rem(place_ref[0] + shift, slices)]


def owner_body(
    place_ref, bias_ref, seed_table, seed_near_table, second_self_ref, second_near_ref,
    cotangent_ref, *refs, fan_two
):
    pre_refs, out_ref = refs[:-1], refs[-1]
    half = pre_refs[0].shape[0]
    mine = pl.ds(pl.multiple_of(place_ref[0] * half, half), half)
    back_self = dot(second_self_ref[mine, :], cotangent_ref[...], 1, 1)
    back_near = dot(second_near_ref[mine, :], cotangent_ref[...], 1, 1) / fan_two

    def spread(back, picks):
        high = back.astype(BF16)
        low = (back - high.astype(F32)).astype(BF16)
        both = dot(jnp.concatenate([high, low], axis=0), picks, 1, 1)
        return both[:half] + both[half:]

    grad_active = spread(back_self, seed_table[...]) + spread(back_near, seed_near_table[...])
    pre = bias_ref[mine, :]
    for pre_ref in pre_refs:
        pre = pre + pre_ref[...].astype(F32)
    sigma = 1.0 / (1.0 + jnp.exp(-pre))
    active = (pre * sigma).astype(BF16)
    slope = (sigma * (1.0 + pre * (1.0 - sigma))).astype(BF16).astype(F32)
    out_ref[:half, :] = (grad_active * slope).astype(BF16)
    own_seeds = dot(active, seed_table[...]).astype(BF16)
    mean_seeds = (dot(active, seed_near_table[...]) / fan_two).astype(BF16)
    seeds = jnp.concatenate([own_seeds, mean_seeds], axis=0)
    width = seeds.shape[1]
    tall = out_ref.shape[0] - half
    for at in range(seeds.shape[0] // tall):
        out_ref[half:, at * width : (at + 1) * width] = seeds[at * tall : (at + 1) * tall]


def unpacked_seeds(ref, half, width):
    return jnp.concatenate(
        [ref[half:, at : at + width] for at in range(0, ref.shape[1], width)], axis=0
    )


def weight_body(place_ref, core_ref, own_ref, near_ref, cotangent_ref, *refs, half, count):
    grads_refs, (keep_ref, give_ref, grads_held, held_ref) = refs[:-4], refs[-4:]
    slices = len(grads_refs)
    cores, tall, cols = held_ref.shape
    hidden = cols // 2
    deep = tall // (2 * count)
    cotangent = cotangent_ref[...]
    for shift, grads_ref in enumerate(grads_refs):
        at = lax.rem(place_ref[0] + slices - shift, slices)
        grads_held[pl.ds(pl.multiple_of(at * half, half), half), :] = grads_ref[:half, :]
        second = dot(unpacked_seeds(grads_ref, half, cotangent.shape[0]), cotangent)
        for piece in range(half // deep):
            index = at * (half // deep) + piece
            core = lax.div(index, count)
            x = lax.rem(index, count)
            span = pl.ds(pl.multiple_of((2 * x + 1) * deep, deep), deep)
            for side in range(2):
                held_ref[core, span, side * hidden : (side + 1) * hidden] = second[
                    side * half + piece * deep : side * half + (piece + 1) * deep
                ]
    grads = grads_held[...]
    for side, ref in enumerate((own_ref, near_ref)):
        part = dot(ref[...], grads, 1, 1)
        for core in range(cores):
            for x in range(count):
                low = (core * count + x) * deep
                held_ref[
                    core, 2 * x * deep : (2 * x + 1) * deep, side * hidden : (side + 1) * hidden
                ] = part[low : low + deep]
    keep_ref[...] = held_ref[core_ref[0]]
    give_ref[...] = held_ref[1 - core_ref[0]].astype(BF16)


def split_body(place_ref, keep_ref, got_ref, *out_refs):
    count = len(out_refs)
    step = out_refs[0].shape[0]
    for shift, out_ref in enumerate(out_refs):
        at = lax.rem(place_ref[0] + shift, count)
        span = pl.ds(pl.multiple_of(at * step, step), step)
        out_ref[...] = (keep_ref[span, :] + got_ref[span, :].astype(F32)).astype(BF16)


def add_body(*refs):
    total = refs[0][...].astype(F32)
    for ref in refs[1:-1]:
        total = total + ref[...].astype(F32)
    refs[-1][...] = total.astype(BF16)


def finish_body(core_ref, x_ref, *refs, count, cores):
    mine, other, outs = refs[:count], refs[count : 2 * count], refs[2 * count :]
    deep = mine[0].shape[0] // 2
    hidden = outs[0].shape[1]
    for shift in range(count):
        x = lax.rem(x_ref[0] + count - shift, count)
        own, got = mine[shift][...].astype(F32), other[shift][...].astype(F32)
        for core in range(cores):
            value = jnp.where(core_ref[0] == core, own, got)
            span = pl.ds(pl.multiple_of((core * count + x) * deep, deep), deep)
            for at, out_ref in enumerate(outs):
                layer, side = at // 2, at % 2
                out_ref[span, :] = value[
                    layer * deep : (layer + 1) * deep, side * hidden : (side + 1) * hidden
                ]


def embed_body(place_ref, second_self_ref, second_near_ref, *refs, half):
    grads_refs, out_ref = refs[:-1], refs[-1]
    slices = len(grads_refs)
    total = jnp.zeros(out_ref.shape, F32)
    for shift, grads_ref in enumerate(grads_refs):
        at = lax.rem(place_ref[0] + slices - shift, slices)
        rows = pl.ds(pl.multiple_of(at * half, half), half)
        seeds = unpacked_seeds(grads_ref, half, out_ref.shape[0])
        total = total + dot(seeds[:half], second_self_ref[rows, :], 0, 0)
        total = total + dot(seeds[half:], second_near_ref[rows, :], 0, 0)
    out_ref[...] = total.astype(BF16)


def exchange(value, axis):
    return lax.all_to_all(value, axis, split_axis=0, concat_axis=0, tiled=True)


def shifted(pieces, axis, count):
    return [
        piece
        if shift == 0
        else lax.ppermute(piece, axis, [(at, (at + shift) % count) for at in range(count)])
        for shift, piece in enumerate(pieces)
    ]


def swapped(value, axis, count, step):
    return lax.ppermute(value, axis, [(at, at ^ step) for at in range(count)])


def per_device(
    features,
    first_self,
    first_neighbor,
    first_bias,
    second_self,
    second_neighbor,
    send_rows,
    arrive_count,
    self_slot,
    neighbor_slot,
    degree,
    seed_self,
    seed_neighbor,
    cotangent,
    sizes,
):
    count_x, count_z, cores, slices = (sizes[axis] for axis in AXES)
    peers = count_x * count_z * cores
    rows, slice_cols = features.shape
    hidden = first_self.shape[1]
    half = hidden // slices
    slots = send_rows.shape[1]
    capacity = slots // peers
    mids, fan = neighbor_slot.shape
    seeds, fan_two = seed_neighbor.shape
    out_cols = second_self.shape[1]
    pieces = 4
    at_feat, at_core, at_x = (
        lax.axis_index(axis).astype(I32).reshape(1) for axis in ("feat", "core", "x")
    )

    (picked,) = call(
        pick_body, [((slots, slice_cols), BF16)], (send_rows, features), "pick",
        2 * slots * rows * slice_cols, 2 * slots * rows, far=(0, 1),
        scratch=[
            pltpu.VMEM(send_rows.shape, I32), pltpu.VMEM(features.shape, BF16),
            pltpu.SemaphoreType.DMA((2,)),
        ],
    )
    routed = exchange(picked.reshape(peers, capacity, slice_cols), AXES[:3]).reshape(slots, slice_cols)

    slot_at = lax.broadcasted_iota(I32, (peers, capacity, 128), 1)
    mask = (slot_at < arrive_count.reshape(peers, 1, 1)).astype(BF16).reshape(slots, 128)
    near_table, seed_table, seed_near_table = call(
        count_body,
        [((slots, mids), BF16), ((mids, seeds), BF16), ((mids, seeds), BF16)],
        (
            neighbor_slot.T, degree.reshape(1, mids), mask,
            seed_self.reshape(1, seeds), seed_neighbor.T,
        ),
        "count", 0, 16 * slots * mids, scratch=[pltpu.VMEM((fan, mids), I32)],
    )
    bias = first_bias.reshape(hidden, 1)
    routed, seed_table, bias = lax.optimization_barrier((routed, seed_table, bias))

    own_rows, near_rows, *pre = call(
        functools.partial(gather_body, slices=slices),
        [((slice_cols, mids), BF16)] * 2 + [((half, mids), BF16)] * slices,
        (
            at_feat, routed, self_slot.reshape(1, mids), mask,
            near_table.reshape(pieces, slots // pieces, mids), degree.reshape(1, mids),
            first_self, first_neighbor,
        ),
        "gather", 4 * slots * slice_cols * mids, 4 * slots * mids, scalars=1, far=(4,),
        scratch=[
            pltpu.VMEM((pieces, slots // pieces, mids), BF16),
            pltpu.VMEM((slices, half, mids), BF16), pltpu.SemaphoreType.DMA((pieces,)),
        ],
    )
    pre = shifted(pre, "feat", slices)
    tall = 2 * half * seeds // mids
    (grads,) = call(
        functools.partial(owner_body, fan_two=fan_two), [((half + tall, mids), BF16)],
        (
            at_feat, bias, seed_table, seed_near_table, second_self, second_neighbor, cotangent, *pre,
        ),
        "owner", 16 * half * seeds * mids, 8 * half * mids, scalars=1,
    )
    grads = shifted([grads] * slices, "feat", slices)
    tall = 2 * hidden // cores
    keep, give = call(
        functools.partial(weight_body, half=half, count=count_x),
        [((tall, 2 * hidden), F32), ((tall, 2 * hidden), BF16)],
        (at_feat, at_core, own_rows, near_rows, cotangent, *grads), "weight",
        4 * slice_cols * mids * hidden, 8 * slice_cols * mids,
        scratch=[pltpu.VMEM((hidden, mids), BF16), pltpu.VMEM((cores, tall, 2 * hidden), F32)],
        scalars=2,
    )
    got = swapped(give, "core", cores, 1)
    shard = (tall // count_x, 2 * hidden)
    parts = call(
        split_body, [(shard, BF16)] * count_x, (at_x, keep, got), "split", 0, 16 * tall * hidden,
        scalars=1,
    )
    (mixed,) = call(
        add_body, [(shard, BF16)], shifted(parts, "x", count_x), "add", 0, 4 * tall * hidden
    )
    (seed_embedding,) = call(
        functools.partial(embed_body, half=half), [((seeds, out_cols), BF16)],
        (at_feat, second_self, second_neighbor, *grads), "embed",
        4 * seeds * hidden * out_cols, 8 * seeds * hidden, scalars=1,
    )
    stride = 1
    while stride < count_z:
        got = swapped(mixed, "z", count_z, stride)
        if 2 * stride == count_z:
            got, seed_embedding = lax.optimization_barrier((got, seed_embedding))
        (mixed,) = call(
            add_body, [(shard, BF16)], (mixed, got), "add",
            0, 2 * tall * hidden,
        )
        stride *= 2
    mine = shifted([mixed] * count_x, "x", count_x)
    other = [swapped(piece, "core", cores, 1) for piece in mine]
    grad_first_self, grad_first_neighbor, grad_second_self, grad_second_neighbor = call(
        functools.partial(finish_body, count=count_x, cores=cores),
        [((slice_cols, hidden), F32)] * 2 + [((hidden, out_cols), F32)] * 2,
        (at_core, at_x, *mine, *other), "finish", 0, 24 * tall * hidden, scalars=2,
    )
    return (
        seed_embedding,
        grad_first_self,
        grad_first_neighbor,
        grad_second_self,
        grad_second_neighbor,
    )


def solution(mesh):
    shape = (4, 8, 2, mesh.shape["feat"])
    sizes = dict(zip(AXES, shape))
    mesh = Mesh(mesh.devices.reshape(shape), AXES)
    dom = AXES[:3]
    in_specs = (
        P(dom, "feat"),
        P("feat", None),
        P("feat", None),
        P(),
        P(),
        P(),
        P(dom, None),
        P(dom, None),
        P(dom),
        P(dom, None),
        P(dom),
        P(dom),
        P(dom, None),
        P(dom, None),
    )
    out_specs = (P(dom, None), P("feat", None), P("feat", None), P(), P())
    return jax.shard_map(
        functools.partial(per_device, sizes=sizes),
        mesh=mesh,
        in_specs=in_specs,
        out_specs=out_specs,
        check_vma=False,
    )
```
